32 devices in a mesh: groups: 2 (over y), seq: 4 (over z), tower: 2 (over x), mp: 2 (over core).
Axes of the slice: x: 2, y: 2, z: 4, core: 2. Of those that a mesh axis runs over, the one named last changes fastest.
Arguments:
- video_q: bfloat16 [1024, 3072], P(('groups', 'seq'), ('tower', 'mp')), parts along dimension 0, may hold values from -24 to 24
- video_k: bfloat16 [1024, 3072], P(('groups', 'seq'), ('tower', 'mp')), parts along dimension 0, may hold values from -24 to 24
- video_v: bfloat16 [1024, 3072], P(('groups', 'seq'), ('tower', 'mp')), parts along dimension 0, may hold values from -6 to 6
- audio_q: bfloat16 [512, 3072], P(('groups', 'seq'), ('tower', 'mp')), parts along dimension 0, may hold values from -24 to 24
- audio_k: bfloat16 [512, 3072], P(('groups', 'seq'), ('tower', 'mp')), parts along dimension 0, may hold values from -24 to 24
- audio_v: bfloat16 [512, 3072], P(('groups', 'seq'), ('tower', 'mp')), parts along dimension 0, may hold values from -6 to 6
- offsets: int32 [512], P('groups'), parts along dimension 0, may hold values from 0 to 3, as said below
- counts: int32 [8], P('groups'), parts along dimension 0, may hold values from 1 to 128, 384 in all
Outputs:
- video_self: bfloat16 [1024, 3072], P(('groups', 'seq'), ('tower', 'mp')), parts along dimension 0
- video_cross: bfloat16 [1024, 3072], P(('groups', 'seq'), ('tower', 'mp')), parts along dimension 0
- audio_self: bfloat16 [512, 3072], P(('groups', 'seq'), ('tower', 'mp')), parts along dimension 0
- audio_cross: bfloat16 [512, 3072], P(('groups', 'seq'), ('tower', 'mp')), parts along dimension 0
The draws below stay inside these ranges and needn't reach their ends.
There are 2 independent parts, one for each index of `groups`. The reference program is written for one: setup_inputs(seed, part) draws one part's arguments, and reference() takes and returns one part's arrays. A program takes and returns all parts, laid end to end along the dimension named above; each array names one. Nothing has to cross between parts.
Inputs may be any that keep to these rules, and one draw needn't show every extreme that they name: offsets[a] differs from a // 64 by at most 1.
All inputs are finite; a program needn't handle non-finite values.
Results may differ from the reference program's by a relative error of at most 0.0065.
Values may be sent and summed in bfloat16 or wider, within the bound.
No kernel may reach another device: no remote copies, remote signals or barrier semaphores. Data moves between devices by JAX's collectives and lax.ppermute only.
A program may use at most 64 MiB of HBM per device.

```python
import math
import jax
import jax.numpy as jnp
import numpy as np
from jax import lax

HEADS = 24
HEAD_DIM = 128
VTOK_DEV = 128
ATOK_DEV = 64
SPAN = 1
FRAMES = 4
VIDEO = 512
AUDIO = 256
N_SEQ = 4


def base_rows(key, salt, row_count):
    draw_key = jax.random.fold_in(key, salt)
    return jnp.clip(jax.random.normal(draw_key, (row_count, HEADS * HEAD_DIM), jnp.float32), -6.0, 6.0)


def query_rows(key, salt, row_count):
    drawn = base_rows(key, salt, row_count)
    return drawn.astype(jnp.bfloat16)


def draw_video_q(key, part):
    return query_rows(key, 11, VIDEO)


def draw_audio_q(key, part):
    return query_rows(key, 13, AUDIO)


def draw_video_k(key, part):
    drawn = base_rows(key, 17, VIDEO)
    return drawn.astype(jnp.bfloat16)


def draw_audio_k(key, part):
    drawn = base_rows(key, 19, AUDIO)
    return drawn.astype(jnp.bfloat16)


def draw_offsets(key, part):
    positions = jnp.arange(AUDIO, dtype=jnp.int32)
    aligned = positions // ATOK_DEV
    jitter = jax.random.randint(jax.random.fold_in(key, 31), (AUDIO,), -1, 2, jnp.int32)
    within = positions % ATOK_DEV
    jitter = jnp.where(within == 0, -1, jnp.where(within == ATOK_DEV - 1, 1, jitter))
    return jnp.clip(aligned + jitter, 0, FRAMES - 1).astype(jnp.int32)


def steps_of(key, dims, pieces, least, top_value):
    loudness, own = 1.0, jax.random.fold_in(key, 6)
    for axis_at, parts in pieces:
        draws = jnp.exp(jax.random.uniform(jax.random.fold_in(own, axis_at), (parts,), jnp.float32, least / len(pieces), top_value / len(pieces)))
        loudness = loudness * jnp.repeat(draws, dims[axis_at] // parts).reshape([-1 if axis == axis_at else 1 for axis in range(len(dims))])
    return loudness


def split_up(amount, total, most, lean):
    weights = [(1 << 20) // math.isqrt(rank ** lean) + 1 for rank in range(2, amount + 1)]
    spare, given = total - most - (amount - 1), [1] * (amount - 1)
    while spare > 0:
        candidates = [i for i in range(amount - 1) if given[i] < most]
        whole, budget = sum([weights[i] for i in candidates]), spare
        for i in candidates:
            more = min(most - given[i], max(1, budget * weights[i] // whole), spare)
            given[i] = given[i] + more
            spare = spare - more
    return np.array([most] + given)


def ragged_sizes(key, count, total, most, skew):
    if count == 2:
        one = jax.random.randint(key, (), max(1, total - most), min(most, total - 1) + 1)
        return jnp.stack([one, total - one])
    sizes = jnp.asarray(split_up(count, total, most, skew), jnp.int32)
    couples = (count - 1) // 2
    giver, receiver = sizes[1:1 + 2 * couples:2], sizes[2:2 + 2 * couples:2]
    room = jnp.minimum(giver - 1, most - receiver)
    moved = jax.random.randint(jax.random.fold_in(key, 1), (couples,), 0, 1 << 20) % (room + 1)
    sizes = sizes.at[1:1 + 2 * couples:2].set(giver - moved).at[2:2 + 2 * couples:2].set(receiver + moved)
    return sizes[jax.random.permutation(jax.random.fold_in(key, 2), count)]


def gaussian(own_key, dims, deviation, bound, pieces=(), held_as=jnp.bfloat16):
    values = deviation * jax.random.normal(own_key, dims, jnp.float32)
    if pieces:
        values = values * steps_of(own_key, dims, pieces, -0.22, 0.18)
    return jnp.clip(values, -bound, bound).astype(held_as)


def setup_inputs(seed: int = 0, part: int = 0) -> dict:
    key_of = jax.random.split(jax.random.key(seed), 9)
    part_splits = jax.random.split(jax.random.fold_in(key_of[8], part), 9)
    video_q = draw_video_q(jax.random.fold_in(jax.random.fold_in(key_of[8], part), 71), part)
    video_k = draw_video_k(jax.random.fold_in(jax.random.fold_in(key_of[8], part), 71), part)
    video_v = gaussian(part_splits[2], (VIDEO, HEADS * HEAD_DIM), 1.0, 6.0, ((0, 4), (1, 4)))
    audio_q = draw_audio_q(jax.random.fold_in(jax.random.fold_in(key_of[8], part), 71), part)
    audio_k = draw_audio_k(jax.random.fold_in(jax.random.fold_in(key_of[8], part), 71), part)
    audio_v = gaussian(part_splits[5], (AUDIO, HEADS * HEAD_DIM), 1.0, 6.0, ((0, 4), (1, 4)))
    offsets = draw_offsets(jax.random.fold_in(jax.random.fold_in(key_of[8], part), 71), part)
    counts = ragged_sizes(part_splits[7], FRAMES, VTOK_DEV * N_SEQ * 3 // 4, VTOK_DEV, 2).astype(jnp.int32)
    return {"video_q": video_q, "video_k": video_k, "video_v": video_v, "audio_q": audio_q, "audio_k": audio_k, "audio_v": audio_v, "offsets": offsets, "counts": counts}


def attend(queries, key_rows, value_rows, allowed):
    scaling = HEAD_DIM ** -0.5

    def one_head(head_id):
        scores = jnp.dot(queries[:, head_id, :], key_rows[:, head_id, :].T, preferred_element_type=jnp.float32) * scaling
        scores = jnp.where(allowed, scores, -jnp.inf)
        row_peak = jnp.max(scores, axis=1, keepdims=True)
        weights = jnp.where(allowed, jnp.exp(scores - row_peak), 0.0)
        weight_sum = jnp.sum(weights, axis=1, keepdims=True)
        blended = jnp.dot(weights.astype(jnp.bfloat16), value_rows[:, head_id, :], preferred_element_type=jnp.float32)
        return (blended / weight_sum).astype(jnp.bfloat16)

    stacked = lax.map(one_head, jnp.arange(HEADS, dtype=jnp.int32))
    return jnp.transpose(stacked, (1, 0, 2)).reshape(queries.shape[0], HEADS * HEAD_DIM)


def reference(video_q, video_k, video_v, audio_q, audio_k, audio_v, offsets, counts):
    video_query = video_q.reshape(VIDEO, HEADS, HEAD_DIM)
    video_key = video_k.reshape(VIDEO, HEADS, HEAD_DIM)
    video_value = video_v.reshape(VIDEO, HEADS, HEAD_DIM)
    audio_query = audio_q.reshape(AUDIO, HEADS, HEAD_DIM)
    audio_key = audio_k.reshape(AUDIO, HEADS, HEAD_DIM)
    audio_value = audio_v.reshape(AUDIO, HEADS, HEAD_DIM)
    video_pos = jnp.arange(VIDEO, dtype=jnp.int32)
    video_frame = video_pos // VTOK_DEV
    video_live = (video_pos % VTOK_DEV) < counts[video_frame]
    video_self = attend(video_query, video_key, video_value, video_live[None, :])
    audio_self = attend(audio_query, audio_key, audio_value, jnp.ones((1, AUDIO), jnp.bool_))
    video_cross = attend(video_query, audio_key, audio_value, jnp.abs(offsets[None, :] - video_frame[:, None]) <= SPAN)
    audio_reach = (jnp.abs(offsets[:, None] - video_frame[None, :]) <= SPAN) & video_live[None, :]
    audio_cross = attend(audio_query, video_key, video_value, audio_reach)
    return (video_self, video_cross, audio_self, audio_cross)
```

```python
import functools

import jax
import jax.numpy as jnp
from jax import lax
from jax.experimental import pallas as pl
from jax.experimental.pallas import tpu as pltpu
from jax.sharding import PartitionSpec as P


HEAD_DIM = 128
SPAN = 1
MASKED = -1e30
LOG2E = 1.4426950408889634
DEAD = 1 << 20
VMEM = pl.BlockSpec(memory_space=pltpu.VMEM)
SMEM = pl.BlockSpec(memory_space=pltpu.SMEM)
ANY = pl.BlockSpec(memory_space=pl.ANY)
PARAMS = pltpu.CompilerParams(vmem_limit_bytes=16 << 20)


def attend(queries, key_rows, value_rows, allowed):
    scores = jnp.einsum(
        "qhe,khe->hqk", queries, key_rows, preferred_element_type=jnp.float32
    ) * HEAD_DIM ** (-0.5)
    scores = jnp.where(allowed[None], scores, MASKED)
    peak = jnp.max(scores, axis=2)
    weights = jnp.where(allowed[None], jnp.exp(scores - peak[:, :, None]), 0.0)
    total = jnp.sum(weights, axis=2)
    blended = jnp.einsum(
        "hqk,khe->hqe", weights.astype(jnp.bfloat16), value_rows, preferred_element_type=jnp.float32
    )
    blended = blended / total[:, :, None]
    return jnp.transpose(blended, (1, 0, 2)).reshape(blended.shape[1], -1).astype(jnp.bfloat16)


def gathered(video_q, video_k, video_v, audio_q, audio_k, audio_v, offsets, counts):
    my_frame = lax.axis_index("seq")
    video_rows, audio_rows = video_q.shape[0], audio_q.shape[0]

    def heads(rows):
        return rows.reshape(rows.shape[0], -1, HEAD_DIM)

    def everywhere(rows):
        return heads(lax.all_gather(rows, "seq", axis=0, tiled=True))

    my_offsets = lax.dynamic_slice_in_dim(offsets, my_frame * audio_rows, audio_rows)
    keys, values = everywhere(video_k), everywhere(video_v)
    audio_keys, audio_values = everywhere(audio_k), everywhere(audio_v)
    positions = jnp.arange(keys.shape[0], dtype=jnp.int32)
    source = positions // video_rows
    is_live = positions % video_rows < jnp.repeat(counts, video_rows)
    video_self = attend(heads(video_q), keys, values, is_live[None, :])
    in_reach = (jnp.abs(my_offsets[:, None] - source[None, :]) <= SPAN) & is_live[None, :]
    audio_cross = attend(heads(audio_q), keys, values, in_reach)
    every = jnp.ones((1, audio_keys.shape[0]), jnp.bool_)
    audio_self = attend(heads(audio_q), audio_keys, audio_values, every)
    in_reach = jnp.abs(offsets - my_frame) <= SPAN
    video_cross = attend(heads(video_q), audio_keys, audio_values, in_reach[None, :])
    return (video_self, video_cross, audio_self, audio_cross)


def blend(queries, keys, values, allowed):
    scores = lax.dot_general(
        queries, keys, (((1,), (1,)), ((), ())), preferred_element_type=jnp.float32
    )
    if allowed is not None:
        scores = jnp.where(allowed, scores, MASKED)
    peak = jnp.max(scores, axis=1, keepdims=True)
    weights = jnp.exp2((scores - peak) * (HEAD_DIM ** (-0.5) * LOG2E))
    total = jnp.sum(weights, axis=1, keepdims=True)
    mixed = jnp.dot(weights.astype(jnp.bfloat16), values, preferred_element_type=jnp.float32)
    return (mixed * (1.0 / total)).astype(jnp.bfloat16)


def audio_kernel(role_ref, gap_ref, q_own, q_mate, b0, b1, b2, b3, own_ref, mate_ref):
    video_rows = q_own.shape[0] - b0.shape[0] // 2
    audio_rows = b0.shape[0] // 2

    @pl.when(role_ref[0] == 0)
    def _():
        reach = [jnp.abs(gap_ref[i : i + 1, :]) <= SPAN for i in range(2)]
        for head in range(q_own.shape[1] // HEAD_DIM):
            cols = slice(head * HEAD_DIM, (head + 1) * HEAD_DIM)
            keys = jnp.concatenate([b[:audio_rows, cols] for b in (b0, b1, b2, b3)], axis=0)
            values = jnp.concatenate([b[audio_rows:, cols] for b in (b0, b1, b2, b3)], axis=0)
            for who, (q_ref, o_ref) in enumerate(((q_own, own_ref), (q_mate, mate_ref))):
                o_ref[:video_rows, cols] = blend(q_ref[:video_rows, cols], keys, values, reach[who])
            both = jnp.concatenate([q_own[video_rows:, cols], q_mate[video_rows:, cols]], axis=0)
            out = blend(both, keys, values, None)
            own_ref[video_rows:, cols] = out[:audio_rows]
            mate_ref[video_rows:, cols] = out[audio_rows:]


def video_kernel(first, role_ref, frame_ref, off_ref, q_own, q_mate, b0, b1, b2, b3, own_ref, mate_ref):
    video_rows = b0.shape[0] // 2
    audio_rows = q_own.shape[0] - video_rows

    @pl.when(role_ref[0] == 0)
    def _():
        frames = frame_ref[...]
        live = frames < DEAD
        reach = jnp.abs(off_ref[...] - frames) <= SPAN
        for head in range(b0.shape[1] // HEAD_DIM):
            cols = slice(head * HEAD_DIM, (head + 1) * HEAD_DIM)
            q_cols = slice((first + head) * HEAD_DIM, (first + head + 1) * HEAD_DIM)
            keys = jnp.concatenate([b[:video_rows, cols] for b in (b0, b1, b2, b3)], axis=0)
            values = jnp.concatenate([b[video_rows:, cols] for b in (b0, b1, b2, b3)], axis=0)
            for q_ref, o_ref in ((q_own, own_ref), (q_mate, mate_ref)):
                o_ref[:video_rows, cols] = blend(q_ref[:video_rows, q_cols], keys, values, live)
            both = jnp.concatenate([q_own[video_rows:, q_cols], q_mate[video_rows:, q_cols]], axis=0)
            out = blend(both, keys, values, reach)
            own_ref[video_rows:, cols] = out[:audio_rows]
            mate_ref[video_rows:, cols] = out[audio_rows:]


def place_kernel(video_rows, role_ref, *refs):
    n = (len(refs) - 5) // 2
    own, back = refs[:n], refs[n : 2 * n]
    video_self, video_cross, audio_self, audio_cross = refs[2 * n : 2 * n + 4]
    sem = refs[-1]

    def copies(parts):
        yield parts[0].at[:video_rows], video_cross
        yield parts[0].at[video_rows:], audio_self
        at = 0
        for part in parts[1:]:
            cols = pl.ds(at, part.shape[1])
            yield part.at[:video_rows], video_self.at[:, cols]
            yield part.at[video_rows:], audio_cross.at[:, cols]
            at += part.shape[1]

    for role, parts in ((0, own), (1, back)):

        @pl.when(role_ref[0] == role)
        def _(parts=parts):
            moves = [
                pltpu.make_async_copy(src, dst, sem.at[i])
                for i, (src, dst) in enumerate(copies(parts))
            ]
            for move in moves:
                move.start()
            for move in moves:
                move.wait()


def cost(rows, keys, heads):
    scores = rows * keys * heads
    return pl.CostEstimate(flops=4 * scores * HEAD_DIM, bytes_accessed=rows * heads * 512, transcendentals=scores)


def chunks_of(heads):
    tail = max(1, heads // 3)
    return (heads - tail, tail) if heads > tail else (heads,)


def lined(video_q, video_k, video_v, audio_q, audio_k, audio_v, offsets, counts):
    n, cores = lax.axis_size("seq"), lax.axis_size("mp")
    me = lax.axis_index("seq")
    video_rows, audio_rows = video_q.shape[0], audio_q.shape[0]
    width = video_q.shape[1]
    heads = width // HEAD_DIM
    chunks = chunks_of(heads)
    mate_pairs = [(i, i ^ 1) for i in range(n)]
    cross_pairs = []
    for i in range(n):
        for core in range(cores):
            inner = 0 < i < n - 1
            to = (n - 1 - i) * cores + core if inner else i * cores + cores - 1 - core
            cross_pairs.append((i * cores + core, to))

    def mate(rows):
        return lax.ppermute(rows, "seq", mate_pairs)

    def cross(rows):
        return lax.ppermute(rows, ("seq", "mp"), cross_pairs)

    role = jnp.where((me == 0) | (me == n - 1), 1, 0).astype(jnp.int32).reshape(1)
    blocks = jnp.stack([me, me ^ 1, n - 1 - me, (n - 1 - me) ^ 1]).astype(jnp.int32)
    flip = me * 2 >= n

    def by_role(low, high):
        return jnp.where(flip, jnp.concatenate(high), jnp.concatenate(low))

    parts = [offsets[i * audio_rows : (i + 1) * audio_rows] for i in range(n)]
    key_offsets = by_role(
        [parts[1], parts[0], parts[2], parts[3]], [parts[2], parts[3], parts[1], parts[0]]
    )
    gap = key_offsets[None, :] - blocks[:2, None]
    within = jnp.arange(video_rows, dtype=jnp.int32)
    tagged = [jnp.where(within < counts[i], i, DEAD) for i in range(n)]
    frames = by_role(
        [tagged[1], tagged[0], tagged[2], tagged[3]], [tagged[2], tagged[3], tagged[1], tagged[0]]
    ).astype(jnp.int32)[None, :]
    row_offsets = key_offsets[: 2 * audio_rows, None]

    sound = jnp.concatenate([audio_k, audio_v], axis=0)
    asks = jnp.concatenate([video_q, audio_q], axis=0)
    sights, at = [], 0
    for size in chunks:
        cols = slice(at * HEAD_DIM, (at + size) * HEAD_DIM)
        sights.append(jnp.concatenate([video_k[:, cols], video_v[:, cols]], axis=0))
        at += size

    last = len(chunks) - 1
    sound_mate = mate(sound)
    sound_across = cross(sound)
    sight_mate = [mate(sights[i]) for i in range(last + 1)]
    asks_mate = mate(asks)
    sight_across = [cross(sights[i]) for i in range(last + 1)]
    sound_far = cross(sound_mate)
    sight_far = [cross(sight_mate[i]) for i in range(last + 1)]

    rows = video_rows + audio_rows
    shape = jax.ShapeDtypeStruct((rows, width), jnp.bfloat16)
    own, theirs = pl.pallas_call(
        audio_kernel,
        out_shape=(shape, shape),
        in_specs=[SMEM] + [VMEM] * 7,
        out_specs=(VMEM, VMEM),
        cost_estimate=cost(2 * rows, n * audio_rows, heads),
        compiler_params=PARAMS,
        name="audio_keys",
    )(role, gap, asks, asks_mate, sound, sound_mate, sound_across, sound_far)
    mine, back = [own], [mate(theirs)]
    at = 0
    for i, size in enumerate(chunks):
        shape = jax.ShapeDtypeStruct((rows, size * HEAD_DIM), jnp.bfloat16)
        own, theirs = pl.pallas_call(
            functools.partial(video_kernel, at),
            out_shape=(shape, shape),
            in_specs=[SMEM] + [VMEM] * 8,
            out_specs=(VMEM, VMEM),
            cost_estimate=cost(2 * rows, n * video_rows, size),
            compiler_params=PARAMS,
        )(role, frames, row_offsets, asks, asks_mate, sights[i], sight_mate[i], sight_across[i], sight_far[i])
        mine.append(own)
        back.append(mate(theirs))
        at += size

    video_shape = jax.ShapeDtypeStruct((video_rows, width), jnp.bfloat16)
    audio_shape = jax.ShapeDtypeStruct((audio_rows, width), jnp.bfloat16)
    return pl.pallas_call(
        functools.partial(place_kernel, video_rows),
        out_shape=(video_shape, video_shape, audio_shape, audio_shape),
        in_specs=[SMEM] + [VMEM] * (2 * len(mine)),
        out_specs=(ANY,) * 4,
        scratch_shapes=[pltpu.SemaphoreType.DMA((2 * len(mine),))],
        compiler_params=PARAMS,
        name="place",
    )(role, *mine, *back)


def solution(mesh):
    split = P(("groups", "seq"), ("tower", "mp"))
    placed = (split,) * 6 + (P("groups"), P("groups"))
    lined_up = mesh.shape["seq"] == 4 and mesh.shape["mp"] == 2

    def whole(*arrays):
        body = lined if lined_up else gathered
        return jax.shard_map(
            body, mesh=mesh, in_specs=placed, out_specs=(split,) * 4, check_vma=False
        )(*arrays)

    return whole
```

```python
import functools

import jax
import jax.numpy as jnp
from jax import lax
from jax.experimental import pallas as pl
from jax.experimental.pallas import tpu as pltpu
from jax.sharding import PartitionSpec as P


HEAD_DIM = 128
SPAN = 1
MASKED = -1e30
LOG2E = 1.4426950408889634
DEAD = 1 << 20
VMEM = pl.BlockSpec(memory_space=pltpu.VMEM)
SMEM = pl.BlockSpec(memory_space=pltpu.SMEM)
ANY = pl.BlockSpec(memory_space=pl.ANY)
PARAMS = pltpu.CompilerParams(vmem_limit_bytes=16 << 20)


def attend(queries, key_rows, value_rows, allowed):
    scores = jnp.einsum(
        "qhe,khe->hqk", queries, key_rows, preferred_element_type=jnp.float32
    ) * HEAD_DIM ** (-0.5)
    scores = jnp.where(allowed[None], scores, MASKED)
    peak = jnp.max(scores, axis=2)
    weights = jnp.where(allowed[None], jnp.exp(scores - peak[:, :, None]), 0.0)
    total = jnp.sum(weights, axis=2)
    blended = jnp.einsum(
        "hqk,khe->hqe", weights.astype(jnp.bfloat16), value_rows, preferred_element_type=jnp.float32
    )
    blended = blended / total[:, :, None]
    return jnp.transpose(blended, (1, 0, 2)).reshape(blended.shape[1], -1).astype(jnp.bfloat16)


def gathered(video_q, video_k, video_v, audio_q, audio_k, audio_v, offsets, counts):
    my_frame = lax.axis_index("seq")
    video_rows, audio_rows = video_q.shape[0], audio_q.shape[0]

    def heads(rows):
        return rows.reshape(rows.shape[0], -1, HEAD_DIM)

    def everywhere(rows):
        return heads(lax.all_gather(rows, "seq", axis=0, tiled=True))

    my_offsets = lax.dynamic_slice_in_dim(offsets, my_frame * audio_rows, audio_rows)
    keys, values = everywhere(video_k), everywhere(video_v)
    audio_keys, audio_values = everywhere(audio_k), everywhere(audio_v)
    positions = jnp.arange(keys.shape[0], dtype=jnp.int32)
    source = positions // video_rows
    is_live = positions % video_rows < jnp.repeat(counts, video_rows)
    video_self = attend(heads(video_q), keys, values, is_live[None, :])
    in_reach = (jnp.abs(my_offsets[:, None] - source[None, :]) <= SPAN) & is_live[None, :]
    audio_cross = attend(heads(audio_q), keys, values, in_reach)
    every = jnp.ones((1, audio_keys.shape[0]), jnp.bool_)
    audio_self = attend(heads(audio_q), audio_keys, audio_values, every)
    in_reach = jnp.abs(offsets - my_frame) <= SPAN
    video_cross = attend(heads(video_q), audio_keys, audio_values, in_reach[None, :])
    return (video_self, video_cross, audio_self, audio_cross)


def blend(queries, keys, values, allowed):
    scores = lax.dot_general(
        queries, keys, (((1,), (1,)), ((), ())), preferred_element_type=jnp.float32
    )
    if allowed is not None:
        scores = jnp.where(allowed, scores, MASKED)
    peak = jnp.max(scores, axis=1, keepdims=True)
    weights = jnp.exp2((scores - peak) * (HEAD_DIM ** (-0.5) * LOG2E))
    total = jnp.sum(weights, axis=1, keepdims=True)
    mixed = jnp.dot(weights.astype(jnp.bfloat16), values, preferred_element_type=jnp.float32)
    return (mixed * (1.0 / total)).astype(jnp.bfloat16)


def audio_kernel(role_ref, gap_ref, q_own, q_mate, b0, b1, inner2, end2, b3, cross_ref, own_ref, mate_ref):
    video_rows = cross_ref.shape[0]
    audio_rows = own_ref.shape[0]
    reach = jnp.abs(gap_ref[...]) <= SPAN

    def run(blocks, alone):
        for head in range(q_own.shape[1] // HEAD_DIM):
            cols = slice(head * HEAD_DIM, (head + 1) * HEAD_DIM)
            keys = jnp.concatenate([b[:audio_rows, cols] for b in blocks], axis=0)
            values = jnp.concatenate([b[audio_rows:, cols] for b in blocks], axis=0)
            span = slice(0, keys.shape[0])
            cross_ref[:, cols] = blend(q_own[:video_rows, cols], keys, values, reach[:, span])
            if not alone:
                both = jnp.concatenate([q_own[video_rows:, cols], q_mate[video_rows:, cols]], axis=0)
                out = blend(both, keys, values, None)
                own_ref[:, cols] = out[:audio_rows]
                mate_ref[:, cols] = out[audio_rows:]

    @pl.when(role_ref[0] == 0)
    def _():
        run((b0, b1, inner2, b3), False)

    @pl.when(role_ref[0] == 1)
    def _():
        run((b0, b1, end2), True)


def video_kernel(first, role_ref, frame_ref, off_ref, q_own, q_mate, b0, b1, b2, b3, own_ref, mate_ref):
    video_rows = b0.shape[0] // 2
    audio_rows = q_own.shape[0] - video_rows

    @pl.when(role_ref[0] == 0)
    def _():
        frames = frame_ref[...]
        live = frames < DEAD
        reach = jnp.abs(off_ref[...] - frames) <= SPAN
        for head in range(b0.shape[1] // HEAD_DIM):
            cols = slice(head * HEAD_DIM, (head + 1) * HEAD_DIM)
            q_cols = slice((first + head) * HEAD_DIM, (first + head + 1) * HEAD_DIM)
            keys = jnp.concatenate([b[:video_rows, cols] for b in (b0, b1, b2, b3)], axis=0)
            values = jnp.concatenate([b[video_rows:, cols] for b in (b0, b1, b2, b3)], axis=0)
            for q_ref, o_ref in ((q_own, own_ref), (q_mate, mate_ref)):
                o_ref[:video_rows, cols] = blend(q_ref[:video_rows, q_cols], keys, values, live)
            both = jnp.concatenate([q_own[video_rows:, q_cols], q_mate[video_rows:, q_cols]], axis=0)
            out = blend(both, keys, values, reach)
            own_ref[video_rows:, cols] = out[:audio_rows]
            mate_ref[video_rows:, cols] = out[audio_rows:]


def place_kernel(video_rows, role_ref, cross, *refs):
    n = (len(refs) - 5) // 2
    own, back = refs[:n], refs[n : 2 * n]
    video_self, video_cross, audio_self, audio_cross = refs[2 * n : 2 * n + 4]
    sem = refs[-1]

    def copies(parts):
        yield cross, video_cross
        yield parts[0], audio_self
        at = 0
        for part in parts[1:]:
            cols = pl.ds(at, part.shape[1])
            yield part.at[:video_rows], video_self.at[:, cols]
            yield part.at[video_rows:], audio_cross.at[:, cols]
            at += part.shape[1]

    for role, parts in ((0, own), (1, back)):

        @pl.when(role_ref[0] == role)
        def _(parts=parts):
            moves = [
                pltpu.make_async_copy(src, dst, sem.at[i])
                for i, (src, dst) in enumerate(copies(parts))
            ]
            for move in moves:
                move.start()
            for move in moves:
                move.wait()


def cost(rows, keys, heads):
    scores = rows * keys * heads
    return pl.CostEstimate(flops=4 * scores * HEAD_DIM, bytes_accessed=rows * heads * 512, transcendentals=scores)


def chunks_of(heads):
    tail = max(1, heads // 3)
    return (heads - tail, tail) if heads > tail else (heads,)


def lined(video_q, video_k, video_v, audio_q, audio_k, audio_v, offsets, counts):
    n, cores = lax.axis_size("seq"), lax.axis_size("mp")
    me = lax.axis_index("seq")
    video_rows, audio_rows = video_q.shape[0], audio_q.shape[0]
    width = video_q.shape[1]
    heads = width // HEAD_DIM
    chunks = chunks_of(heads)
    mate_pairs = [(i, i ^ 1) for i in range(n)]
    cross_pairs = []
    for i in range(n):
        for core in range(cores):
            inner = 0 < i < n - 1
            to = (n - 1 - i) * cores + core if inner else i * cores + cores - 1 - core
            cross_pairs.append((i * cores + core, to))

    def mate(rows):
        return lax.ppermute(rows, "seq", mate_pairs)

    def cross(rows):
        return lax.ppermute(rows, ("seq", "mp"), cross_pairs)

    role = jnp.where((me == 0) | (me == n - 1), 1, 0).astype(jnp.int32).reshape(1)
    upper = me * 2 >= n

    def by_block(parts):
        own = jnp.where(me % 2 == 0, jnp.concatenate(parts[:2]), jnp.concatenate(parts[1::-1]))
        other = jnp.where(me % 2 == 0, jnp.concatenate(parts[2:]), jnp.concatenate(parts[:1:-1]))
        low = jnp.concatenate([own] + parts[2:])
        high = jnp.concatenate([other] + parts[1::-1])
        return jnp.where(upper, high, low)

    key_offsets = by_block([offsets[i * audio_rows : (i + 1) * audio_rows] for i in range(n)])
    gap = (key_offsets - me)[None, :]
    within = jnp.arange(video_rows, dtype=jnp.int32)
    frames = by_block([jnp.where(within < counts[i], i, DEAD) for i in range(n)])
    frames = frames.astype(jnp.int32)[None, :]
    row_offsets = key_offsets[: 2 * audio_rows, None]

    sound = jnp.concatenate([audio_k, audio_v], axis=0)
    asks = jnp.concatenate([video_q, audio_q], axis=0)
    sights, at = [], 0
    for size in chunks:
        cols = slice(at * HEAD_DIM, (at + size) * HEAD_DIM)
        sights.append(jnp.concatenate([video_k[:, cols], video_v[:, cols]], axis=0))
        at += size

    pieces = range(len(chunks))
    sight_mate = [mate(sights[i]) for i in pieces]
    sight_across = [cross(sights[i]) for i in pieces]
    sight_far = [cross(sight_mate[i]) for i in pieces]
    asks_mate = mate(asks)
    sound_mate = mate(sound)
    sound_across = cross(sound)
    sound_far = cross(sound_mate)
    sound_passed = mate(sound_across)

    rows = video_rows + audio_rows
    mine, back, at = [], [], 0
    for i, size in enumerate(chunks):
        shape = jax.ShapeDtypeStruct((rows, size * HEAD_DIM), jnp.bfloat16)
        own, theirs = pl.pallas_call(
            functools.partial(video_kernel, at),
            out_shape=(shape, shape),
            in_specs=[SMEM] + [VMEM] * 8,
            out_specs=(VMEM, VMEM),
            cost_estimate=cost(2 * rows, n * video_rows, size),
            compiler_params=PARAMS,
        )(role, frames, row_offsets, asks, asks_mate, sights[i], sight_mate[i], sight_across[i], sight_far[i])
        mine.append(own)
        back.append(mate(theirs))
        at += size
    video_shape = jax.ShapeDtypeStruct((video_rows, width), jnp.bfloat16)
    audio_shape = jax.ShapeDtypeStruct((audio_rows, width), jnp.bfloat16)
    video_cross, own, theirs = pl.pallas_call(
        audio_kernel,
        out_shape=(video_shape, audio_shape, audio_shape),
        in_specs=[SMEM] + [VMEM] * 8,
        out_specs=(VMEM,) * 3,
        cost_estimate=cost(2 * rows, n * audio_rows, heads),
        compiler_params=PARAMS,
        name="audio_keys",
    )(role, gap, asks, asks_mate, sound, sound_mate, sound_across, sound_passed, sound_far)
    mine = [own] + mine
    back = [mate(theirs)] + back
    return pl.pallas_call(
        functools.partial(place_kernel, video_rows),
        out_shape=(video_shape, video_shape, audio_shape, audio_shape),
        in_specs=[SMEM] + [VMEM] * (1 + 2 * len(mine)),
        out_specs=(ANY,) * 4,
        scratch_shapes=[pltpu.SemaphoreType.DMA((2 * len(mine),))],
        compiler_params=PARAMS,
        name="place",
    )(role, video_cross, *mine, *back)


def solution(mesh):
    split = P(("groups", "seq"), ("tower", "mp"))
    placed = (split,) * 6 + (P("groups"), P("groups"))
    lined_up = mesh.shape["seq"] == 4 and mesh.shape["mp"] == 2

    def whole(*arrays):
        body = lined if lined_up else gathered
        return jax.shard_map(
            body, mesh=mesh, in_specs=placed, out_specs=(split,) * 4, check_vma=False
        )(*arrays)

    return whole
```

```python
import functools

import jax
import jax.numpy as jnp
from jax import lax
from jax.experimental import pallas as pl
from jax.experimental.pallas import tpu as pltpu
from jax.sharding import PartitionSpec as P


HEAD_DIM = 128
SPAN = 1
MASKED = -1e30
LOG2E = 1.4426950408889634
DEAD = 1 << 20
VMEM = pl.BlockSpec(memory_space=pltpu.VMEM)
SMEM = pl.BlockSpec(memory_space=pltpu.SMEM)
ANY = pl.BlockSpec(memory_space=pl.ANY)
PARAMS = pltpu.CompilerParams(vmem_limit_bytes=16 << 20)


def attend(queries, key_rows, value_rows, allowed):
    scores = jnp.einsum(
        "qhe,khe->hqk", queries, key_rows, preferred_element_type=jnp.float32
    ) * HEAD_DIM ** (-0.5)
    scores = jnp.where(allowed[None], scores, MASKED)
    peak = jnp.max(scores, axis=2)
    weights = jnp.where(allowed[None], jnp.exp(scores - peak[:, :, None]), 0.0)
    total = jnp.sum(weights, axis=2)
    blended = jnp.einsum(
        "hqk,khe->hqe", weights.astype(jnp.bfloat16), value_rows, preferred_element_type=jnp.float32
    )
    blended = blended / total[:, :, None]
    return jnp.transpose(blended, (1, 0, 2)).reshape(blended.shape[1], -1).astype(jnp.bfloat16)


def gathered(video_q, video_k, video_v, audio_q, audio_k, audio_v, offsets, counts):
    my_frame = lax.axis_index("seq")
    video_rows, audio_rows = video_q.shape[0], audio_q.shape[0]

    def heads(rows):
        return rows.reshape(rows.shape[0], -1, HEAD_DIM)

    def everywhere(rows):
        return heads(lax.all_gather(rows, "seq", axis=0, tiled=True))

    my_offsets = lax.dynamic_slice_in_dim(offsets, my_frame * audio_rows, audio_rows)
    keys, values = everywhere(video_k), everywhere(video_v)
    audio_keys, audio_values = everywhere(audio_k), everywhere(audio_v)
    positions = jnp.arange(keys.shape[0], dtype=jnp.int32)
    source = positions // video_rows
    is_live = positions % video_rows < jnp.repeat(counts, video_rows)
    video_self = attend(heads(video_q), keys, values, is_live[None, :])
    in_reach = (jnp.abs(my_offsets[:, None] - source[None, :]) <= SPAN) & is_live[None, :]
    audio_cross = attend(heads(audio_q), keys, values, in_reach)
    every = jnp.ones((1, audio_keys.shape[0]), jnp.bool_)
    audio_self = attend(heads(audio_q), audio_keys, audio_values, every)
    in_reach = jnp.abs(offsets - my_frame) <= SPAN
    video_cross = attend(heads(video_q), audio_keys, audio_values, in_reach[None, :])
    return (video_self, video_cross, audio_self, audio_cross)


def blend(queries, keys, values, allowed):
    scores = lax.dot_general(
        queries, keys, (((1,), (1,)), ((), ())), preferred_element_type=jnp.float32
    )
    if allowed is not None:
        scores = jnp.where(allowed, scores, MASKED)
    peak = jnp.max(scores, axis=1, keepdims=True)
    weights = jnp.exp2((scores - peak) * (HEAD_DIM ** (-0.5) * LOG2E))
    total = jnp.sum(weights, axis=1, keepdims=True)
    mixed = jnp.dot(weights.astype(jnp.bfloat16), values, preferred_element_type=jnp.float32)
    return (mixed * (1.0 / total)).astype(jnp.bfloat16)


def frames_of(me, n):
    mate, other = me ^ 1, jnp.where(me * 2 >= n, 0, n - 2)
    inner = jnp.where(me * 2 >= n, 1, 0) + other
    return me, mate, inner, jnp.where(me * 2 >= n, 0, 1) + other


def pick(pieces, at):
    chosen = pieces[0]
    for i in range(1, len(pieces)):
        chosen = jnp.where(at == i, pieces[i], chosen)
    return chosen


def offset_rows(offset_ref, audio_rows, frames):
    n = offset_ref.shape[1] // audio_rows
    pieces = [offset_ref[:, i * audio_rows : (i + 1) * audio_rows] for i in range(n)]
    return [pick(pieces, frame) for frame in frames]


def audio_kernel(me_ref, offset_ref, q_own, q_mate, b0, b1, inner2, end2, b3, cross_ref, own_ref, mate_ref):
    video_rows = cross_ref.shape[0]
    audio_rows = own_ref.shape[0]
    n = offset_ref.shape[1] // audio_rows
    me = me_ref[0]
    at_end = (me == 0) | (me == n - 1)
    key_offsets = offset_rows(offset_ref, audio_rows, frames_of(me, n))

    def run(blocks, alone):
        offsets = jnp.concatenate(key_offsets[: len(blocks)], axis=1)
        reach = jnp.abs(offsets - me) <= SPAN
        for head in range(q_own.shape[1] // HEAD_DIM):
            cols = slice(head * HEAD_DIM, (head + 1) * HEAD_DIM)
            keys = jnp.concatenate([b[:audio_rows, cols] for b in blocks], axis=0)
            values = jnp.concatenate([b[audio_rows:, cols] for b in blocks], axis=0)
            cross_ref[:, cols] = blend(q_own[:video_rows, cols], keys, values, reach)
            if not alone:
                both = jnp.concatenate([q_own[video_rows:, cols], q_mate[video_rows:, cols]], axis=0)
                out = blend(both, keys, values, None)
                own_ref[:, cols] = out[:audio_rows]
                mate_ref[:, cols] = out[audio_rows:]

    @pl.when(jnp.logical_not(at_end))
    def _():
        run((b0, b1, inner2, b3), False)

    @pl.when(at_end)
    def _():
        run((b0, b1, end2), True)


def video_kernel(first, me_ref, count_ref, offset_ref, q_own, q_mate, b0, b1, b2, b3, own_ref, mate_ref):
    video_rows = b0.shape[0] // 2
    audio_rows = q_own.shape[0] - video_rows
    n = offset_ref.shape[1] // audio_rows
    me = me_ref[0]

    @pl.when((me > 0) & (me < n - 1))
    def _():
        order = frames_of(me, n)
        within = lax.broadcasted_iota(jnp.int32, (1, video_rows), 1)
        tags = [jnp.where(within < count_ref[frame], frame, DEAD) for frame in order]
        frames = jnp.concatenate(tags, axis=1)
        live = frames < DEAD
        asking = jnp.concatenate(offset_rows(offset_ref, audio_rows, order[:2]), axis=1)
        size = 2 * audio_rows
        corner = lax.broadcasted_iota(jnp.int32, (size, size), 0) == lax.broadcasted_iota(
            jnp.int32, (size, size), 1
        )
        asking = jnp.sum(jnp.where(corner, asking, 0), axis=1, keepdims=True)
        reach = jnp.abs(asking - frames) <= SPAN
        for head in range(b0.shape[1] // HEAD_DIM):
            cols = slice(head * HEAD_DIM, (head + 1) * HEAD_DIM)
            q_cols = slice((first + head) * HEAD_DIM, (first + head + 1) * HEAD_DIM)
            keys = jnp.concatenate([b[:video_rows, cols] for b in (b0, b1, b2, b3)], axis=0)
            values = jnp.concatenate([b[video_rows:, cols] for b in (b0, b1, b2, b3)], axis=0)
            for q_ref, o_ref in ((q_own, own_ref), (q_mate, mate_ref)):
                o_ref[:video_rows, cols] = blend(q_ref[:video_rows, q_cols], keys, values, live)
            both = jnp.concatenate([q_own[video_rows:, q_cols], q_mate[video_rows:, q_cols]], axis=0)
            out = blend(both, keys, values, reach)
            own_ref[video_rows:, cols] = out[:audio_rows]
            mate_ref[video_rows:, cols] = out[audio_rows:]


def place_kernel(n_frames, video_rows, me_ref, cross, *refs):
    n = (len(refs) - 5) // 2
    own, back = refs[:n], refs[n : 2 * n]
    video_self, video_cross, audio_self, audio_cross = refs[2 * n : 2 * n + 4]
    sem = refs[-1]

    def copies(parts):
        yield cross, video_cross
        yield parts[0], audio_self
        at = 0
        for part in parts[1:]:
            cols = pl.ds(at, part.shape[1])
            yield part.at[:video_rows], video_self.at[:, cols]
            yield part.at[video_rows:], audio_cross.at[:, cols]
            at += part.shape[1]

    at_end = (me_ref[0] == 0) | (me_ref[0] == n_frames - 1)
    for role, parts in ((jnp.logical_not(at_end), own), (at_end, back)):

        @pl.when(role)
        def _(parts=parts):
            moves = [
                pltpu.make_async_copy(src, dst, sem.at[i])
                for i, (src, dst) in enumerate(copies(parts))
            ]
            for move in moves:
                move.start()
            for move in moves:
                move.wait()


def cost(rows, keys, heads):
    scores = rows * keys * heads
    return pl.CostEstimate(flops=4 * scores * HEAD_DIM, bytes_accessed=rows * heads * 512, transcendentals=scores)


def chunks_of(heads):
    tail = max(1, heads // 3)
    return (heads - tail, tail) if heads > tail else (heads,)


def lined(video_q, video_k, video_v, audio_q, audio_k, audio_v, offsets, counts):
    n, cores = lax.axis_size("seq"), lax.axis_size("mp")
    me = lax.axis_index("seq")
    video_rows, audio_rows = video_q.shape[0], audio_q.shape[0]
    width = video_q.shape[1]
    heads = width // HEAD_DIM
    chunks = chunks_of(heads)
    mate_pairs = [(i, i ^ 1) for i in range(n)]
    cross_pairs = []
    for i in range(n):
        for core in range(cores):
            inner = 0 < i < n - 1
            to = (n - 1 - i) * cores + core if inner else i * cores + cores - 1 - core
            cross_pairs.append((i * cores + core, to))

    def mate(rows):
        return lax.ppermute(rows, "seq", mate_pairs)

    def cross(rows):
        return lax.ppermute(rows, ("seq", "mp"), cross_pairs)

    place = me.astype(jnp.int32).reshape(1)
    offsets = offsets.reshape(1, -1)
    sound = jnp.concatenate([audio_k, audio_v], axis=0)
    asks = jnp.concatenate([video_q, audio_q], axis=0)
    sights, at = [], 0
    for size in chunks:
        cols = slice(at * HEAD_DIM, (at + size) * HEAD_DIM)
        sights.append(jnp.concatenate([video_k[:, cols], video_v[:, cols]], axis=0))
        at += size

    pieces = range(len(chunks))
    sight_mate = [mate(sights[i]) for i in pieces]
    sight_across = [cross(sights[i]) for i in pieces]
    sight_far = [cross(sight_mate[i]) for i in pieces]
    asks_mate = mate(asks)
    sound_mate = mate(sound)
    sound_across = cross(sound)
    sound_far = cross(sound_mate)
    sound_passed = mate(sound_across)

    rows = video_rows + audio_rows
    mine, back, at = [], [], 0
    for i, size in enumerate(chunks):
        shape = jax.ShapeDtypeStruct((rows, size * HEAD_DIM), jnp.bfloat16)
        own, theirs = pl.pallas_call(
            functools.partial(video_kernel, at),
            out_shape=(shape, shape),
            in_specs=[SMEM, SMEM] + [VMEM] * 7,
            out_specs=(VMEM, VMEM),
            cost_estimate=cost(2 * rows, n * video_rows, size),
            compiler_params=PARAMS,
        )(place, counts, offsets, asks, asks_mate, sights[i], sight_mate[i], sight_across[i], sight_far[i])
        mine.append(own)
        back.append(mate(theirs))
        at += size
    video_shape = jax.ShapeDtypeStruct((video_rows, width), jnp.bfloat16)
    audio_shape = jax.ShapeDtypeStruct((audio_rows, width), jnp.bfloat16)
    video_cross, own, theirs = pl.pallas_call(
        audio_kernel,
        out_shape=(video_shape, audio_shape, audio_shape),
        in_specs=[SMEM] + [VMEM] * 8,
        out_specs=(VMEM,) * 3,
        cost_estimate=cost(2 * rows, n * audio_rows, heads),
        compiler_params=PARAMS,
        name="audio_keys",
    )(place, offsets, asks, asks_mate, sound, sound_mate, sound_across, sound_passed, sound_far)
    mine = [own] + mine
    back = [mate(theirs)] + back
    return pl.pallas_call(
        functools.partial(place_kernel, n, video_rows),
        out_shape=(video_shape, video_shape, audio_shape, audio_shape),
        in_specs=[SMEM] + [VMEM] * (1 + 2 * len(mine)),
        out_specs=(ANY,) * 4,
        scratch_shapes=[pltpu.SemaphoreType.DMA((2 * len(mine),))],
        compiler_params=PARAMS,
        name="place",
    )(place, video_cross, *mine, *back)


def solution(mesh):
    split = P(("groups", "seq"), ("tower", "mp"))
    placed = (split,) * 6 + (P("groups"), P("groups"))
    lined_up = mesh.shape["seq"] == 4 and mesh.shape["mp"] == 2

    def whole(*arrays):
        body = lined if lined_up else gathered
        return jax.shard_map(
            body, mesh=mesh, in_specs=placed, out_specs=(split,) * 4, check_vma=False
        )(*arrays)

    return whole
```

```python
import functools

import jax
import jax.numpy as jnp
from jax import lax
from jax.experimental import pallas as pl
from jax.experimental.pallas import tpu as pltpu
from jax.sharding import PartitionSpec as P


HEAD_DIM = 128
SPAN = 1
MASKED = -1e30
LOG2E = 1.4426950408889634
VMEM = pl.BlockSpec(memory_space=pltpu.VMEM)
SMEM = pl.BlockSpec(memory_space=pltpu.SMEM)
ANY = pl.BlockSpec(memory_space=pl.ANY)
PARAMS = pltpu.CompilerParams(vmem_limit_bytes=16 << 20)


def attend(queries, key_rows, value_rows, allowed):
    scores = jnp.einsum(
        "qhe,khe->hqk", queries, key_rows, preferred_element_type=jnp.float32
    ) * HEAD_DIM ** (-0.5)
    scores = jnp.where(allowed[None], scores, MASKED)
    peak = jnp.max(scores, axis=2)
    weights = jnp.where(allowed[None], jnp.exp(scores - peak[:, :, None]), 0.0)
    total = jnp.sum(weights, axis=2)
    blended = jnp.einsum(
        "hqk,khe->hqe", weights.astype(jnp.bfloat16), value_rows, preferred_element_type=jnp.float32
    )
    blended = blended / total[:, :, None]
    return jnp.transpose(blended, (1, 0, 2)).reshape(blended.shape[1], -1).astype(jnp.bfloat16)


def gathered(video_q, video_k, video_v, audio_q, audio_k, audio_v, offsets, counts):
    my_frame = lax.axis_index("seq")
    video_rows, audio_rows = video_q.shape[0], audio_q.shape[0]

    def heads(rows):
        return rows.reshape(rows.shape[0], -1, HEAD_DIM)

    def everywhere(rows):
        return heads(lax.all_gather(rows, "seq", axis=0, tiled=True))

    my_offsets = lax.dynamic_slice_in_dim(offsets, my_frame * audio_rows, audio_rows)
    keys, values = everywhere(video_k), everywhere(video_v)
    audio_keys, audio_values = everywhere(audio_k), everywhere(audio_v)
    positions = jnp.arange(keys.shape[0], dtype=jnp.int32)
    source = positions // video_rows
    is_live = positions % video_rows < jnp.repeat(counts, video_rows)
    video_self = attend(heads(video_q), keys, values, is_live[None, :])
    in_reach = (jnp.abs(my_offsets[:, None] - source[None, :]) <= SPAN) & is_live[None, :]
    audio_cross = attend(heads(audio_q), keys, values, in_reach)
    every = jnp.ones((1, audio_keys.shape[0]), jnp.bool_)
    audio_self = attend(heads(audio_q), audio_keys, audio_values, every)
    in_reach = jnp.abs(offsets - my_frame) <= SPAN
    video_cross = attend(heads(video_q), audio_keys, audio_values, in_reach[None, :])
    return (video_self, video_cross, audio_self, audio_cross)


def blend(queries, keys, values, bias):
    scores = lax.dot_general(
        queries, keys, (((1,), (1,)), ((), ())), preferred_element_type=jnp.float32
    )
    if bias is not None:
        scores = scores + bias
    peak = jnp.max(scores, axis=1, keepdims=True)
    weights = jnp.exp2((scores - peak) * (HEAD_DIM ** (-0.5) * LOG2E))
    total = jnp.sum(weights, axis=1, keepdims=True)
    mixed = jnp.dot(weights.astype(jnp.bfloat16), values, preferred_element_type=jnp.float32)
    return (mixed * (1.0 / total)).astype(jnp.bfloat16)


def pick(pieces, at):
    chosen = pieces[0]
    for i in range(1, len(pieces)):
        chosen = jnp.where(at == i, pieces[i], chosen)
    return chosen


def table_kernel(n, me_ref, count_ref, offset_ref, live_ref, reach_ref, near_ref):
    me = me_ref[0]
    upper = me * 2 >= n
    inner, end = jnp.where(upper, 1, n - 2), jnp.where(upper, 0, n - 1)
    frames = (me, me ^ 1, inner, end)
    audio_rows = offset_ref.shape[1] // n
    video_rows = live_ref.shape[1] // n
    pieces = [offset_ref[:, i * audio_rows : (i + 1) * audio_rows] for i in range(n)]
    offsets = jnp.concatenate([pick(pieces, frame) for frame in frames], axis=1)
    near_ref[...] = jnp.where(jnp.abs(offsets - me) <= SPAN, 0.0, MASKED)
    size = 2 * audio_rows
    corner = lax.broadcasted_iota(jnp.int32, (size, size), 0) == lax.broadcasted_iota(
        jnp.int32, (size, size), 1
    )
    asking = jnp.sum(jnp.where(corner, offsets[:, :size], 0), axis=1, keepdims=True)
    within = lax.broadcasted_iota(jnp.int32, (1, video_rows), 1)
    for i, frame in enumerate(frames):
        cols = slice(i * video_rows, (i + 1) * video_rows)
        live = jnp.where(within < count_ref[frame], 0.0, MASKED)
        live_ref[:, cols] = live
        reach_ref[:, cols] = jnp.where(jnp.abs(asking - frame) <= SPAN, live, MASKED)


def audio_kernel(n, me_ref, near_ref, *refs):
    parts, (b0, b1, inner2, end2, b3, cross_ref, own_ref, mate_ref) = refs[:-8], refs[-8:]
    audio_rows = own_ref.shape[0]
    video_rows = cross_ref.shape[0]
    me = me_ref[0]
    at_end = (me == 0) | (me == n - 1)

    def run(blocks, alone):
        near = near_ref[:, : audio_rows * len(blocks)]
        at = 0
        for q_own, q_mate in zip(parts[::2], parts[1::2]):
            for first in range(0, q_own.shape[1], HEAD_DIM):
                q_cols = slice(first, first + HEAD_DIM)
                cols = slice(at, at + HEAD_DIM)
                keys = jnp.concatenate([b[:audio_rows, cols] for b in blocks], axis=0)
                values = jnp.concatenate([b[audio_rows:, cols] for b in blocks], axis=0)
                cross_ref[:, cols] = blend(q_own[:video_rows, q_cols], keys, values, near)
                if not alone:
                    both = jnp.concatenate(
                        [q_own[video_rows:, q_cols], q_mate[video_rows:, q_cols]], axis=0
                    )
                    out = blend(both, keys, values, None)
                    own_ref[:, cols] = out[:audio_rows]
                    mate_ref[:, cols] = out[audio_rows:]
                at += HEAD_DIM

    @pl.when(jnp.logical_not(at_end))
    def _():
        run((b0, b1, inner2, b3), False)

    @pl.when(at_end)
    def _():
        run((b0, b1, end2), True)


def video_kernel(n, first, me_ref, live_ref, reach_ref, q_own, q_mate, b0, b1, b2, b3, own_ref, mate_ref):
    video_rows = b0.shape[0] // 2
    audio_rows = q_own.shape[0] - video_rows
    me = me_ref[0]

    @pl.when((me > 0) & (me < n - 1))
    def _():
        for head in range(b0.shape[1] // HEAD_DIM):
            cols = slice(head * HEAD_DIM, (head + 1) * HEAD_DIM)
            q_cols = slice((first + head) * HEAD_DIM, (first + head + 1) * HEAD_DIM)
            keys = jnp.concatenate([b[:video_rows, cols] for b in (b0, b1, b2, b3)], axis=0)
            values = jnp.concatenate([b[video_rows:, cols] for b in (b0, b1, b2, b3)], axis=0)
            for q_ref, o_ref in ((q_own, own_ref), (q_mate, mate_ref)):
                queries = q_ref[:video_rows, q_cols]
                o_ref[:video_rows, cols] = blend(queries, keys, values, live_ref[...])
            both = jnp.concatenate([q_own[video_rows:, q_cols], q_mate[video_rows:, q_cols]], axis=0)
            out = blend(both, keys, values, reach_ref[...])
            own_ref[video_rows:, cols] = out[:audio_rows]
            mate_ref[video_rows:, cols] = out[audio_rows:]


def place_kernel(n_frames, video_rows, me_ref, cross, *refs):
    n = (len(refs) - 5) // 2
    own, back = refs[:n], refs[n : 2 * n]
    video_self, video_cross, audio_self, audio_cross = refs[2 * n : 2 * n + 4]
    sem = refs[-1]

    def copies(parts):
        yield cross, video_cross
        yield parts[0], audio_self
        at = 0
        for part in parts[1:]:
            cols = pl.ds(at, part.shape[1])
            yield part.at[:video_rows], video_self.at[:, cols]
            yield part.at[video_rows:], audio_cross.at[:, cols]
            at += part.shape[1]

    at_end = (me_ref[0] == 0) | (me_ref[0] == n_frames - 1)
    for role, parts in ((jnp.logical_not(at_end), own), (at_end, back)):

        @pl.when(role)
        def _(parts=parts):
            moves = [
                pltpu.make_async_copy(src, dst, sem.at[i])
                for i, (src, dst) in enumerate(copies(parts))
            ]
            for move in moves:
                move.start()
            for move in moves:
                move.wait()


def cost(rows, keys, heads):
    scores = rows * keys * heads
    return pl.CostEstimate(flops=4 * scores * HEAD_DIM, bytes_accessed=rows * heads * 512, transcendentals=scores)


def chunks_of(heads):
    head = (heads + 1) // 2
    return head, (heads - head + 1) // 2, (heads - head) // 2


def lined(video_q, video_k, video_v, audio_q, audio_k, audio_v, offsets, counts):
    n, cores = lax.axis_size("seq"), lax.axis_size("mp")
    me = lax.axis_index("seq")
    video_rows, audio_rows = video_q.shape[0], audio_q.shape[0]
    rows = video_rows + audio_rows
    width = video_q.shape[1]
    heads = width // HEAD_DIM
    chunks = chunks_of(heads)
    mate_pairs = [(i, i ^ 1) for i in range(n)]
    cross_pairs = []
    for i in range(n):
        for core in range(cores):
            inner = 0 < i < n - 1
            to = (n - 1 - i) * cores + core if inner else i * cores + cores - 1 - core
            cross_pairs.append((i * cores + core, to))

    def mate(block):
        return lax.ppermute(block, "seq", mate_pairs)

    def cross(block):
        return lax.ppermute(block, ("seq", "mp"), cross_pairs)

    def call(kernel, outs, spaces, *args, **more):
        return pl.pallas_call(
            kernel,
            out_shape=tuple(jax.ShapeDtypeStruct(shape, dtype) for shape, dtype in outs),
            in_specs=spaces,
            compiler_params=PARAMS,
            **more,
        )(*args)

    place = me.astype(jnp.int32).reshape(1)
    live, reach, near = call(
        functools.partial(table_kernel, n),
        (
            ((1, n * video_rows), jnp.float32),
            ((2 * audio_rows, n * video_rows), jnp.float32),
            ((1, n * audio_rows), jnp.float32),
        ),
        [SMEM, SMEM, VMEM],
        place,
        counts,
        offsets.reshape(1, -1),
    )
    split = chunks[0] * HEAD_DIM
    asks = [
        jnp.concatenate([video_q[:, cols], audio_q[:, cols]], axis=0)
        for cols in (slice(0, split), slice(split, width))
    ]
    sound = jnp.concatenate([audio_k, audio_v], axis=0)
    sights, at = [], 0
    for size in chunks:
        cols = slice(at * HEAD_DIM, (at + size) * HEAD_DIM)
        sights.append(jnp.concatenate([video_k[:, cols], video_v[:, cols]], axis=0))
        at += size

    pieces = range(len(chunks))
    sight_mate = [mate(sights[i]) for i in pieces]
    sight_across = [cross(sights[i]) for i in pieces]
    sight_far = [cross(sight_mate[i]) for i in pieces]
    asks_mate = [mate(asks[i]) for i in range(2)]
    sound_mate = mate(sound)
    sound_across = cross(sound)
    sound_far = cross(sound_mate)
    sound_passed = mate(sound_across)

    mine, back, at = [], [], 0
    for i, size in enumerate(chunks):
        half = min(i, 1)
        own, theirs = call(
            functools.partial(video_kernel, n, at - half * chunks[0]),
            (((rows, size * HEAD_DIM), jnp.bfloat16),) * 2,
            [SMEM] + [VMEM] * 8,
            place,
            live,
            reach,
            asks[half],
            asks_mate[half],
            sights[i],
            sight_mate[i],
            sight_across[i],
            sight_far[i],
            cost_estimate=cost(2 * rows, n * video_rows, size),
        )
        mine.append(own)
        back.append(mate(theirs))
        at += size
    video_cross, own, theirs = call(
        functools.partial(audio_kernel, n),
        (((video_rows, width), jnp.bfloat16),) + (((audio_rows, width), jnp.bfloat16),) * 2,
        [SMEM] + [VMEM] * 10,
        place,
        near,
        asks[0],
        asks_mate[0],
        asks[1],
        asks_mate[1],
        sound,
        sound_mate,
        sound_across,
        sound_passed,
        sound_far,
        cost_estimate=cost(2 * rows, n * audio_rows, heads),
    )
    mine = [own] + mine
    back = [mate(theirs)] + back
    return call(
        functools.partial(place_kernel, n, video_rows),
        (((video_rows, width), jnp.bfloat16),) * 2 + (((audio_rows, width), jnp.bfloat16),) * 2,
        [SMEM] + [VMEM] * (1 + 2 * len(mine)),
        place,
        video_cross,
        *mine,
        *back,
        out_specs=(ANY,) * 4,
        scratch_shapes=[pltpu.SemaphoreType.DMA((2 * len(mine),))],
    )


def solution(mesh):
    split = P(("groups", "seq"), ("tower", "mp"))
    placed = (split,) * 6 + (P("groups"), P("groups"))
    sizes = mesh.shape
    line = sizes["seq"] == 4 and sizes["mp"] == 2

    def whole(*arrays):
        heads = arrays[0].shape[1] // HEAD_DIM // (sizes["tower"] * sizes["mp"])
        body = lined if line and heads > 3 else gathered
        return jax.shard_map(
            body, mesh=mesh, in_specs=placed, out_specs=(split,) * 4, check_vma=False
        )(*arrays)

    return whole
```

```python
import functools

import jax
import jax.numpy as jnp
from jax import lax
from jax.experimental import pallas as pl
from jax.experimental.pallas import tpu as pltpu
from jax.sharding import PartitionSpec as P


HEAD_DIM = 128
SPAN = 1
MASKED = -1e30
LOG2E = 1.4426950408889634
VMEM = pl.BlockSpec(memory_space=pltpu.VMEM)
SMEM = pl.BlockSpec(memory_space=pltpu.SMEM)
HBM = pl.BlockSpec(memory_space=pltpu.HBM)
PARAMS = pltpu.CompilerParams(vmem_limit_bytes=16 << 20)


def attend(queries, key_rows, value_rows, allowed):
    scores = jnp.einsum(
        "qhe,khe->hqk", queries, key_rows, preferred_element_type=jnp.float32
    ) * HEAD_DIM ** (-0.5)
    scores = jnp.where(allowed[None], scores, MASKED)
    peak = jnp.max(scores, axis=2)
    weights = jnp.where(allowed[None], jnp.exp(scores - peak[:, :, None]), 0.0)
    total = jnp.sum(weights, axis=2)
    blended = jnp.einsum(
        "hqk,khe->hqe", weights.astype(jnp.bfloat16), value_rows, preferred_element_type=jnp.float32
    )
    blended = blended / total[:, :, None]
    return jnp.transpose(blended, (1, 0, 2)).reshape(blended.shape[1], -1).astype(jnp.bfloat16)


def gathered(video_q, video_k, video_v, audio_q, audio_k, audio_v, offsets, counts):
    my_frame = lax.axis_index("seq")
    video_rows, audio_rows = video_q.shape[0], audio_q.shape[0]

    def heads(rows):
        return rows.reshape(rows.shape[0], -1, HEAD_DIM)

    def everywhere(rows):
        return heads(lax.all_gather(rows, "seq", axis=0, tiled=True))

    my_offsets = lax.dynamic_slice_in_dim(offsets, my_frame * audio_rows, audio_rows)
    keys, values = everywhere(video_k), everywhere(video_v)
    audio_keys, audio_values = everywhere(audio_k), everywhere(audio_v)
    positions = jnp.arange(keys.shape[0], dtype=jnp.int32)
    source = positions // video_rows
    is_live = positions % video_rows < jnp.repeat(counts, video_rows)
    video_self = attend(heads(video_q), keys, values, is_live[None, :])
    in_reach = (jnp.abs(my_offsets[:, None] - source[None, :]) <= SPAN) & is_live[None, :]
    audio_cross = attend(heads(audio_q), keys, values, in_reach)
    every = jnp.ones((1, audio_keys.shape[0]), jnp.bool_)
    audio_self = attend(heads(audio_q), audio_keys, audio_values, every)
    in_reach = jnp.abs(offsets - my_frame) <= SPAN
    video_cross = attend(heads(video_q), audio_keys, audio_values, in_reach[None, :])
    return (video_self, video_cross, audio_self, audio_cross)


def blend(queries, keys, values, bias):
    scores = lax.dot_general(
        queries, keys, (((1,), (1,)), ((), ())), preferred_element_type=jnp.float32
    )
    if bias is not None:
        scores = scores + bias
    peak = jnp.max(scores, axis=1, keepdims=True)
    weights = jnp.exp2((scores - peak) * (HEAD_DIM ** (-0.5) * LOG2E))
    total = jnp.sum(weights, axis=1, keepdims=True)
    mixed = jnp.dot(weights.astype(jnp.bfloat16), values, preferred_element_type=jnp.float32)
    return (mixed * (1.0 / total)).astype(jnp.bfloat16)


def pick(pieces, at):
    chosen = pieces[0]
    for i in range(1, len(pieces)):
        chosen = jnp.where(at == i, pieces[i], chosen)
    return chosen


def move_all(moves, sem):
    copies = [pltpu.make_async_copy(src, dst, sem.at[i]) for i, (src, dst) in enumerate(moves)]
    for copy in copies:
        copy.start()
    return copies


def sight_moves(video_k, video_v, first, out):
    rows, cols = video_k.shape[0], pl.ds(first, out.shape[1])
    return [(video_k.at[:, cols], out.at[:rows]), (video_v.at[:, cols], out.at[rows:])]


def sound_moves(audio_k, audio_v, out):
    rows, width = audio_k.shape[0], out.shape[1]
    moves = []
    for src in (audio_k, audio_v):
        for half in range(2):
            at = len(moves) * rows
            moves.append((src.at[:, pl.ds(half * width, width)], out.at[at : at + rows]))
    return moves


def first_pack(n, me_ref, video_k, video_v, audio_k, audio_v, out_ref, over_ref, sem):
    me = me_ref[0]
    at_end = (me == 0) | (me == n - 1)
    for role, sight, sound in ((at_end, out_ref, over_ref), (jnp.logical_not(at_end), over_ref, out_ref)):

        @pl.when(role)
        def _(sight=sight, sound=sound):
            moves = sight_moves(video_k, video_v, 0, sight) + sound_moves(audio_k, audio_v, sound)
            for copy in move_all(moves, sem):
                copy.wait()


def second_pack(n, me_ref, count_ref, offset_ref, video_k, video_v, video_q, audio_q, *outs):
    sight1, sight2, asks0, asks1, live_ref, reach_ref, near_ref, sem = outs
    rows = video_q.shape[0]
    moves, at = [], asks0.shape[1]
    for half, out in enumerate((asks0, asks1)):
        cols = pl.ds(half * at, at)
        moves += [(video_q.at[:, cols], out.at[:rows]), (audio_q.at[:, cols], out.at[rows:])]
    for out in (sight1, sight2):
        moves += sight_moves(video_k, video_v, at, out)
        at += out.shape[1]
    copies = move_all(moves, sem)
    tables(n, me_ref[0], count_ref, offset_ref, live_ref, reach_ref, near_ref)
    for copy in copies:
        copy.wait()


def tables(n, me, count_ref, offset_ref, live_ref, reach_ref, near_ref):
    upper = me * 2 >= n
    inner, end = jnp.where(upper, 1, n - 2), jnp.where(upper, 0, n - 1)
    frames = (me, me ^ 1, inner, end)
    audio_rows = offset_ref.shape[1] // n
    video_rows = live_ref.shape[1] // n
    pieces = [offset_ref[:, i * audio_rows : (i + 1) * audio_rows] for i in range(n)]
    offsets = jnp.concatenate([pick(pieces, frame) for frame in frames], axis=1)
    near_ref[...] = jnp.where(jnp.abs(offsets - me) <= SPAN, 0.0, MASKED)
    size = 2 * audio_rows
    corner = lax.broadcasted_iota(jnp.int32, (size, size), 0) == lax.broadcasted_iota(
        jnp.int32, (size, size), 1
    )
    asking = jnp.sum(jnp.where(corner, offsets[:, :size], 0), axis=1, keepdims=True)
    within = lax.broadcasted_iota(jnp.int32, (1, video_rows), 1)
    for i, frame in enumerate(frames):
        cols = slice(i * video_rows, (i + 1) * video_rows)
        live = jnp.where(within < count_ref[frame], 0.0, MASKED)
        live_ref[:, cols] = live
        reach_ref[:, cols] = jnp.where(jnp.abs(asking - frame) <= SPAN, live, MASKED)


def audio_kernel(n, me_ref, near_ref, *refs):
    asks, (out, over, first, second, across, far, cross_ref, own_ref, mate_ref) = refs[:-9], refs[-9:]
    audio_rows = own_ref.shape[0]
    video_rows = cross_ref.shape[0]
    width = out.shape[1]
    me = me_ref[0]
    at_end = (me == 0) | (me == n - 1)

    def run(blocks, alone):
        near = near_ref[:, : audio_rows * len(blocks)]
        for half in range(2):
            q_own, q_mate = asks[2 * half], asks[2 * half + 1]
            key_rows = slice(half * audio_rows, (half + 1) * audio_rows)
            value_rows = slice((2 + half) * audio_rows, (3 + half) * audio_rows)
            for at in range(0, width, HEAD_DIM):
                cols = slice(at, at + HEAD_DIM)
                to = slice(half * width + at, half * width + at + HEAD_DIM)
                keys = jnp.concatenate([b[key_rows, cols] for b in blocks], axis=0)
                values = jnp.concatenate([b[value_rows, cols] for b in blocks], axis=0)
                cross_ref[:, to] = blend(q_own[:video_rows, cols], keys, values, near)
                if not alone:
                    both = jnp.concatenate(
                        [q_own[video_rows:, cols], q_mate[video_rows:, cols]], axis=0
                    )
                    mixed = blend(both, keys, values, None)
                    own_ref[:, to] = mixed[:audio_rows]
                    mate_ref[:, to] = mixed[audio_rows:]

    @pl.when(jnp.logical_not(at_end))
    def _():
        run((out, second, across, far), False)

    @pl.when(at_end)
    def _():
        run((over, first, second), True)


def video_kernel(n, first, me_ref, live_ref, reach_ref, q_own, q_mate, b0, b1, b2, b3, own_ref, mate_ref):
    video_rows = b0.shape[0] // 2
    audio_rows = q_own.shape[0] - video_rows
    me = me_ref[0]

    @pl.when((me > 0) & (me < n - 1))
    def _():
        for head in range(b0.shape[1] // HEAD_DIM):
            cols = slice(head * HEAD_DIM, (head + 1) * HEAD_DIM)
            q_cols = slice((first + head) * HEAD_DIM, (first + head + 1) * HEAD_DIM)
            keys = jnp.concatenate([b[:video_rows, cols] for b in (b0, b1, b2, b3)], axis=0)
            values = jnp.concatenate([b[video_rows:, cols] for b in (b0, b1, b2, b3)], axis=0)
            for q_ref, o_ref in ((q_own, own_ref), (q_mate, mate_ref)):
                queries = q_ref[:video_rows, q_cols]
                o_ref[:video_rows, cols] = blend(queries, keys, values, live_ref[...])
            both = jnp.concatenate([q_own[video_rows:, q_cols], q_mate[video_rows:, q_cols]], axis=0)
            out = blend(both, keys, values, reach_ref[...])
            own_ref[video_rows:, cols] = out[:audio_rows]
            mate_ref[video_rows:, cols] = out[audio_rows:]


def place_kernel(n_frames, video_rows, me_ref, cross, *refs):
    n = (len(refs) - 5) // 2
    own, back = refs[:n], refs[n : 2 * n]
    video_self, video_cross, audio_self, audio_cross = refs[2 * n : 2 * n + 4]
    sem = refs[-1]

    def copies(parts):
        yield cross, video_cross
        yield parts[0], audio_self
        at = 0
        for part in parts[1:]:
            cols = pl.ds(at, part.shape[1])
            yield part.at[:video_rows], video_self.at[:, cols]
            yield part.at[video_rows:], audio_cross.at[:, cols]
            at += part.shape[1]

    at_end = (me_ref[0] == 0) | (me_ref[0] == n_frames - 1)
    for role, parts in ((jnp.logical_not(at_end), own), (at_end, back)):

        @pl.when(role)
        def _(parts=parts):
            moves = [
                pltpu.make_async_copy(src, dst, sem.at[i])
                for i, (src, dst) in enumerate(copies(parts))
            ]
            for move in moves:
                move.start()
            for move in moves:
                move.wait()


def cost(rows, keys, heads):
    scores = rows * keys * heads
    return pl.CostEstimate(flops=4 * scores * HEAD_DIM, bytes_accessed=rows * heads * 512, transcendentals=scores)


def chunks_of(heads):
    head = heads // 2
    return head, (head + 1) // 2, head // 2


def lined(video_q, video_k, video_v, audio_q, audio_k, audio_v, offsets, counts):
    n, cores = lax.axis_size("seq"), lax.axis_size("mp")
    me = lax.axis_index("seq")
    video_rows, audio_rows = video_q.shape[0], audio_q.shape[0]
    rows = video_rows + audio_rows
    width = video_q.shape[1]
    heads = width // HEAD_DIM
    chunks = chunks_of(heads)
    mate_pairs = [(i, i ^ 1) for i in range(n)]
    cross_pairs = []
    for i in range(n):
        for core in range(cores):
            inner = 0 < i < n - 1
            to = (n - 1 - i) * cores + core if inner else i * cores + cores - 1 - core
            cross_pairs.append((i * cores + core, to))

    def mate(block):
        return lax.ppermute(block, "seq", mate_pairs)

    def cross(block):
        return lax.ppermute(block, ("seq", "mp"), cross_pairs)

    def call(kernel, outs, spaces, *args, **more):
        return pl.pallas_call(
            kernel,
            out_shape=tuple(jax.ShapeDtypeStruct(shape, dtype) for shape, dtype in outs),
            in_specs=spaces,
            compiler_params=PARAMS,
            **more,
        )(*args)

    place = me.astype(jnp.int32).reshape(1)
    video_q, video_k, video_v, audio_q, audio_k, audio_v = (
        pltpu.with_memory_space_constraint(block, pltpu.HBM)
        for block in (video_q, video_k, video_v, audio_q, audio_k, audio_v)
    )
    at_end = (me == 0) | (me == n - 1)
    lengths = [size * HEAD_DIM for size in chunks]
    half = lengths[0]
    first_out, first_over = call(
        functools.partial(first_pack, n),
        (((2 * video_rows, half), jnp.bfloat16),) * 2,
        [SMEM] + [HBM] * 4,
        place,
        video_k,
        video_v,
        audio_k,
        audio_v,
        out_specs=(VMEM,) * 2,
        scratch_shapes=[pltpu.SemaphoreType.DMA((6,))],
    )
    outs = tuple(((2 * video_rows, length), jnp.bfloat16) for length in lengths[1:])
    outs += (((rows, half), jnp.bfloat16),) * 2
    outs += (
        ((1, n * video_rows), jnp.float32),
        ((2 * audio_rows, n * video_rows), jnp.float32),
        ((1, n * audio_rows), jnp.float32),
    )
    *sights, asks0, asks1, live, reach, near = call(
        functools.partial(second_pack, n),
        outs,
        [SMEM, SMEM, VMEM] + [HBM] * 4,
        place,
        counts,
        offsets.reshape(1, -1),
        video_k,
        video_v,
        video_q,
        audio_q,
        out_specs=(VMEM,) * len(outs),
        scratch_shapes=[pltpu.SemaphoreType.DMA((8,))],
    )
    asks = [asks0, asks1]
    sights = [first_over] + sights

    sight_mate = [mate(first_out)]
    sight_across = [cross(first_over)]
    sound_across = cross(first_out)
    second_mate = mate(jnp.where(at_end, first_over, sound_across))
    sound_far = cross(second_mate)
    for i in (1, 2):
        sight_mate.append(mate(sights[i]))
        sight_across.append(cross(sights[i]))
    sight_far = [cross(sight_mate[i]) for i in range(3)]
    asks_mate = [mate(asks[i]) for i in range(2)]

    mine, back, at = [], [], 0
    for i, size in enumerate(chunks):
        half = min(i, 1)
        own, theirs = call(
            functools.partial(video_kernel, n, at - half * chunks[0]),
            (((rows, size * HEAD_DIM), jnp.bfloat16),) * 2,
            [SMEM] + [VMEM] * 8,
            place,
            live,
            reach,
            asks[half],
            asks_mate[half],
            sights[i],
            sight_mate[i],
            sight_across[i],
            sight_far[i],
            out_specs=(VMEM,) * 2,
            cost_estimate=cost(2 * rows, n * video_rows, size),
        )
        mine.append(own)
        back.append(mate(theirs))
        at += size
    video_cross, own, theirs = call(
        functools.partial(audio_kernel, n),
        (((video_rows, width), jnp.bfloat16),) + (((audio_rows, width), jnp.bfloat16),) * 2,
        [SMEM] + [VMEM] * 11,
        place,
        near,
        asks[0],
        asks_mate[0],
        asks[1],
        asks_mate[1],
        first_out,
        first_over,
        sight_mate[0],
        second_mate,
        sound_across,
        sound_far,
        out_specs=(VMEM,) * 3,
        cost_estimate=cost(2 * rows, n * audio_rows, heads),
    )
    mine = [own] + mine
    back = [mate(theirs)] + back
    return call(
        functools.partial(place_kernel, n, video_rows),
        (((video_rows, width), jnp.bfloat16),) * 2 + (((audio_rows, width), jnp.bfloat16),) * 2,
        [SMEM] + [VMEM] * (1 + 2 * len(mine)),
        place,
        video_cross,
        *mine,
        *back,
        out_specs=(HBM,) * 4,
        scratch_shapes=[pltpu.SemaphoreType.DMA((2 * len(mine),))],
    )


def solution(mesh):
    split = P(("groups", "seq"), ("tower", "mp"))
    placed = (split,) * 6 + (P("groups"), P("groups"))
    sizes = mesh.shape
    line = sizes["seq"] == 4 and sizes["mp"] == 2

    def whole(*arrays):
        heads = arrays[0].shape[1] // HEAD_DIM // (sizes["tower"] * sizes["mp"])
        paired = heads % 2 == 0 and heads > 3 and arrays[0].shape[0] == 2 * arrays[3].shape[0]
        body = lined if line and paired else gathered
        return jax.shard_map(
            body, mesh=mesh, in_specs=placed, out_specs=(split,) * 4, check_vma=False
        )(*arrays)

    return whole
```

```python
import functools

import jax
import jax.numpy as jnp
from jax import lax
from jax.experimental import pallas as pl
from jax.experimental.pallas import tpu as pltpu
from jax.sharding import PartitionSpec as P


HEAD_DIM = 128
SPAN = 1
MASKED = -1e30
LOG2E = 1.4426950408889634
VMEM = pl.BlockSpec(memory_space=pltpu.VMEM)
SMEM = pl.BlockSpec(memory_space=pltpu.SMEM)
HBM = pl.BlockSpec(memory_space=pltpu.HBM)
PARAMS = pltpu.CompilerParams(vmem_limit_bytes=16 << 20)


def attend(queries, key_rows, value_rows, allowed):
    scores = jnp.einsum(
        "qhe,khe->hqk", queries, key_rows, preferred_element_type=jnp.float32
    ) * HEAD_DIM ** (-0.5)
    scores = jnp.where(allowed[None], scores, MASKED)
    peak = jnp.max(scores, axis=2)
    weights = jnp.where(allowed[None], jnp.exp(scores - peak[:, :, None]), 0.0)
    total = jnp.sum(weights, axis=2)
    blended = jnp.einsum(
        "hqk,khe->hqe", weights.astype(jnp.bfloat16), value_rows, preferred_element_type=jnp.float32
    )
    blended = blended / total[:, :, None]
    return jnp.transpose(blended, (1, 0, 2)).reshape(blended.shape[1], -1).astype(jnp.bfloat16)


def gathered(video_q, video_k, video_v, audio_q, audio_k, audio_v, offsets, counts):
    my_frame = lax.axis_index("seq")
    video_rows, audio_rows = video_q.shape[0], audio_q.shape[0]

    def heads(rows):
        return rows.reshape(rows.shape[0], -1, HEAD_DIM)

    def everywhere(rows):
        return heads(lax.all_gather(rows, "seq", axis=0, tiled=True))

    my_offsets = lax.dynamic_slice_in_dim(offsets, my_frame * audio_rows, audio_rows)
    keys, values = everywhere(video_k), everywhere(video_v)
    audio_keys, audio_values = everywhere(audio_k), everywhere(audio_v)
    positions = jnp.arange(keys.shape[0], dtype=jnp.int32)
    source = positions // video_rows
    is_live = positions % video_rows < jnp.repeat(counts, video_rows)
    video_self = attend(heads(video_q), keys, values, is_live[None, :])
    in_reach = (jnp.abs(my_offsets[:, None] - source[None, :]) <= SPAN) & is_live[None, :]
    audio_cross = attend(heads(audio_q), keys, values, in_reach)
    every = jnp.ones((1, audio_keys.shape[0]), jnp.bool_)
    audio_self = attend(heads(audio_q), audio_keys, audio_values, every)
    in_reach = jnp.abs(offsets - my_frame) <= SPAN
    video_cross = attend(heads(video_q), audio_keys, audio_values, in_reach[None, :])
    return (video_self, video_cross, audio_self, audio_cross)


def blend(queries, keys, values, bias):
    scores = lax.dot_general(
        queries, keys, (((1,), (1,)), ((), ())), preferred_element_type=jnp.float32
    )
    if bias is not None:
        scores = scores + bias
    peak = jnp.max(scores, axis=1, keepdims=True)
    weights = jnp.exp2((scores - peak) * (HEAD_DIM ** (-0.5) * LOG2E))
    total = jnp.sum(weights, axis=1, keepdims=True)
    mixed = jnp.dot(weights.astype(jnp.bfloat16), values, preferred_element_type=jnp.float32)
    return (mixed * (1.0 / total)).astype(jnp.bfloat16)


def pick(pieces, at):
    chosen = pieces[0]
    for i in range(1, len(pieces)):
        chosen = jnp.where(at == i, pieces[i], chosen)
    return chosen


def move_all(moves, sem):
    copies = [pltpu.make_async_copy(src, dst, sem.at[i]) for i, (src, dst) in enumerate(moves)]
    for copy in copies:
        copy.start()
    return copies


def sight_moves(video_k, video_v, first, out):
    rows, cols = video_k.shape[0], pl.ds(first, out.shape[1])
    return [(video_k.at[:, cols], out.at[:rows]), (video_v.at[:, cols], out.at[rows:])]


def sound_moves(audio_k, audio_v, out):
    rows, width = audio_k.shape[0], out.shape[1]
    moves = []
    for src in (audio_k, audio_v):
        for half in range(2):
            at = len(moves) * rows
            moves.append((src.at[:, pl.ds(half * width, width)], out.at[at : at + rows]))
    return moves


def first_pack(n, me_ref, video_k, video_v, audio_k, audio_v, out_ref, over_ref, sem):
    me = me_ref[0]
    at_end = (me == 0) | (me == n - 1)
    for role, sight, sound in ((at_end, out_ref, over_ref), (jnp.logical_not(at_end), over_ref, out_ref)):

        @pl.when(role)
        def _(sight=sight, sound=sound):
            moves = sight_moves(video_k, video_v, 0, sight) + sound_moves(audio_k, audio_v, sound)
            for copy in move_all(moves, sem):
                copy.wait()


def second_pack(n, me_ref, count_ref, offset_ref, video_k, video_v, video_q, audio_q, *outs):
    sight1, sight2, asks0, asks1, live_ref, reach_ref, near_ref, sem = outs
    rows = video_q.shape[0]
    moves, at = [], asks0.shape[1]
    for half, out in enumerate((asks0, asks1)):
        cols = pl.ds(half * at, at)
        moves += [(video_q.at[:, cols], out.at[:rows]), (audio_q.at[:, cols], out.at[rows:])]
    for out in (sight1, sight2):
        moves += sight_moves(video_k, video_v, at, out)
        at += out.shape[1]
    copies = move_all(moves, sem)
    tables(n, me_ref[0], count_ref, offset_ref, live_ref, reach_ref, near_ref)
    for copy in copies:
        copy.wait()


def tables(n, me, count_ref, offset_ref, live_ref, reach_ref, near_ref):
    upper = me * 2 >= n
    inner, end = jnp.where(upper, 1, n - 2), jnp.where(upper, 0, n - 1)
    frames = (me, me ^ 1, inner, end)
    audio_rows = offset_ref.shape[1] // n
    video_rows = live_ref.shape[1] // n
    pieces = [offset_ref[:, i * audio_rows : (i + 1) * audio_rows] for i in range(n)]
    offsets = jnp.concatenate([pick(pieces, frame) for frame in frames], axis=1)
    near_ref[...] = jnp.where(jnp.abs(offsets - me) <= SPAN, 0.0, MASKED)
    size = 2 * audio_rows
    corner = lax.broadcasted_iota(jnp.int32, (size, size), 0) == lax.broadcasted_iota(
        jnp.int32, (size, size), 1
    )
    asking = jnp.sum(jnp.where(corner, offsets[:, :size], 0), axis=1, keepdims=True)
    within = lax.broadcasted_iota(jnp.int32, (1, video_rows), 1)
    for i, frame in enumerate(frames):
        cols = slice(i * video_rows, (i + 1) * video_rows)
        live = jnp.where(within < count_ref[frame], 0.0, MASKED)
        live_ref[:, cols] = live
        reach_ref[:, cols] = jnp.where(jnp.abs(asking - frame) <= SPAN, live, MASKED)


def sound_blocks(blocks, audio_rows, half, cols):
    key_rows = slice(half * audio_rows, (half + 1) * audio_rows)
    value_rows = slice((2 + half) * audio_rows, (3 + half) * audio_rows)
    keys = jnp.concatenate([b[key_rows, cols] for b in blocks], axis=0)
    values = jnp.concatenate([b[value_rows, cols] for b in blocks], axis=0)
    return keys, values


def audio_mate_kernel(n, me_ref, asks0, asks1, out, second, across, far, mate_ref):
    audio_rows, width = mate_ref.shape[0], out.shape[1]
    video_rows = asks0.shape[0] - audio_rows
    me = me_ref[0]

    @pl.when((me > 0) & (me < n - 1))
    def _():
        for half, asks in enumerate((asks0, asks1)):
            for at in range(0, width, HEAD_DIM):
                cols = slice(at, at + HEAD_DIM)
                to = slice(half * width + at, half * width + at + HEAD_DIM)
                keys, values = sound_blocks((out, second, across, far), audio_rows, half, cols)
                mate_ref[:, to] = blend(asks[video_rows:, cols], keys, values, None)


def audio_own_kernel(n, me_ref, near_ref, asks0, asks1, out, over, first, second, across, far, *outs):
    cross_ref, own_ref = outs
    audio_rows, width = own_ref.shape[0], out.shape[1]
    video_rows = cross_ref.shape[0]
    me = me_ref[0]
    at_end = (me == 0) | (me == n - 1)

    def run(blocks, alone):
        near = near_ref[:, : audio_rows * len(blocks)]
        for half, asks in enumerate((asks0, asks1)):
            for at in range(0, width, HEAD_DIM):
                cols = slice(at, at + HEAD_DIM)
                to = slice(half * width + at, half * width + at + HEAD_DIM)
                keys, values = sound_blocks(blocks, audio_rows, half, cols)
                cross_ref[:, to] = blend(asks[:video_rows, cols], keys, values, near)
                if not alone:
                    own_ref[:, to] = blend(asks[video_rows:, cols], keys, values, None)

    @pl.when(jnp.logical_not(at_end))
    def _():
        run((out, second, across, far), False)

    @pl.when(at_end)
    def _():
        run((over, first, second), True)


def video_kernel(n, who, at, shift, me_ref, live_ref, reach_ref, asks, own, mate, keys2, values2, far, out_ref):
    video_rows = own.shape[0] // 2
    audio_rows = asks.shape[0] - video_rows
    me = me_ref[0]

    @pl.when((me > 0) & (me < n - 1))
    def _():
        for head in range(own.shape[1] // HEAD_DIM):
            cols = slice(head * HEAD_DIM, (head + 1) * HEAD_DIM)
            all_cols = slice((at + head) * HEAD_DIM, (at + head + 1) * HEAD_DIM)
            q_cols = slice((at - shift + head) * HEAD_DIM, (at - shift + head + 1) * HEAD_DIM)
            top, low = slice(0, video_rows), slice(video_rows, 2 * video_rows)
            keys = jnp.concatenate(
                [own[top, cols], mate[top, cols], keys2[:, all_cols], far[top, cols]], axis=0
            )
            values = jnp.concatenate(
                [own[low, cols], mate[low, cols], values2[:, all_cols], far[low, cols]], axis=0
            )
            reach = reach_ref[who * audio_rows : (who + 1) * audio_rows, :]
            out_ref[:video_rows, cols] = blend(asks[:video_rows, q_cols], keys, values, live_ref[...])
            out_ref[video_rows:, cols] = blend(asks[video_rows:, q_cols], keys, values, reach)


def place_kernel(n_frames, video_rows, me_ref, cross, *refs):
    n = (len(refs) - 5) // 2
    own, back = refs[:n], refs[n : 2 * n]
    video_self, video_cross, audio_self, audio_cross = refs[2 * n : 2 * n + 4]
    sem = refs[-1]

    def copies(parts):
        yield cross, video_cross
        yield parts[0], audio_self
        at = 0
        for part in parts[1:]:
            cols = pl.ds(at, part.shape[1])
            yield part.at[:video_rows], video_self.at[:, cols]
            yield part.at[video_rows:], audio_cross.at[:, cols]
            at += part.shape[1]

    at_end = (me_ref[0] == 0) | (me_ref[0] == n_frames - 1)
    for role, parts in ((jnp.logical_not(at_end), own), (at_end, back)):

        @pl.when(role)
        def _(parts=parts):
            moves = [
                pltpu.make_async_copy(src, dst, sem.at[i])
                for i, (src, dst) in enumerate(copies(parts))
            ]
            for move in moves:
                move.start()
            for move in moves:
                move.wait()


def cost(rows, keys, heads):
    scores = rows * keys * heads
    return pl.CostEstimate(flops=4 * scores * HEAD_DIM, bytes_accessed=rows * heads * 512, transcendentals=scores)


def chunks_of(heads):
    head = heads // 2
    return head, (head + 1) // 2, head // 2


def lined(video_q, video_k, video_v, audio_q, audio_k, audio_v, offsets, counts):
    n, cores = lax.axis_size("seq"), lax.axis_size("mp")
    me = lax.axis_index("seq")
    video_rows, audio_rows = video_q.shape[0], audio_q.shape[0]
    rows = video_rows + audio_rows
    width = video_q.shape[1]
    heads = width // HEAD_DIM
    chunks = chunks_of(heads)
    mate_pairs = [(i, i ^ 1) for i in range(n)]
    cross_pairs = []
    for i in range(n):
        for core in range(cores):
            inner = 0 < i < n - 1
            to = (n - 1 - i) * cores + core if inner else i * cores + cores - 1 - core
            cross_pairs.append((i * cores + core, to))

    def mate(block):
        return lax.ppermute(block, "seq", mate_pairs)

    def cross(block):
        return lax.ppermute(block, ("seq", "mp"), cross_pairs)

    def call(kernel, outs, spaces, *args, **more):
        return pl.pallas_call(
            kernel,
            out_shape=tuple(jax.ShapeDtypeStruct(shape, dtype) for shape, dtype in outs),
            in_specs=spaces,
            compiler_params=PARAMS,
            **more,
        )(*args)

    place = me.astype(jnp.int32).reshape(1)
    raw_keys, raw_values = video_k, video_v
    video_q, video_k, video_v, audio_q, audio_k, audio_v = (
        pltpu.with_memory_space_constraint(block, pltpu.HBM)
        for block in (video_q, video_k, video_v, audio_q, audio_k, audio_v)
    )
    at_end = (me == 0) | (me == n - 1)
    lengths = [size * HEAD_DIM for size in chunks]
    half = lengths[0]
    first_out, first_over = call(
        functools.partial(first_pack, n),
        (((2 * video_rows, half), jnp.bfloat16),) * 2,
        [SMEM] + [HBM] * 4,
        place,
        video_k,
        video_v,
        audio_k,
        audio_v,
        out_specs=(VMEM,) * 2,
        scratch_shapes=[pltpu.SemaphoreType.DMA((6,))],
    )
    outs = tuple(((2 * video_rows, length), jnp.bfloat16) for length in lengths[1:])
    outs += (((rows, half), jnp.bfloat16),) * 2
    outs += (
        ((1, n * video_rows), jnp.float32),
        ((2 * audio_rows, n * video_rows), jnp.float32),
        ((1, n * audio_rows), jnp.float32),
    )
    *sights, asks0, asks1, live, reach, near = call(
        functools.partial(second_pack, n),
        outs,
        [SMEM, SMEM, VMEM] + [HBM] * 4,
        place,
        counts,
        offsets.reshape(1, -1),
        video_k,
        video_v,
        video_q,
        audio_q,
        out_specs=(VMEM,) * len(outs),
        scratch_shapes=[pltpu.SemaphoreType.DMA((8,))],
    )
    asks = [asks0, asks1]
    sights = [first_over] + sights

    keys_across = cross(raw_keys)
    values_across = cross(raw_values)
    sight_mate = [mate(first_out)]
    sound_across = cross(first_out)
    second_mate = mate(jnp.where(at_end, first_over, sound_across))
    sound_far = cross(second_mate)
    sight_mate += [mate(sights[i]) for i in (1, 2)]
    sight_far = [cross(sight_mate[i]) for i in range(3)]
    asks_mate = [mate(asks[i]) for i in range(2)]

    def look(who, i, queries):
        at, size = sum(chunks[:i]), chunks[i]
        half = min(i, 1)
        return call(
            functools.partial(video_kernel, n, who, at, half * chunks[0]),
            (((rows, size * HEAD_DIM), jnp.bfloat16),),
            [SMEM] + [VMEM] * 8,
            place,
            live,
            reach,
            queries[half],
            sights[i],
            sight_mate[i],
            keys_across,
            values_across,
            sight_far[i],
            out_specs=(VMEM,),
            cost_estimate=cost(rows, n * video_rows, size),
        )[0]

    back = [mate(look(1, i, asks_mate)) for i in range(3)]
    mine = [look(0, i, asks) for i in range(3)]
    theirs = call(
        functools.partial(audio_mate_kernel, n),
        (((audio_rows, width), jnp.bfloat16),),
        [SMEM] + [VMEM] * 6,
        place,
        *asks_mate,
        first_out,
        second_mate,
        sound_across,
        sound_far,
        out_specs=(VMEM,),
        cost_estimate=cost(audio_rows, n * audio_rows, heads),
    )[0]
    video_cross, own = call(
        functools.partial(audio_own_kernel, n),
        (((video_rows, width), jnp.bfloat16), ((audio_rows, width), jnp.bfloat16)),
        [SMEM] + [VMEM] * 9,
        place,
        near,
        *asks,
        first_out,
        first_over,
        sight_mate[0],
        second_mate,
        sound_across,
        sound_far,
        out_specs=(VMEM,) * 2,
        cost_estimate=cost(rows, n * audio_rows, heads),
    )
    mine = [own] + mine
    back = [mate(theirs)] + back
    return call(
        functools.partial(place_kernel, n, video_rows),
        (((video_rows, width), jnp.bfloat16),) * 2 + (((audio_rows, width), jnp.bfloat16),) * 2,
        [SMEM] + [VMEM] * (1 + 2 * len(mine)),
        place,
        video_cross,
        *mine,
        *back,
        out_specs=(HBM,) * 4,
        scratch_shapes=[pltpu.SemaphoreType.DMA((2 * len(mine),))],
    )


def solution(mesh):
    split = P(("groups", "seq"), ("tower", "mp"))
    placed = (split,) * 6 + (P("groups"), P("groups"))
    sizes = mesh.shape
    line = sizes["seq"] == 4 and sizes["mp"] == 2

    def whole(*arrays):
        heads = arrays[0].shape[1] // HEAD_DIM // (sizes["tower"] * sizes["mp"])
        paired = heads % 2 == 0 and heads > 3 and arrays[0].shape[0] == 2 * arrays[3].shape[0]
        body = lined if line and paired else gathered
        return jax.shard_map(
            body, mesh=mesh, in_specs=placed, out_specs=(split,) * 4, check_vma=False
        )(*arrays)

    return whole
```

```python
import functools

import jax
import jax.numpy as jnp
from jax import lax
from jax.experimental import pallas as pl
from jax.experimental.pallas import tpu as pltpu
from jax.sharding import PartitionSpec as P


HEAD_DIM = 128
SPAN = 1
STEP = 128
MASKED = -1e30
LOG2E = 1.4426950408889634
VMEM = pl.BlockSpec(memory_space=pltpu.VMEM)
SMEM = pl.BlockSpec(memory_space=pltpu.SMEM)
HBM = pl.BlockSpec(memory_space=pltpu.HBM)
PARAMS = pltpu.CompilerParams(vmem_limit_bytes=16 << 20)


def attend(queries, key_rows, value_rows, allowed):
    scores = jnp.einsum(
        "qhe,khe->hqk", queries, key_rows, preferred_element_type=jnp.float32
    ) * HEAD_DIM ** (-0.5)
    scores = jnp.where(allowed[None], scores, MASKED)
    peak = jnp.max(scores, axis=2)
    weights = jnp.where(allowed[None], jnp.exp(scores - peak[:, :, None]), 0.0)
    total = jnp.sum(weights, axis=2)
    blended = jnp.einsum(
        "hqk,khe->hqe", weights.astype(jnp.bfloat16), value_rows, preferred_element_type=jnp.float32
    )
    blended = blended / total[:, :, None]
    return jnp.transpose(blended, (1, 0, 2)).reshape(blended.shape[1], -1).astype(jnp.bfloat16)


def gathered(video_q, video_k, video_v, audio_q, audio_k, audio_v, offsets, counts):
    my_frame = lax.axis_index("seq")
    video_rows, audio_rows = video_q.shape[0], audio_q.shape[0]

    def heads(rows):
        return rows.reshape(rows.shape[0], -1, HEAD_DIM)

    def everywhere(rows):
        return heads(lax.all_gather(rows, "seq", axis=0, tiled=True))

    my_offsets = lax.dynamic_slice_in_dim(offsets, my_frame * audio_rows, audio_rows)
    keys, values = everywhere(video_k), everywhere(video_v)
    audio_keys, audio_values = everywhere(audio_k), everywhere(audio_v)
    positions = jnp.arange(keys.shape[0], dtype=jnp.int32)
    source = positions // video_rows
    is_live = positions % video_rows < jnp.repeat(counts, video_rows)
    video_self = attend(heads(video_q), keys, values, is_live[None, :])
    in_reach = (jnp.abs(my_offsets[:, None] - source[None, :]) <= SPAN) & is_live[None, :]
    audio_cross = attend(heads(audio_q), keys, values, in_reach)
    every = jnp.ones((1, audio_keys.shape[0]), jnp.bool_)
    audio_self = attend(heads(audio_q), audio_keys, audio_values, every)
    in_reach = jnp.abs(offsets - my_frame) <= SPAN
    video_cross = attend(heads(video_q), audio_keys, audio_values, in_reach[None, :])
    return (video_self, video_cross, audio_self, audio_cross)


def blend(queries, keys, values, bias):
    scores = lax.dot_general(
        queries, keys, (((1,), (1,)), ((), ())), preferred_element_type=jnp.float32
    )
    if bias is not None:
        scores = scores + bias
    peak = jnp.max(scores, axis=1, keepdims=True)
    weights = jnp.exp2((scores - peak) * (HEAD_DIM ** (-0.5) * LOG2E))
    total = jnp.sum(weights, axis=1, keepdims=True)
    weights = weights.astype(jnp.bfloat16)
    mixed = 0.0
    for at in range(0, keys.shape[0], STEP):
        mixed += jnp.dot(
            weights[:, at : at + STEP], values[at : at + STEP], preferred_element_type=jnp.float32
        )
    return (mixed * (1.0 / total)).astype(jnp.bfloat16)


def pick(pieces, at):
    chosen = pieces[0]
    for i in range(1, len(pieces)):
        chosen = jnp.where(at == i, pieces[i], chosen)
    return chosen


def move_all(moves, sem):
    copies = [pltpu.make_async_copy(src, dst, sem.at[i]) for i, (src, dst) in enumerate(moves)]
    for copy in copies:
        copy.start()
    return copies


def sight_moves(video_k, video_v, first, out):
    rows, cols = video_k.shape[0], pl.ds(first, out.shape[1])
    return [(video_k.at[:, cols], out.at[:rows]), (video_v.at[:, cols], out.at[rows:])]


def sound_moves(audio_k, audio_v, out):
    rows, width = audio_k.shape[0], out.shape[1]
    moves = []
    for src in (audio_k, audio_v):
        for half in range(2):
            at = len(moves) * rows
            moves.append((src.at[:, pl.ds(half * width, width)], out.at[at : at + rows]))
    return moves


def first_pack(n, me_ref, video_k, video_v, audio_k, audio_v, out_ref, over_ref, values_ref, sem):
    me = me_ref[0]
    half = values_ref.shape[1]
    at_end = (me == 0) | (me == n - 1)
    for role, sight, sound in ((at_end, out_ref, over_ref), (jnp.logical_not(at_end), over_ref, out_ref)):

        @pl.when(role)
        def _(sight=sight, sound=sound):
            moves = sight_moves(video_k, video_v, 0, sight) + sound_moves(audio_k, audio_v, sound)
            moves.append((video_v.at[:, pl.ds(0, half)], values_ref))
            for copy in move_all(moves, sem):
                copy.wait()


def second_pack(n, me_ref, count_ref, offset_ref, video_k, video_v, video_q, audio_q, *outs):
    sight1, sight2, asks0, asks1, values_ref, mask0_ref, mask1_ref, near_ref, sem = outs
    rows = video_q.shape[0]
    at = asks0.shape[1]
    moves = [(video_v.at[:, pl.ds(at, at)], values_ref)]
    for half, out in enumerate((asks0, asks1)):
        cols = pl.ds(half * at, at)
        moves += [(video_q.at[:, cols], out.at[:rows]), (audio_q.at[:, cols], out.at[rows:])]
    for out in (sight1, sight2):
        moves += sight_moves(video_k, video_v, at, out)
        at += out.shape[1]
    copies = move_all(moves, sem)
    tables(n, me_ref[0], count_ref, offset_ref, (mask0_ref, mask1_ref), near_ref)
    for copy in copies:
        copy.wait()


def tables(n, me, count_ref, offset_ref, mask_refs, near_ref):
    upper = me * 2 >= n
    inner, end = jnp.where(upper, 1, n - 2), jnp.where(upper, 0, n - 1)
    frames = (me, me ^ 1, inner, end)
    audio_rows = offset_ref.shape[1] // n
    video_rows = mask_refs[0].shape[1] // n
    pieces = [offset_ref[:, i * audio_rows : (i + 1) * audio_rows] for i in range(n)]
    offsets = jnp.concatenate([pick(pieces, frame) for frame in frames], axis=1)
    near = jnp.where(jnp.abs(offsets - me) <= SPAN, 0.0, MASKED)
    near_ref[:video_rows, :] = jnp.broadcast_to(near, (video_rows, n * audio_rows))
    near_ref[video_rows:, :] = jnp.zeros((audio_rows, n * audio_rows), jnp.float32)
    size = 2 * audio_rows
    corner = lax.broadcasted_iota(jnp.int32, (size, size), 0) == lax.broadcasted_iota(
        jnp.int32, (size, size), 1
    )
    asking = jnp.sum(jnp.where(corner, offsets[:, :size], 0), axis=1, keepdims=True)
    within = lax.broadcasted_iota(jnp.int32, (1, video_rows), 1)
    for i, frame in enumerate(frames):
        cols = slice(i * video_rows, (i + 1) * video_rows)
        live = jnp.where(within < count_ref[frame], 0.0, MASKED)
        reach = jnp.where(jnp.abs(asking - frame) <= SPAN, live, MASKED)
        for who, mask_ref in enumerate(mask_refs):
            mask_ref[:video_rows, cols] = jnp.broadcast_to(live, (video_rows, video_rows))
            mask_ref[video_rows:, cols] = reach[who * audio_rows : (who + 1) * audio_rows]


def sound_blocks(blocks, audio_rows, half, cols):
    key_rows = slice(half * audio_rows, (half + 1) * audio_rows)
    value_rows = slice((2 + half) * audio_rows, (3 + half) * audio_rows)
    keys = jnp.concatenate([b[key_rows, cols] for b in blocks], axis=0)
    values = jnp.concatenate([b[value_rows, cols] for b in blocks], axis=0)
    return keys, values


def audio_mate_kernel(n, me_ref, asks0, asks1, out, second, across, far, mate_ref):
    audio_rows, width = mate_ref.shape[0], out.shape[1]
    video_rows = asks0.shape[0] - audio_rows
    me = me_ref[0]

    @pl.when((me > 0) & (me < n - 1))
    def _():
        for half, asks in enumerate((asks0, asks1)):
            for at in range(0, width, HEAD_DIM):
                cols = slice(at, at + HEAD_DIM)
                to = slice(half * width + at, half * width + at + HEAD_DIM)
                keys, values = sound_blocks((out, second, across, far), audio_rows, half, cols)
                mate_ref[:, to] = blend(asks[video_rows:, cols], keys, values, None)


def audio_own_kernel(n, me_ref, near_ref, asks0, asks1, out, over, first, second, across, far, *outs):
    cross_ref, own_ref = outs
    audio_rows, width = own_ref.shape[0], out.shape[1]
    video_rows = cross_ref.shape[0]
    me = me_ref[0]
    at_end = (me == 0) | (me == n - 1)

    def run(blocks):
        for half, asks in enumerate((asks0, asks1)):
            for at in range(0, width, HEAD_DIM):
                cols = slice(at, at + HEAD_DIM)
                to = slice(half * width + at, half * width + at + HEAD_DIM)
                keys, values = sound_blocks(blocks, audio_rows, half, cols)
                mixed = blend(asks[:, cols], keys, values, near_ref[...])
                cross_ref[:, to] = mixed[:video_rows]
                own_ref[:, to] = mixed[video_rows:]

    @pl.when(jnp.logical_not(at_end))
    def _():
        run((out, second, across, far))

    @pl.when(at_end)
    def _():
        run((over, first, second, far))


def video_kernel(n, at, half, me_ref, mask_ref, asks, own, mate, keys2, values2, far, out_ref):
    video_rows = own.shape[0] // 2
    me = me_ref[0]

    @pl.when((me > 0) & (me < n - 1))
    def _():
        for head in range(own.shape[1] // HEAD_DIM):
            cols = slice(head * HEAD_DIM, (head + 1) * HEAD_DIM)
            all_cols = slice((at + head) * HEAD_DIM, (at + head + 1) * HEAD_DIM)
            half_cols = slice((at - half + head) * HEAD_DIM, (at - half + head + 1) * HEAD_DIM)
            top, low = slice(0, video_rows), slice(video_rows, 2 * video_rows)
            keys = jnp.concatenate(
                [own[top, cols], mate[top, cols], keys2[:, all_cols], far[top, cols]], axis=0
            )
            values = jnp.concatenate(
                [own[low, cols], mate[low, cols], values2[:, half_cols], far[low, cols]], axis=0
            )
            out_ref[:, cols] = blend(asks[:, half_cols], keys, values, mask_ref[...])


def place_pieces(parts, first, video_rows, video_self, audio_cross):
    moves, at = [], first
    for part in parts:
        cols = pl.ds(at, part.shape[1])
        moves.append((part.at[:video_rows], video_self.at[:, cols]))
        moves.append((part.at[video_rows:], audio_cross.at[:, cols]))
        at += part.shape[1]
    return moves


def place_kernel(n, me_ref, cross, own0, own1, own2, back0, back1, back2, *outs):
    video_self, video_cross, audio_self, audio_cross, sem = outs
    at_end = (me_ref[0] == 0) | (me_ref[0] == n - 1)
    for role, sound, parts in (
        (jnp.logical_not(at_end), own0, (own1, own2)),
        (at_end, back0, (back1, back2)),
    ):

        @pl.when(role)
        def _(sound=sound, parts=parts):
            moves = [(cross, video_cross), (sound, audio_self)]
            moves += place_pieces(parts, 0, cross.shape[0], video_self, audio_cross)
            for copy in move_all(moves, sem):
                copy.wait()


def place_last_kernel(n, first, me_ref, own, back, old_self, old_cross, video_self, audio_cross, sem):
    at_end = (me_ref[0] == 0) | (me_ref[0] == n - 1)
    for role, part in ((jnp.logical_not(at_end), own), (at_end, back)):

        @pl.when(role)
        def _(part=part):
            moves = place_pieces((part,), first, video_self.shape[0], video_self, audio_cross)
            for copy in move_all(moves, sem):
                copy.wait()


def cost(rows, keys, heads):
    scores = rows * keys * heads
    return pl.CostEstimate(flops=4 * scores * HEAD_DIM, bytes_accessed=rows * heads * 512, transcendentals=scores)


def chunks_of(heads):
    head = heads // 2
    return head, (head + 1) // 2, head // 2


def lined(video_q, video_k, video_v, audio_q, audio_k, audio_v, offsets, counts):
    n, cores = lax.axis_size("seq"), lax.axis_size("mp")
    me = lax.axis_index("seq")
    video_rows, audio_rows = video_q.shape[0], audio_q.shape[0]
    rows = video_rows + audio_rows
    width = video_q.shape[1]
    heads = width // HEAD_DIM
    chunks = chunks_of(heads)
    mate_pairs = [(i, i ^ 1) for i in range(n)]
    cross_pairs = []
    for i in range(n):
        for core in range(cores):
            inner = 0 < i < n - 1
            to = (n - 1 - i) * cores + core if inner else i * cores + cores - 1 - core
            cross_pairs.append((i * cores + core, to))

    def mate(block):
        return lax.ppermute(block, "seq", mate_pairs)

    def cross(block):
        return lax.ppermute(block, ("seq", "mp"), cross_pairs)

    def call(kernel, outs, spaces, *args, **more):
        return pl.pallas_call(
            kernel,
            out_shape=tuple(jax.ShapeDtypeStruct(shape, dtype) for shape, dtype in outs),
            in_specs=spaces,
            compiler_params=PARAMS,
            **more,
        )(*args)

    place = me.astype(jnp.int32).reshape(1)
    raw_keys = video_k
    video_q, video_k, video_v, audio_q, audio_k, audio_v = (
        pltpu.with_memory_space_constraint(block, pltpu.HBM)
        for block in (video_q, video_k, video_v, audio_q, audio_k, audio_v)
    )
    at_end = (me == 0) | (me == n - 1)
    lengths = [size * HEAD_DIM for size in chunks]
    half = lengths[0]
    first_out, first_over, values0 = call(
        functools.partial(first_pack, n),
        (((2 * video_rows, half), jnp.bfloat16),) * 2 + (((video_rows, half), jnp.bfloat16),),
        [SMEM] + [HBM] * 4,
        place,
        video_k,
        video_v,
        audio_k,
        audio_v,
        out_specs=(VMEM,) * 3,
        scratch_shapes=[pltpu.SemaphoreType.DMA((7,))],
    )
    outs = tuple(((2 * video_rows, length), jnp.bfloat16) for length in lengths[1:])
    outs += (((rows, half), jnp.bfloat16),) * 2
    outs += (((video_rows, half), jnp.bfloat16),)
    outs += (((rows, n * video_rows), jnp.float32),) * 2 + (((rows, n * audio_rows), jnp.float32),)
    *sights, asks0, asks1, values1, mask0, mask1, near = call(
        functools.partial(second_pack, n),
        outs,
        [SMEM, SMEM, VMEM] + [HBM] * 4,
        place,
        counts,
        offsets.reshape(1, -1),
        video_k,
        video_v,
        video_q,
        audio_q,
        out_specs=(VMEM,) * len(outs),
        scratch_shapes=[pltpu.SemaphoreType.DMA((9,))],
    )
    asks = [asks0, asks1]
    sights = [first_over] + sights

    keys_across = cross(raw_keys)
    values_across = [cross(values0), cross(values1)]
    sight_mate = [mate(first_out)]
    sound_across = cross(first_out)
    second_mate = mate(jnp.where(at_end, first_over, sound_across))
    sound_far = cross(second_mate)
    sight_mate += [mate(sights[i]) for i in (1, 2)]
    sight_far = [cross(sight_mate[i]) for i in range(3)]
    asks_mate = [mate(asks[i]) for i in range(2)]

    def look(i, queries, mask):
        at, size = sum(chunks[:i]), chunks[i]
        half = min(i, 1)
        return call(
            functools.partial(video_kernel, n, at, half * chunks[0]),
            (((rows, size * HEAD_DIM), jnp.bfloat16),),
            [SMEM] + [VMEM] * 7,
            place,
            mask,
            queries[half],
            sights[i],
            sight_mate[i],
            keys_across,
            values_across[half],
            sight_far[i],
            out_specs=(VMEM,),
            cost_estimate=cost(rows, n * video_rows, size),
        )[0]

    back = [mate(look(i, asks_mate, mask1)) for i in range(3)]
    mine = [look(i, asks, mask0) for i in range(3)]
    theirs = call(
        functools.partial(audio_mate_kernel, n),
        (((audio_rows, width), jnp.bfloat16),),
        [SMEM] + [VMEM] * 6,
        place,
        *asks_mate,
        first_out,
        second_mate,
        sound_across,
        sound_far,
        out_specs=(VMEM,),
        cost_estimate=cost(audio_rows, n * audio_rows, heads),
    )[0]
    video_cross, own = call(
        functools.partial(audio_own_kernel, n),
        (((video_rows, width), jnp.bfloat16), ((audio_rows, width), jnp.bfloat16)),
        [SMEM] + [VMEM] * 9,
        place,
        near,
        *asks,
        first_out,
        first_over,
        sight_mate[0],
        second_mate,
        sound_across,
        sound_far,
        out_specs=(VMEM,) * 2,
        cost_estimate=cost(rows, n * audio_rows, heads),
    )
    back_sound = mate(theirs)
    video_shape = ((video_rows, width), jnp.bfloat16)
    audio_shape = ((audio_rows, width), jnp.bfloat16)
    video_self, video_cross, audio_self, audio_cross = call(
        functools.partial(place_kernel, n),
        (video_shape, video_shape, audio_shape, audio_shape),
        [SMEM] + [VMEM] * 7,
        place,
        video_cross,
        own,
        *mine[:2],
        back_sound,
        *back[:2],
        out_specs=(HBM,) * 4,
        scratch_shapes=[pltpu.SemaphoreType.DMA((6,))],
    )
    video_self, audio_cross = call(
        functools.partial(place_last_kernel, n, width - lengths[2]),
        (video_shape, audio_shape),
        [SMEM] + [VMEM] * 2 + [HBM] * 2,
        place,
        mine[2],
        back[2],
        video_self,
        audio_cross,
        out_specs=(HBM,) * 2,
        scratch_shapes=[pltpu.SemaphoreType.DMA((2,))],
        input_output_aliases={3: 0, 4: 1},
    )
    return video_self, video_cross, audio_self, audio_cross


def solution(mesh):
    split = P(("groups", "seq"), ("tower", "mp"))
    placed = (split,) * 6 + (P("groups"), P("groups"))
    sizes = mesh.shape
    line = sizes["seq"] == 4 and sizes["mp"] == 2

    def whole(*arrays):
        heads = arrays[0].shape[1] // HEAD_DIM // (sizes["tower"] * sizes["mp"])
        paired = heads % 2 == 0 and heads > 3 and arrays[0].shape[0] == 2 * arrays[3].shape[0]
        body = lined if line and paired else gathered
        return jax.shard_map(
            body, mesh=mesh, in_specs=placed, out_specs=(split,) * 4, check_vma=False
        )(*arrays)

    return whole
```

```python
import functools

import jax
import jax.numpy as jnp
from jax import lax
from jax.experimental import pallas as pl
from jax.experimental.pallas import tpu as pltpu
from jax.sharding import PartitionSpec as P


HEAD_DIM = 128
SPAN = 1
STEP = 128
MASKED = -1e30
LOG2E = 1.4426950408889634
VMEM = pl.BlockSpec(memory_space=pltpu.VMEM)
SMEM = pl.BlockSpec(memory_space=pltpu.SMEM)
HBM = pl.BlockSpec(memory_space=pltpu.HBM)
PARAMS = pltpu.CompilerParams(vmem_limit_bytes=16 << 20)


def attend(queries, key_rows, value_rows, allowed):
    scores = jnp.einsum(
        "qhe,khe->hqk", queries, key_rows, preferred_element_type=jnp.float32
    ) * HEAD_DIM ** (-0.5)
    scores = jnp.where(allowed[None], scores, MASKED)
    peak = jnp.max(scores, axis=2)
    weights = jnp.where(allowed[None], jnp.exp(scores - peak[:, :, None]), 0.0)
    total = jnp.sum(weights, axis=2)
    blended = jnp.einsum(
        "hqk,khe->hqe", weights.astype(jnp.bfloat16), value_rows, preferred_element_type=jnp.float32
    )
    blended = blended / total[:, :, None]
    return jnp.transpose(blended, (1, 0, 2)).reshape(blended.shape[1], -1).astype(jnp.bfloat16)


def gathered(video_q, video_k, video_v, audio_q, audio_k, audio_v, offsets, counts):
    my_frame = lax.axis_index("seq")
    video_rows, audio_rows = video_q.shape[0], audio_q.shape[0]

    def heads(rows):
        return rows.reshape(rows.shape[0], -1, HEAD_DIM)

    def everywhere(rows):
        return heads(lax.all_gather(rows, "seq", axis=0, tiled=True))

    my_offsets = lax.dynamic_slice_in_dim(offsets, my_frame * audio_rows, audio_rows)
    keys, values = everywhere(video_k), everywhere(video_v)
    audio_keys, audio_values = everywhere(audio_k), everywhere(audio_v)
    positions = jnp.arange(keys.shape[0], dtype=jnp.int32)
    source = positions // video_rows
    is_live = positions % video_rows < jnp.repeat(counts, video_rows)
    video_self = attend(heads(video_q), keys, values, is_live[None, :])
    in_reach = (jnp.abs(my_offsets[:, None] - source[None, :]) <= SPAN) & is_live[None, :]
    audio_cross = attend(heads(audio_q), keys, values, in_reach)
    every = jnp.ones((1, audio_keys.shape[0]), jnp.bool_)
    audio_self = attend(heads(audio_q), audio_keys, audio_values, every)
    in_reach = jnp.abs(offsets - my_frame) <= SPAN
    video_cross = attend(heads(video_q), audio_keys, audio_values, in_reach[None, :])
    return (video_self, video_cross, audio_self, audio_cross)


def blend(queries, keys, values, bias):
    scores = lax.dot_general(
        queries, keys, (((1,), (1,)), ((), ())), preferred_element_type=jnp.float32
    )
    if bias is not None:
        scores = scores + bias
    peak = jnp.max(scores, axis=1, keepdims=True)
    weights = jnp.exp2((scores - peak) * (HEAD_DIM ** (-0.5) * LOG2E))
    total = jnp.sum(weights, axis=1, keepdims=True)
    weights = weights.astype(jnp.bfloat16)
    mixed = 0.0
    for at in range(0, keys.shape[0], STEP):
        mixed += jnp.dot(
            weights[:, at : at + STEP], values[at : at + STEP], preferred_element_type=jnp.float32
        )
    return (mixed * (1.0 / total)).astype(jnp.bfloat16)


def pick(pieces, at):
    chosen = pieces[0]
    for i in range(1, len(pieces)):
        chosen = jnp.where(at == i, pieces[i], chosen)
    return chosen


def move_all(moves, sem):
    copies = [pltpu.make_async_copy(src, dst, sem.at[i]) for i, (src, dst) in enumerate(moves)]
    for copy in copies:
        copy.start()
    return copies


def sight_moves(video_k, video_v, first, out):
    rows, cols = video_k.shape[0], pl.ds(first, out.shape[1])
    return [(video_k.at[:, cols], out.at[:rows]), (video_v.at[:, cols], out.at[rows:])]


def sound_moves(audio_k, audio_v, out):
    rows, width = audio_k.shape[0], out.shape[1]
    moves = []
    for src in (audio_k, audio_v):
        for half in range(2):
            at = len(moves) * rows
            moves.append((src.at[:, pl.ds(half * width, width)], out.at[at : at + rows]))
    return moves


def first_pack(n, me_ref, video_k, video_v, audio_k, audio_v, out_ref, over_ref, values_ref, sem):
    me = me_ref[0]
    half = values_ref.shape[1]
    at_end = (me == 0) | (me == n - 1)
    for role, sight, sound in ((at_end, out_ref, over_ref), (jnp.logical_not(at_end), over_ref, out_ref)):

        @pl.when(role)
        def _(sight=sight, sound=sound):
            moves = sight_moves(video_k, video_v, 0, sight) + sound_moves(audio_k, audio_v, sound)
            moves.append((video_v.at[:, pl.ds(0, half)], values_ref))
            for copy in move_all(moves, sem):
                copy.wait()


def second_pack(n, me_ref, count_ref, offset_ref, video_k, video_v, video_q, audio_q, *outs):
    sight, asks0, asks1, values_ref, mask0_ref, mask1_ref, near_ref, sem = outs
    rows, half = video_q.shape[0], sight.shape[1]
    moves = sight_moves(video_k, video_v, half, sight)
    moves.append((video_v.at[:, pl.ds(half, half)], values_ref))
    for side, out in enumerate((asks0, asks1)):
        cols = pl.ds(side * half, half)
        moves += [(video_q.at[:, cols], out.at[:rows]), (audio_q.at[:, cols], out.at[rows:])]
    copies = move_all(moves, sem)
    tables(n, me_ref[0], count_ref, offset_ref, (mask0_ref, mask1_ref), near_ref)
    for copy in copies:
        copy.wait()


def tables(n, me, count_ref, offset_ref, mask_refs, near_ref):
    upper = me * 2 >= n
    inner, end = jnp.where(upper, 1, n - 2), jnp.where(upper, 0, n - 1)
    frames = (me, me ^ 1, inner, end)
    audio_rows = offset_ref.shape[1] // n
    video_rows = mask_refs[0].shape[1] // n
    pieces = [offset_ref[:, i * audio_rows : (i + 1) * audio_rows] for i in range(n)]
    offsets = jnp.concatenate([pick(pieces, frame) for frame in frames], axis=1)
    near = jnp.where(jnp.abs(offsets - me) <= SPAN, 0.0, MASKED)
    near_ref[:video_rows, :] = jnp.broadcast_to(near, (video_rows, n * audio_rows))
    near_ref[video_rows:, :] = jnp.zeros((audio_rows, n * audio_rows), jnp.float32)
    size = 2 * audio_rows
    corner = lax.broadcasted_iota(jnp.int32, (size, size), 0) == lax.broadcasted_iota(
        jnp.int32, (size, size), 1
    )
    asking = jnp.sum(jnp.where(corner, offsets[:, :size], 0), axis=1, keepdims=True)
    within = lax.broadcasted_iota(jnp.int32, (1, video_rows), 1)
    for i, frame in enumerate(frames):
        cols = slice(i * video_rows, (i + 1) * video_rows)
        live = jnp.where(within < count_ref[frame], 0.0, MASKED)
        reach = jnp.where(jnp.abs(asking - frame) <= SPAN, live, MASKED)
        for who, mask_ref in enumerate(mask_refs):
            mask_ref[:video_rows, cols] = jnp.broadcast_to(live, (video_rows, video_rows))
            mask_ref[video_rows:, cols] = reach[who * audio_rows : (who + 1) * audio_rows]


def sound_blocks(blocks, audio_rows, half, cols):
    key_rows = slice(half * audio_rows, (half + 1) * audio_rows)
    value_rows = slice((2 + half) * audio_rows, (3 + half) * audio_rows)
    keys = jnp.concatenate([b[key_rows, cols] for b in blocks], axis=0)
    values = jnp.concatenate([b[value_rows, cols] for b in blocks], axis=0)
    return keys, values


def audio_mate_kernel(n, half, me_ref, asks, out, second, across, far, mate_ref):
    audio_rows, width = mate_ref.shape
    video_rows = asks.shape[0] - audio_rows
    me = me_ref[0]

    @pl.when((me > 0) & (me < n - 1))
    def _():
        for at in range(0, width, HEAD_DIM):
            cols = slice(at, at + HEAD_DIM)
            keys, values = sound_blocks((out, second, across, far), audio_rows, half, cols)
            mate_ref[:, cols] = blend(asks[video_rows:, cols], keys, values, None)


def audio_own_kernel(n, me_ref, near_ref, asks0, asks1, out, over, first, second, third, across, far, *outs):
    cross_ref, own_ref = outs
    audio_rows, width = own_ref.shape[0], out.shape[1]
    video_rows = cross_ref.shape[0]
    me = me_ref[0]
    at_end = (me == 0) | (me == n - 1)

    def run(blocks):
        for half, asks in enumerate((asks0, asks1)):
            for at in range(0, width, HEAD_DIM):
                cols = slice(at, at + HEAD_DIM)
                to = slice(half * width + at, half * width + at + HEAD_DIM)
                keys, values = sound_blocks(blocks, audio_rows, half, cols)
                mixed = blend(asks[:, cols], keys, values, near_ref[...])
                cross_ref[:, to] = mixed[:video_rows]
                own_ref[:, to] = mixed[video_rows:]

    @pl.when(jnp.logical_not(at_end))
    def _():
        run((out, second, across, far))

    @pl.when(at_end)
    def _():
        run((over, first, third, far))


def video_kernel(n, at, half, me_ref, mask_ref, asks, own, mate, keys2, values2, far, out_ref):
    video_rows = own.shape[0] // 2
    me = me_ref[0]

    @pl.when((me > 0) & (me < n - 1))
    def _():
        for head in range(far.shape[1] // HEAD_DIM):
            cols = slice(head * HEAD_DIM, (head + 1) * HEAD_DIM)
            all_cols = slice((at + head) * HEAD_DIM, (at + head + 1) * HEAD_DIM)
            half_cols = slice((at - half + head) * HEAD_DIM, (at - half + head + 1) * HEAD_DIM)
            top, low = slice(0, video_rows), slice(video_rows, 2 * video_rows)
            keys = jnp.concatenate(
                [own[top, half_cols], mate[top, half_cols], keys2[:, all_cols], far[top, cols]], axis=0
            )
            values = jnp.concatenate(
                [own[low, half_cols], mate[low, half_cols], values2[:, half_cols], far[low, cols]],
                axis=0,
            )
            out_ref[:, cols] = blend(asks[:, half_cols], keys, values, mask_ref[...])


def place_pieces(parts, first, video_rows, video_self, audio_cross):
    moves, at = [], first
    for part in parts:
        cols = pl.ds(at, part.shape[1])
        moves.append((part.at[:video_rows], video_self.at[:, cols]))
        moves.append((part.at[video_rows:], audio_cross.at[:, cols]))
        at += part.shape[1]
    return moves


def place_kernel(n, me_ref, cross, own_sound, back_sound0, back_sound1, *refs):
    count = (len(refs) - 5) // 2
    own, back = refs[:count], refs[count : 2 * count]
    video_self, video_cross, audio_self, audio_cross, sem = refs[2 * count :]
    at_end = (me_ref[0] == 0) | (me_ref[0] == n - 1)
    for role, sounds, parts in (
        (jnp.logical_not(at_end), (own_sound,), own),
        (at_end, (back_sound0, back_sound1), back),
    ):

        @pl.when(role)
        def _(sounds=sounds, parts=parts):
            moves = [(cross, video_cross)]
            for i, sound in enumerate(sounds):
                length = sound.shape[1]
                moves.append((sound, audio_self.at[:, pl.ds(i * length, length)]))
            moves += place_pieces(parts, 0, cross.shape[0], video_self, audio_cross)
            for copy in move_all(moves, sem):
                copy.wait()


def place_last_kernel(n, first, me_ref, own, back, old_self, old_cross, video_self, audio_cross, sem):
    at_end = (me_ref[0] == 0) | (me_ref[0] == n - 1)
    for role, part in ((jnp.logical_not(at_end), own), (at_end, back)):

        @pl.when(role)
        def _(part=part):
            moves = place_pieces((part,), first, video_self.shape[0], video_self, audio_cross)
            for copy in move_all(moves, sem):
                copy.wait()


def cost(rows, keys, heads):
    scores = rows * keys * heads
    return pl.CostEstimate(flops=4 * scores * HEAD_DIM, bytes_accessed=rows * heads * 512, transcendentals=scores)


def lined(video_q, video_k, video_v, audio_q, audio_k, audio_v, offsets, counts):
    n, cores = lax.axis_size("seq"), lax.axis_size("mp")
    me = lax.axis_index("seq")
    video_rows, audio_rows = video_q.shape[0], audio_q.shape[0]
    rows = video_rows + audio_rows
    width = video_q.shape[1]
    heads = width // HEAD_DIM
    chunks = (heads // 2,) + (1,) * (heads // 2)
    last = len(chunks) - 1
    mate_pairs = [(i, i ^ 1) for i in range(n)]
    cross_pairs = []
    for i in range(n):
        for core in range(cores):
            inner = 0 < i < n - 1
            to = (n - 1 - i) * cores + core if inner else i * cores + cores - 1 - core
            cross_pairs.append((i * cores + core, to))

    def mate(block):
        return lax.ppermute(block, "seq", mate_pairs)

    def cross(block):
        return lax.ppermute(block, ("seq", "mp"), cross_pairs)

    def call(kernel, outs, spaces, *args, **more):
        return pl.pallas_call(
            kernel,
            out_shape=tuple(jax.ShapeDtypeStruct(shape, dtype) for shape, dtype in outs),
            in_specs=spaces,
            compiler_params=PARAMS,
            **more,
        )(*args)

    place = me.astype(jnp.int32).reshape(1)
    raw_keys = video_k
    video_q, video_k, video_v, audio_q, audio_k, audio_v = (
        pltpu.with_memory_space_constraint(block, pltpu.HBM)
        for block in (video_q, video_k, video_v, audio_q, audio_k, audio_v)
    )
    at_end = (me == 0) | (me == n - 1)
    half = width // 2
    first_out, first_over, values0 = call(
        functools.partial(first_pack, n),
        (((2 * video_rows, half), jnp.bfloat16),) * 2 + (((video_rows, half), jnp.bfloat16),),
        [SMEM] + [HBM] * 4,
        place,
        video_k,
        video_v,
        audio_k,
        audio_v,
        out_specs=(VMEM,) * 3,
        scratch_shapes=[pltpu.SemaphoreType.DMA((7,))],
    )
    outs = (((2 * video_rows, half), jnp.bfloat16),)
    outs += (((rows, half), jnp.bfloat16),) * 2 + (((video_rows, half), jnp.bfloat16),)
    outs += (((rows, n * video_rows), jnp.float32),) * 2 + (((rows, n * audio_rows), jnp.float32),)
    sight, asks0, asks1, values1, mask0, mask1, near = call(
        functools.partial(second_pack, n),
        outs,
        [SMEM, SMEM, VMEM] + [HBM] * 4,
        place,
        counts,
        offsets.reshape(1, -1),
        video_k,
        video_v,
        video_q,
        audio_q,
        out_specs=(VMEM,) * len(outs),
        scratch_shapes=[pltpu.SemaphoreType.DMA((7,))],
    )
    asks = [asks0, asks1]
    sights = [first_over, sight]

    keys_across = cross(raw_keys)
    values_across = [cross(values0), cross(values1)]
    first_mate = mate(first_out)
    sound_across = cross(first_out)
    second_mate = mate(first_over)
    sound_far = cross(second_mate)
    third_mate = mate(jnp.where(at_end, sight, sound_across))
    sight_mate = [first_mate, third_mate]
    sight_far = [cross(first_mate)]
    for i in range(1, last + 1):
        piece = third_mate[:, (i - 1) * HEAD_DIM : i * HEAD_DIM]
        sight_far.append(cross(piece))
    asks_mate = [mate(asks[i]) for i in range(2)]

    def look(i, queries, mask):
        at, size = sum(chunks[:i]), chunks[i]
        half = min(i, 1)
        return call(
            functools.partial(video_kernel, n, at, half * chunks[0]),
            (((rows, size * HEAD_DIM), jnp.bfloat16),),
            [SMEM] + [VMEM] * 7,
            place,
            mask,
            queries[half],
            sights[half],
            sight_mate[half],
            keys_across,
            values_across[half],
            sight_far[i],
            out_specs=(VMEM,),
            cost_estimate=cost(rows, n * video_rows, size),
        )[0]

    back = [mate(look(i, asks_mate, mask1)) for i in range(last + 1)]
    mine = [look(i, asks, mask0) for i in range(last + 1)]
    back_sound = []
    for i in range(2):
        theirs = call(
            functools.partial(audio_mate_kernel, n, i),
            (((audio_rows, half), jnp.bfloat16),),
            [SMEM] + [VMEM] * 5,
            place,
            asks_mate[i],
            first_out,
            second_mate,
            sound_across,
            sound_far,
            out_specs=(VMEM,),
            cost_estimate=cost(audio_rows, n * audio_rows, heads // 2),
        )[0]
        back_sound.append(mate(theirs))
    video_cross, own = call(
        functools.partial(audio_own_kernel, n),
        (((video_rows, width), jnp.bfloat16), ((audio_rows, width), jnp.bfloat16)),
        [SMEM] + [VMEM] * 10,
        place,
        near,
        *asks,
        first_out,
        first_over,
        first_mate,
        second_mate,
        third_mate,
        sound_across,
        sound_far,
        out_specs=(VMEM,) * 2,
        cost_estimate=cost(rows, n * audio_rows, heads),
    )
    video_shape = ((video_rows, width), jnp.bfloat16)
    audio_shape = ((audio_rows, width), jnp.bfloat16)
    video_self, video_cross, audio_self, audio_cross = call(
        functools.partial(place_kernel, n),
        (video_shape, video_shape, audio_shape, audio_shape),
        [SMEM] + [VMEM] * (4 + 2 * last),
        place,
        video_cross,
        own,
        *back_sound,
        *mine[:last],
        *back[:last],
        out_specs=(HBM,) * 4,
        scratch_shapes=[pltpu.SemaphoreType.DMA((3 + 2 * last,))],
    )
    video_self, audio_cross = call(
        functools.partial(place_last_kernel, n, width - HEAD_DIM),
        (video_shape, audio_shape),
        [SMEM] + [VMEM] * 2 + [HBM] * 2,
        place,
        mine[last],
        back[last],
        video_self,
        audio_cross,
        out_specs=(HBM,) * 2,
        scratch_shapes=[pltpu.SemaphoreType.DMA((2,))],
        input_output_aliases={3: 0, 4: 1},
    )
    return video_self, video_cross, audio_self, audio_cross


def solution(mesh):
    split = P(("groups", "seq"), ("tower", "mp"))
    placed = (split,) * 6 + (P("groups"), P("groups"))
    sizes = mesh.shape
    line = sizes["seq"] == 4 and sizes["mp"] == 2

    def whole(*arrays):
        heads = arrays[0].shape[1] // HEAD_DIM // (sizes["tower"] * sizes["mp"])
        paired = heads % 2 == 0 and heads > 3 and arrays[0].shape[0] == 2 * arrays[3].shape[0]
        body = lined if line and paired else gathered
        return jax.shard_map(
            body, mesh=mesh, in_specs=placed, out_specs=(split,) * 4, check_vma=False
        )(*arrays)

    return whole
```

```python
import functools

import jax
import jax.numpy as jnp
from jax import lax
from jax.experimental import pallas as pl
from jax.experimental.pallas import tpu as pltpu
from jax.sharding import PartitionSpec as P


HEAD_DIM = 128
SPAN = 1
STEP = 128
MASKED = -1e30
LOG2E = 1.4426950408889634
VMEM = pl.BlockSpec(memory_space=pltpu.VMEM)
SMEM = pl.BlockSpec(memory_space=pltpu.SMEM)
HBM = pl.BlockSpec(memory_space=pltpu.HBM)
PARAMS = pltpu.CompilerParams(vmem_limit_bytes=16 << 20)


def attend(queries, key_rows, value_rows, allowed):
    scores = jnp.einsum(
        "qhe,khe->hqk", queries, key_rows, preferred_element_type=jnp.float32
    ) * HEAD_DIM ** (-0.5)
    scores = jnp.where(allowed[None], scores, MASKED)
    peak = jnp.max(scores, axis=2)
    weights = jnp.where(allowed[None], jnp.exp(scores - peak[:, :, None]), 0.0)
    total = jnp.sum(weights, axis=2)
    blended = jnp.einsum(
        "hqk,khe->hqe", weights.astype(jnp.bfloat16), value_rows, preferred_element_type=jnp.float32
    )
    blended = blended / total[:, :, None]
    return jnp.transpose(blended, (1, 0, 2)).reshape(blended.shape[1], -1).astype(jnp.bfloat16)


def gathered(video_q, video_k, video_v, audio_q, audio_k, audio_v, offsets, counts):
    my_frame = lax.axis_index("seq")
    video_rows, audio_rows = video_q.shape[0], audio_q.shape[0]

    def heads(rows):
        return rows.reshape(rows.shape[0], -1, HEAD_DIM)

    def everywhere(rows):
        return heads(lax.all_gather(rows, "seq", axis=0, tiled=True))

    my_offsets = lax.dynamic_slice_in_dim(offsets, my_frame * audio_rows, audio_rows)
    keys, values = everywhere(video_k), everywhere(video_v)
    audio_keys, audio_values = everywhere(audio_k), everywhere(audio_v)
    positions = jnp.arange(keys.shape[0], dtype=jnp.int32)
    source = positions // video_rows
    is_live = positions % video_rows < jnp.repeat(counts, video_rows)
    video_self = attend(heads(video_q), keys, values, is_live[None, :])
    in_reach = (jnp.abs(my_offsets[:, None] - source[None, :]) <= SPAN) & is_live[None, :]
    audio_cross = attend(heads(audio_q), keys, values, in_reach)
    every = jnp.ones((1, audio_keys.shape[0]), jnp.bool_)
    audio_self = attend(heads(audio_q), audio_keys, audio_values, every)
    in_reach = jnp.abs(offsets - my_frame) <= SPAN
    video_cross = attend(heads(video_q), audio_keys, audio_values, in_reach[None, :])
    return (video_self, video_cross, audio_self, audio_cross)


def blend(queries, keys, values, bias):
    scores = lax.dot_general(
        queries, keys, (((1,), (1,)), ((), ())), preferred_element_type=jnp.float32
    )
    if bias is not None:
        scores = scores + bias
    peak = jnp.max(scores, axis=1, keepdims=True)
    weights = jnp.exp2((scores - peak) * (HEAD_DIM ** (-0.5) * LOG2E))
    total = jnp.sum(weights, axis=1, keepdims=True)
    weights = weights.astype(jnp.bfloat16)
    mixed = 0.0
    for at in range(0, keys.shape[0], STEP):
        mixed += jnp.dot(
            weights[:, at : at + STEP], values[at : at + STEP], preferred_element_type=jnp.float32
        )
    return (mixed * (1.0 / total)).astype(jnp.bfloat16)


def pick(pieces, at):
    chosen = pieces[0]
    for i in range(1, len(pieces)):
        chosen = jnp.where(at == i, pieces[i], chosen)
    return chosen


def move_all(moves, sem):
    copies = [pltpu.make_async_copy(src, dst, sem.at[i]) for i, (src, dst) in enumerate(moves)]
    for copy in copies:
        copy.start()
    return copies


def sight_moves(video_k, video_v, first, out):
    rows, cols = video_k.shape[0], pl.ds(first, out.shape[1])
    return [(video_k.at[:, cols], out.at[:rows]), (video_v.at[:, cols], out.at[rows:])]


def sound_moves(audio_k, audio_v, out):
    rows, width = audio_k.shape[0], out.shape[1]
    moves = []
    for src in (audio_k, audio_v):
        for half in range(2):
            at = len(moves) * rows
            moves.append((src.at[:, pl.ds(half * width, width)], out.at[at : at + rows]))
    return moves


def first_pack(n, me_ref, video_k, video_v, audio_k, audio_v, out_ref, over_ref, values_ref, sem):
    me = me_ref[0]
    half = values_ref.shape[1]
    at_end = (me == 0) | (me == n - 1)
    for role, sight, sound in ((at_end, out_ref, over_ref), (jnp.logical_not(at_end), over_ref, out_ref)):

        @pl.when(role)
        def _(sight=sight, sound=sound):
            moves = sight_moves(video_k, video_v, 0, sight) + sound_moves(audio_k, audio_v, sound)
            moves.append((video_v.at[:, pl.ds(0, half)], values_ref))
            for copy in move_all(moves, sem):
                copy.wait()


def second_pack(n, me_ref, count_ref, offset_ref, video_k, video_v, video_q, audio_q, *outs):
    sight1, sight2, asks0, asks1, values_ref, mask0_ref, mask1_ref, near_ref, sem = outs
    rows = video_q.shape[0]
    at = asks0.shape[1]
    moves = [(video_v.at[:, pl.ds(at, at)], values_ref)]
    for half, out in enumerate((asks0, asks1)):
        cols = pl.ds(half * at, at)
        moves += [(video_q.at[:, cols], out.at[:rows]), (audio_q.at[:, cols], out.at[rows:])]
    for out in (sight1, sight2):
        moves += sight_moves(video_k, video_v, at, out)
        at += out.shape[1]
    copies = move_all(moves, sem)
    tables(n, me_ref[0], count_ref, offset_ref, (mask0_ref, mask1_ref), near_ref)
    for copy in copies:
        copy.wait()


def tables(n, me, count_ref, offset_ref, mask_refs, near_ref):
    upper = me * 2 >= n
    inner, end = jnp.where(upper, 1, n - 2), jnp.where(upper, 0, n - 1)
    frames = (me, me ^ 1, inner, end)
    audio_rows = offset_ref.shape[1] // n
    video_rows = mask_refs[0].shape[1] // n
    pieces = [offset_ref[:, i * audio_rows : (i + 1) * audio_rows] for i in range(n)]
    offsets = jnp.concatenate([pick(pieces, frame) for frame in frames], axis=1)
    near = jnp.where(jnp.abs(offsets - me) <= SPAN, 0.0, MASKED)
    near_ref[:video_rows, :] = jnp.broadcast_to(near, (video_rows, n * audio_rows))
    near_ref[video_rows:, :] = jnp.zeros((audio_rows, n * audio_rows), jnp.float32)
    size = 2 * audio_rows
    corner = lax.broadcasted_iota(jnp.int32, (size, size), 0) == lax.broadcasted_iota(
        jnp.int32, (size, size), 1
    )
    asking = jnp.sum(jnp.where(corner, offsets[:, :size], 0), axis=1, keepdims=True)
    within = lax.broadcasted_iota(jnp.int32, (1, video_rows), 1)
    for i, frame in enumerate(frames):
        cols = slice(i * video_rows, (i + 1) * video_rows)
        live = jnp.where(within < count_ref[frame], 0.0, MASKED)
        reach = jnp.where(jnp.abs(asking - frame) <= SPAN, live, MASKED)
        for who, mask_ref in enumerate(mask_refs):
            mask_ref[:video_rows, cols] = jnp.broadcast_to(live, (video_rows, video_rows))
            mask_ref[video_rows:, cols] = reach[who * audio_rows : (who + 1) * audio_rows]


def sound_blocks(blocks, audio_rows, half, cols):
    key_rows = slice(half * audio_rows, (half + 1) * audio_rows)
    value_rows = slice((2 + half) * audio_rows, (3 + half) * audio_rows)
    keys = jnp.concatenate([b[key_rows, cols] for b in blocks], axis=0)
    values = jnp.concatenate([b[value_rows, cols] for b in blocks], axis=0)
    return keys, values


def audio_mate_kernel(n, me_ref, asks0, asks1, out, second, across, far, mate_ref):
    audio_rows, width = mate_ref.shape[0], out.shape[1]
    video_rows = asks0.shape[0] - audio_rows
    me = me_ref[0]

    @pl.when((me > 0) & (me < n - 1))
    def _():
        for half, asks in enumerate((asks0, asks1)):
            for at in range(0, width, HEAD_DIM):
                cols = slice(at, at + HEAD_DIM)
                to = slice(half * width + at, half * width + at + HEAD_DIM)
                keys, values = sound_blocks((out, second, across, far), audio_rows, half, cols)
                mate_ref[:, to] = blend(asks[video_rows:, cols], keys, values, None)


def audio_own_kernel(n, me_ref, near_ref, asks0, asks1, out, second, across, far, cross_ref, own_ref):
    audio_rows, width = own_ref.shape[0], out.shape[1]
    video_rows = cross_ref.shape[0]
    me = me_ref[0]

    @pl.when((me > 0) & (me < n - 1))
    def _():
        for half, asks in enumerate((asks0, asks1)):
            for at in range(0, width, HEAD_DIM):
                cols = slice(at, at + HEAD_DIM)
                to = slice(half * width + at, half * width + at + HEAD_DIM)
                keys, values = sound_blocks((out, second, across, far), audio_rows, half, cols)
                mixed = blend(asks[:, cols], keys, values, near_ref[...])
                cross_ref[:, to] = mixed[:video_rows]
                own_ref[:, to] = mixed[video_rows:]


def audio_end_kernel(n, me_ref, near_ref, asks0, asks1, over, first, part1, part2, far, cross_ref):
    video_rows, width = cross_ref.shape[0], over.shape[1]
    audio_rows = over.shape[0] // 4
    me = me_ref[0]

    @pl.when((me == 0) | (me == n - 1))
    def _():
        for half, asks in enumerate((asks0, asks1)):
            for at in range(0, width, HEAD_DIM):
                cols = slice(at, at + HEAD_DIM)
                to = slice(half * width + at, half * width + at + HEAD_DIM)
                shift = 0 if at < part1.shape[1] else part1.shape[1]
                part = (part2 if shift else part1).at[:, at - shift : at - shift + HEAD_DIM]
                blocks = [b.at[:, cols] for b in (over, first)] + [part, far.at[:, cols]]
                every = slice(0, HEAD_DIM)
                keys, values = sound_blocks(blocks, audio_rows, half, every)
                cross_ref[:, to] = blend(asks[:video_rows, cols], keys, values, near_ref[:video_rows])


def video_kernel(n, at, half, offset, me_ref, mask_ref, asks, own, mate, keys2, values2, far, out_ref):
    video_rows = own.shape[0] // 2
    me = me_ref[0]

    @pl.when((me > 0) & (me < n - 1))
    def _():
        for head in range(far.shape[1] // HEAD_DIM):
            cols = slice(head * HEAD_DIM, (head + 1) * HEAD_DIM)
            near_cols = slice((offset + head) * HEAD_DIM, (offset + head + 1) * HEAD_DIM)
            all_cols = slice((at + head) * HEAD_DIM, (at + head + 1) * HEAD_DIM)
            half_cols = slice((at - half + head) * HEAD_DIM, (at - half + head + 1) * HEAD_DIM)
            top, low = slice(0, video_rows), slice(video_rows, 2 * video_rows)
            keys = jnp.concatenate(
                [own[top, near_cols], mate[top, near_cols], keys2[:, all_cols], far[top, cols]], axis=0
            )
            values = jnp.concatenate(
                [own[low, near_cols], mate[low, near_cols], values2[:, half_cols], far[low, cols]],
                axis=0,
            )
            out_ref[:, cols] = blend(asks[:, half_cols], keys, values, mask_ref[...])


def place_pieces(parts, first, video_rows, video_self, audio_cross):
    moves, at = [], first
    for part in parts:
        cols = pl.ds(at, part.shape[1])
        moves.append((part.at[:video_rows], video_self.at[:, cols]))
        moves.append((part.at[video_rows:], audio_cross.at[:, cols]))
        at += part.shape[1]
    return moves


def place_kernel(n, me_ref, own_cross, end_cross, *refs):
    count = (len(refs) - 5) // 2
    own, back = refs[:count], refs[count : 2 * count]
    video_self, video_cross, audio_self, audio_cross, sem = refs[2 * count :]
    at_end = (me_ref[0] == 0) | (me_ref[0] == n - 1)
    for role, cross, parts in (
        (jnp.logical_not(at_end), own_cross, own),
        (at_end, end_cross, back),
    ):

        @pl.when(role)
        def _(cross=cross, parts=parts):
            moves = [(cross, video_cross), (parts[0], audio_self)]
            moves += place_pieces(parts[1:], 0, cross.shape[0], video_self, audio_cross)
            for copy in move_all(moves, sem):
                copy.wait()


def place_last_kernel(n, first, me_ref, own, back, old_self, old_cross, video_self, audio_cross, sem):
    at_end = (me_ref[0] == 0) | (me_ref[0] == n - 1)
    for role, part in ((jnp.logical_not(at_end), own), (at_end, back)):

        @pl.when(role)
        def _(part=part):
            moves = place_pieces((part,), first, video_self.shape[0], video_self, audio_cross)
            for copy in move_all(moves, sem):
                copy.wait()


def cost(rows, keys, heads):
    scores = rows * keys * heads
    return pl.CostEstimate(flops=4 * scores * HEAD_DIM, bytes_accessed=rows * heads * 512, transcendentals=scores)


def chunks_of(heads):
    head = heads // 2
    return head, (head + 1) // 2, head // 2


def lined(video_q, video_k, video_v, audio_q, audio_k, audio_v, offsets, counts):
    n, cores = lax.axis_size("seq"), lax.axis_size("mp")
    me = lax.axis_index("seq")
    video_rows, audio_rows = video_q.shape[0], audio_q.shape[0]
    rows = video_rows + audio_rows
    width = video_q.shape[1]
    heads = width // HEAD_DIM
    chunks = chunks_of(heads)
    mate_pairs = [(i, i ^ 1) for i in range(n)]
    cross_pairs = []
    for i in range(n):
        for core in range(cores):
            inner = 0 < i < n - 1
            to = (n - 1 - i) * cores + core if inner else i * cores + cores - 1 - core
            cross_pairs.append((i * cores + core, to))

    def mate(block):
        return lax.ppermute(block, "seq", mate_pairs)

    def cross(block):
        return lax.ppermute(block, ("seq", "mp"), cross_pairs)

    def call(kernel, outs, spaces, *args, **more):
        return pl.pallas_call(
            kernel,
            out_shape=tuple(jax.ShapeDtypeStruct(shape, dtype) for shape, dtype in outs),
            in_specs=spaces,
            compiler_params=PARAMS,
            **more,
        )(*args)

    place = me.astype(jnp.int32).reshape(1)
    raw_keys = video_k
    video_q, video_k, video_v, audio_q, audio_k, audio_v = (
        pltpu.with_memory_space_constraint(block, pltpu.HBM)
        for block in (video_q, video_k, video_v, audio_q, audio_k, audio_v)
    )
    at_end = (me == 0) | (me == n - 1)
    lengths = [size * HEAD_DIM for size in chunks]
    half = lengths[0]
    first_out, first_over, values0 = call(
        functools.partial(first_pack, n),
        (((2 * video_rows, half), jnp.bfloat16),) * 2 + (((video_rows, half), jnp.bfloat16),),
        [SMEM] + [HBM] * 4,
        place,
        video_k,
        video_v,
        audio_k,
        audio_v,
        out_specs=(VMEM,) * 3,
        scratch_shapes=[pltpu.SemaphoreType.DMA((7,))],
    )
    outs = tuple(((2 * video_rows, length), jnp.bfloat16) for length in lengths[1:])
    outs += (((rows, half), jnp.bfloat16),) * 2
    outs += (((video_rows, half), jnp.bfloat16),)
    outs += (((rows, n * video_rows), jnp.float32),) * 2 + (((rows, n * audio_rows), jnp.float32),)
    *sights, asks0, asks1, values1, mask0, mask1, near = call(
        functools.partial(second_pack, n),
        outs,
        [SMEM, SMEM, VMEM] + [HBM] * 4,
        place,
        counts,
        offsets.reshape(1, -1),
        video_k,
        video_v,
        video_q,
        audio_q,
        out_specs=(VMEM,) * len(outs),
        scratch_shapes=[pltpu.SemaphoreType.DMA((9,))],
    )
    asks = [asks0, asks1]
    sights = [first_over] + sights

    keys_across = cross(raw_keys)
    values_across = [cross(values0), cross(values1)]
    sight_mate = [mate(first_out)]
    sound_across = cross(first_out)
    second_mate = mate(first_over)
    sound_far = cross(second_mate)
    at = 0
    for i in (1, 2):
        part = sound_across[:, at : at + lengths[i]]
        sight_mate.append(mate(jnp.where(at_end, sights[i], part)))
        at += lengths[i]
    pieces = [(0, chunks[0], 0, 0)]
    sight_far = [cross(sight_mate[0])]
    for source in (1, 2):
        for i in range(chunks[source]):
            pieces.append((sum(chunks[:source]) + i, 1, source, i))
            part = sight_mate[source]
            if chunks[source] > 1:
                part = part[:, i * HEAD_DIM : (i + 1) * HEAD_DIM]
            sight_far.append(cross(part))
    last = len(pieces) - 1
    asks_mate = [mate(asks[i]) for i in range(2)]

    def look(i, queries, mask):
        at, size, source, offset = pieces[i]
        half = min(source, 1)
        return call(
            functools.partial(video_kernel, n, at, half * chunks[0], offset),
            (((rows, size * HEAD_DIM), jnp.bfloat16),),
            [SMEM] + [VMEM] * 7,
            place,
            mask,
            queries[half],
            sights[source],
            sight_mate[source],
            keys_across,
            values_across[half],
            sight_far[i],
            out_specs=(VMEM,),
            cost_estimate=cost(rows, n * video_rows, size),
        )[0]

    back = [mate(look(i, asks_mate, mask1)) for i in range(last + 1)]
    mine = [look(i, asks, mask0) for i in range(last + 1)]
    theirs = call(
        functools.partial(audio_mate_kernel, n),
        (((audio_rows, width), jnp.bfloat16),),
        [SMEM] + [VMEM] * 6,
        place,
        *asks_mate,
        first_out,
        second_mate,
        sound_across,
        sound_far,
        out_specs=(VMEM,),
        cost_estimate=cost(audio_rows, n * audio_rows, heads),
    )[0]
    own_cross, own = call(
        functools.partial(audio_own_kernel, n),
        (((video_rows, width), jnp.bfloat16), ((audio_rows, width), jnp.bfloat16)),
        [SMEM] + [VMEM] * 7,
        place,
        near,
        *asks,
        first_out,
        second_mate,
        sound_across,
        sound_far,
        out_specs=(VMEM,) * 2,
        cost_estimate=cost(rows, n * audio_rows, heads),
    )
    end_cross = call(
        functools.partial(audio_end_kernel, n),
        (((video_rows, width), jnp.bfloat16),),
        [SMEM] + [VMEM] * 8,
        place,
        near,
        *asks,
        first_over,
        sight_mate[0],
        sight_mate[1],
        sight_mate[2],
        sound_far,
        out_specs=(VMEM,),
        cost_estimate=cost(rows, n * audio_rows, heads),
    )[0]
    back_sound = mate(theirs)
    video_shape = ((video_rows, width), jnp.bfloat16)
    audio_shape = ((audio_rows, width), jnp.bfloat16)
    video_self, video_cross, audio_self, audio_cross = call(
        functools.partial(place_kernel, n),
        (video_shape, video_shape, audio_shape, audio_shape),
        [SMEM] + [VMEM] * (4 + 2 * last),
        place,
        own_cross,
        end_cross,
        own,
        *mine[:last],
        back_sound,
        *back[:last],
        out_specs=(HBM,) * 4,
        scratch_shapes=[pltpu.SemaphoreType.DMA((2 + 2 * last,))],
    )
    video_self, audio_cross = call(
        functools.partial(place_last_kernel, n, width - HEAD_DIM),
        (video_shape, audio_shape),
        [SMEM] + [VMEM] * 2 + [HBM] * 2,
        place,
        mine[last],
        back[last],
        video_self,
        audio_cross,
        out_specs=(HBM,) * 2,
        scratch_shapes=[pltpu.SemaphoreType.DMA((2,))],
        input_output_aliases={3: 0, 4: 1},
    )
    return video_self, video_cross, audio_self, audio_cross


def solution(mesh):
    split = P(("groups", "seq"), ("tower", "mp"))
    placed = (split,) * 6 + (P("groups"), P("groups"))
    sizes = mesh.shape
    line = sizes["seq"] == 4 and sizes["mp"] == 2

    def whole(*arrays):
        heads = arrays[0].shape[1] // HEAD_DIM // (sizes["tower"] * sizes["mp"])
        paired = heads % 2 == 0 and heads > 3 and arrays[0].shape[0] == 2 * arrays[3].shape[0]
        body = lined if line and paired else gathered
        return jax.shard_map(
            body, mesh=mesh, in_specs=placed, out_specs=(split,) * 4, check_vma=False
        )(*arrays)

    return whole
```

```python
import functools

import jax
import jax.numpy as jnp
from jax import lax
from jax.experimental import pallas as pl
from jax.experimental.pallas import tpu as pltpu
from jax.sharding import PartitionSpec as P


HEAD_DIM = 128
SPAN = 1
STEP = 128
MASKED = -1e30
LOG2E = 1.4426950408889634
VMEM = pl.BlockSpec(memory_space=pltpu.VMEM)
SMEM = pl.BlockSpec(memory_space=pltpu.SMEM)
HBM = pl.BlockSpec(memory_space=pltpu.HBM)
PARAMS = pltpu.CompilerParams(vmem_limit_bytes=16 << 20)


def attend(queries, key_rows, value_rows, allowed):
    scores = jnp.einsum(
        "qhe,khe->hqk", queries, key_rows, preferred_element_type=jnp.float32
    ) * HEAD_DIM ** (-0.5)
    scores = jnp.where(allowed[None], scores, MASKED)
    peak = jnp.max(scores, axis=2)
    weights = jnp.where(allowed[None], jnp.exp(scores - peak[:, :, None]), 0.0)
    total = jnp.sum(weights, axis=2)
    blended = jnp.einsum(
        "hqk,khe->hqe", weights.astype(jnp.bfloat16), value_rows, preferred_element_type=jnp.float32
    )
    blended = blended / total[:, :, None]
    return jnp.transpose(blended, (1, 0, 2)).reshape(blended.shape[1], -1).astype(jnp.bfloat16)


def gathered(video_q, video_k, video_v, audio_q, audio_k, audio_v, offsets, counts):
    my_frame = lax.axis_index("seq")
    video_rows, audio_rows = video_q.shape[0], audio_q.shape[0]

    def heads(rows):
        return rows.reshape(rows.shape[0], -1, HEAD_DIM)

    def everywhere(rows):
        return heads(lax.all_gather(rows, "seq", axis=0, tiled=True))

    my_offsets = lax.dynamic_slice_in_dim(offsets, my_frame * audio_rows, audio_rows)
    keys, values = everywhere(video_k), everywhere(video_v)
    audio_keys, audio_values = everywhere(audio_k), everywhere(audio_v)
    positions = jnp.arange(keys.shape[0], dtype=jnp.int32)
    source = positions // video_rows
    is_live = positions % video_rows < jnp.repeat(counts, video_rows)
    video_self = attend(heads(video_q), keys, values, is_live[None, :])
    in_reach = (jnp.abs(my_offsets[:, None] - source[None, :]) <= SPAN) & is_live[None, :]
    audio_cross = attend(heads(audio_q), keys, values, in_reach)
    every = jnp.ones((1, audio_keys.shape[0]), jnp.bool_)
    audio_self = attend(heads(audio_q), audio_keys, audio_values, every)
    in_reach = jnp.abs(offsets - my_frame) <= SPAN
    video_cross = attend(heads(video_q), audio_keys, audio_values, in_reach[None, :])
    return (video_self, video_cross, audio_self, audio_cross)


def blend(queries, keys, values, bias):
    scores = lax.dot_general(
        queries, keys, (((1,), (1,)), ((), ())), preferred_element_type=jnp.float32
    )
    if bias is not None:
        scores = scores + bias
    peak = jnp.max(scores, axis=1, keepdims=True)
    weights = jnp.exp2((scores - peak) * (HEAD_DIM ** (-0.5) * LOG2E))
    total = jnp.sum(weights, axis=1, keepdims=True)
    weights = weights.astype(jnp.bfloat16)
    mixed = 0.0
    for at in range(0, keys.shape[0], STEP):
        mixed += jnp.dot(
            weights[:, at : at + STEP], values[at : at + STEP], preferred_element_type=jnp.float32
        )
    return (mixed * (1.0 / total)).astype(jnp.bfloat16)


def pick(pieces, at):
    chosen = pieces[0]
    for i in range(1, len(pieces)):
        chosen = jnp.where(at == i, pieces[i], chosen)
    return chosen


def move_all(moves, sem):
    copies = [pltpu.make_async_copy(src, dst, sem.at[i]) for i, (src, dst) in enumerate(moves)]
    for copy in copies:
        copy.start()
    return copies


def sight_moves(video_k, video_v, first, out):
    rows, cols = video_k.shape[0], pl.ds(first, out.shape[1])
    return [(video_k.at[:, cols], out.at[:rows]), (video_v.at[:, cols], out.at[rows:])]


def sound_moves(audio_k, audio_v, out):
    rows, width = audio_k.shape[0], out.shape[1]
    moves = []
    for src in (audio_k, audio_v):
        for half in range(2):
            at = len(moves) * rows
            moves.append((src.at[:, pl.ds(half * width, width)], out.at[at : at + rows]))
    return moves


def first_pack(n, me_ref, video_k, video_v, audio_k, audio_v, out_ref, over_ref, values_ref, sem):
    me = me_ref[0]
    half = values_ref.shape[1]
    at_end = (me == 0) | (me == n - 1)
    for role, sight, sound in ((at_end, out_ref, over_ref), (jnp.logical_not(at_end), over_ref, out_ref)):

        @pl.when(role)
        def _(sight=sight, sound=sound):
            moves = sight_moves(video_k, video_v, 0, sight) + sound_moves(audio_k, audio_v, sound)
            moves.append((video_v.at[:, pl.ds(0, half)], values_ref))
            for copy in move_all(moves, sem):
                copy.wait()


def second_pack(n, me_ref, count_ref, offset_ref, video_k, video_v, video_q, audio_q, *outs):
    sight1, sight2, asks0, asks1, values_ref, mask0_ref, mask1_ref, near_ref, sem = outs
    half = asks0.shape[1]
    low, high = pl.ds(0, half), pl.ds(half, half)
    rows, more = video_q.shape[0], audio_q.shape[0]
    moves = [
        (video_q.at[:, low], asks0.at[:rows]),
        (audio_q.at[:, low], asks0.at[rows : rows + more]),
        (audio_q.at[:, high], asks0.at[rows + more :]),
        (video_q.at[:, high], asks1),
        (video_v.at[:, high], values_ref),
    ]
    at = half
    for out in (sight1, sight2):
        moves += sight_moves(video_k, video_v, at, out)
        at += out.shape[1]
    copies = move_all(moves, sem)
    tables(n, me_ref[0], count_ref, offset_ref, (mask0_ref, mask1_ref), near_ref)
    for copy in copies:
        copy.wait()


def tables(n, me, count_ref, offset_ref, mask_refs, near_ref):
    upper = me * 2 >= n
    inner, end = jnp.where(upper, 1, n - 2), jnp.where(upper, 0, n - 1)
    frames = (me, me ^ 1, inner, end)
    audio_rows = offset_ref.shape[1] // n
    video_rows = mask_refs[0].shape[1] // n
    pieces = [offset_ref[:, i * audio_rows : (i + 1) * audio_rows] for i in range(n)]
    offsets = jnp.concatenate([pick(pieces, frame) for frame in frames], axis=1)
    near = jnp.where(jnp.abs(offsets - me) <= SPAN, 0.0, MASKED)
    near_ref[:video_rows, :] = jnp.broadcast_to(near, (video_rows, n * audio_rows))
    near_ref[video_rows:, :] = jnp.zeros((audio_rows, n * audio_rows), jnp.float32)
    size = 2 * audio_rows
    corner = lax.broadcasted_iota(jnp.int32, (size, size), 0) == lax.broadcasted_iota(
        jnp.int32, (size, size), 1
    )
    asking = jnp.sum(jnp.where(corner, offsets[:, :size], 0), axis=1, keepdims=True)
    within = lax.broadcasted_iota(jnp.int32, (1, video_rows), 1)
    for i, frame in enumerate(frames):
        cols = slice(i * video_rows, (i + 1) * video_rows)
        live = jnp.where(within < count_ref[frame], 0.0, MASKED)
        reach = jnp.where(jnp.abs(asking - frame) <= SPAN, live, MASKED)
        for who, mask_ref in enumerate(mask_refs):
            mask_ref[:video_rows, cols] = jnp.broadcast_to(live, (video_rows, video_rows))
            mask_ref[video_rows:, cols] = reach[who * audio_rows : (who + 1) * audio_rows]


def sound_blocks(blocks, audio_rows, half, cols):
    key_rows = slice(half * audio_rows, (half + 1) * audio_rows)
    value_rows = slice((2 + half) * audio_rows, (3 + half) * audio_rows)
    keys = jnp.concatenate([b[key_rows, cols] for b in blocks], axis=0)
    values = jnp.concatenate([b[value_rows, cols] for b in blocks], axis=0)
    return keys, values


def queries_of(half, asks0, asks1, video_rows, audio_rows, cols):
    rows = video_rows + audio_rows
    if half == 0:
        return asks0[:rows, cols]
    return jnp.concatenate([asks1[:, cols], asks0[rows:, cols]], axis=0)


def audio_mate_kernel(n, me_ref, asks0, out, second, across, far, mate_ref):
    audio_rows, width = mate_ref.shape[0], out.shape[1]
    me = me_ref[0]

    @pl.when((me > 0) & (me < n - 1))
    def _():
        for half in range(2):
            first = asks0.shape[0] - (2 - half) * audio_rows
            for at in range(0, width, HEAD_DIM):
                cols = slice(at, at + HEAD_DIM)
                to = slice(half * width + at, half * width + at + HEAD_DIM)
                keys, values = sound_blocks((out, second, across, far), audio_rows, half, cols)
                mate_ref[:, to] = blend(asks0[first : first + audio_rows, cols], keys, values, None)


def audio_own_kernel(n, me_ref, near_ref, asks0, asks1, out, second, across, far, cross_ref, own_ref):
    audio_rows, width = own_ref.shape[0], out.shape[1]
    video_rows = cross_ref.shape[0]
    me = me_ref[0]

    @pl.when((me > 0) & (me < n - 1))
    def _():
        for half in range(2):
            for at in range(0, width, HEAD_DIM):
                cols = slice(at, at + HEAD_DIM)
                to = slice(half * width + at, half * width + at + HEAD_DIM)
                keys, values = sound_blocks((out, second, across, far), audio_rows, half, cols)
                queries = queries_of(half, asks0, asks1, video_rows, audio_rows, cols)
                mixed = blend(queries, keys, values, near_ref[...])
                cross_ref[:, to] = mixed[:video_rows]
                own_ref[:, to] = mixed[video_rows:]


def audio_end_kernel(n, me_ref, near_ref, asks0, asks1, over, first, part1, part2, far, cross_ref):
    video_rows, width = cross_ref.shape[0], over.shape[1]
    audio_rows = over.shape[0] // 4
    me = me_ref[0]

    @pl.when((me == 0) | (me == n - 1))
    def _():
        for half, asks in enumerate((asks0, asks1)):
            for at in range(0, width, HEAD_DIM):
                cols = slice(at, at + HEAD_DIM)
                to = slice(half * width + at, half * width + at + HEAD_DIM)
                shift = 0 if at < part1.shape[1] else part1.shape[1]
                part = (part2 if shift else part1).at[:, at - shift : at - shift + HEAD_DIM]
                blocks = [b.at[:, cols] for b in (over, first)] + [part, far.at[:, cols]]
                every = slice(0, HEAD_DIM)
                keys, values = sound_blocks(blocks, audio_rows, half, every)
                cross_ref[:, to] = blend(asks[:video_rows, cols], keys, values, near_ref[:video_rows])


def video_kernel(n, at, half, offset, me_ref, mask_ref, *refs):
    *asks, own, mate, keys2, values2, far, out_ref = refs
    video_rows = own.shape[0] // 2
    audio_rows = out_ref.shape[0] - video_rows
    me = me_ref[0]

    @pl.when((me > 0) & (me < n - 1))
    def _():
        for head in range(far.shape[1] // HEAD_DIM):
            cols = slice(head * HEAD_DIM, (head + 1) * HEAD_DIM)
            near_cols = slice((offset + head) * HEAD_DIM, (offset + head + 1) * HEAD_DIM)
            all_cols = slice((at + head) * HEAD_DIM, (at + head + 1) * HEAD_DIM)
            half_cols = slice((at - half + head) * HEAD_DIM, (at - half + head + 1) * HEAD_DIM)
            top, low = slice(0, video_rows), slice(video_rows, 2 * video_rows)
            keys = jnp.concatenate(
                [own[top, near_cols], mate[top, near_cols], keys2[:, all_cols], far[top, cols]], axis=0
            )
            values = jnp.concatenate(
                [own[low, near_cols], mate[low, near_cols], values2[:, half_cols], far[low, cols]],
                axis=0,
            )
            queries = queries_of(len(asks) - 1, asks[0], asks[-1], video_rows, audio_rows, half_cols)
            out_ref[:, cols] = blend(queries, keys, values, mask_ref[...])


def place_pieces(parts, first, video_rows, video_self, audio_cross):
    moves, at = [], first
    for part in parts:
        cols = pl.ds(at, part.shape[1])
        moves.append((part.at[:video_rows], video_self.at[:, cols]))
        moves.append((part.at[video_rows:], audio_cross.at[:, cols]))
        at += part.shape[1]
    return moves


def place_kernel(n, me_ref, own_cross, end_cross, *refs):
    count = (len(refs) - 5) // 2
    own, back = refs[:count], refs[count : 2 * count]
    video_self, video_cross, audio_self, audio_cross, sem = refs[2 * count :]
    at_end = (me_ref[0] == 0) | (me_ref[0] == n - 1)
    for role, cross, parts in (
        (jnp.logical_not(at_end), own_cross, own),
        (at_end, end_cross, back),
    ):

        @pl.when(role)
        def _(cross=cross, parts=parts):
            moves = [(cross, video_cross), (parts[0], audio_self)]
            moves += place_pieces(parts[1:], 0, cross.shape[0], video_self, audio_cross)
            for copy in move_all(moves, sem):
                copy.wait()


def place_last_kernel(n, first, me_ref, own, back, old_self, old_cross, video_self, audio_cross, sem):
    at_end = (me_ref[0] == 0) | (me_ref[0] == n - 1)
    for role, part in ((jnp.logical_not(at_end), own), (at_end, back)):

        @pl.when(role)
        def _(part=part):
            moves = place_pieces((part,), first, video_self.shape[0], video_self, audio_cross)
            for copy in move_all(moves, sem):
                copy.wait()


def cost(rows, keys, heads):
    scores = rows * keys * heads
    return pl.CostEstimate(flops=4 * scores * HEAD_DIM, bytes_accessed=rows * heads * 512, transcendentals=scores)


def chunks_of(heads):
    head = heads // 2
    return head, (head + 1) // 2, head // 2


def lined(video_q, video_k, video_v, audio_q, audio_k, audio_v, offsets, counts):
    n, cores = lax.axis_size("seq"), lax.axis_size("mp")
    me = lax.axis_index("seq")
    video_rows, audio_rows = video_q.shape[0], audio_q.shape[0]
    rows = video_rows + audio_rows
    width = video_q.shape[1]
    heads = width // HEAD_DIM
    chunks = chunks_of(heads)
    mate_pairs = [(i, i ^ 1) for i in range(n)]
    cross_pairs = []
    for i in range(n):
        for core in range(cores):
            inner = 0 < i < n - 1
            to = (n - 1 - i) * cores + core if inner else i * cores + cores - 1 - core
            cross_pairs.append((i * cores + core, to))

    def mate(block):
        return lax.ppermute(block, "seq", mate_pairs)

    def cross(block):
        return lax.ppermute(block, ("seq", "mp"), cross_pairs)

    def call(kernel, outs, spaces, *args, **more):
        return pl.pallas_call(
            kernel,
            out_shape=tuple(jax.ShapeDtypeStruct(shape, dtype) for shape, dtype in outs),
            in_specs=spaces,
            compiler_params=PARAMS,
            **more,
        )(*args)

    place = me.astype(jnp.int32).reshape(1)
    raw_keys = video_k
    video_q, video_k, video_v, audio_q, audio_k, audio_v = (
        pltpu.with_memory_space_constraint(block, pltpu.HBM)
        for block in (video_q, video_k, video_v, audio_q, audio_k, audio_v)
    )
    at_end = (me == 0) | (me == n - 1)
    lengths = [size * HEAD_DIM for size in chunks]
    half = lengths[0]
    first_out, first_over, values0 = call(
        functools.partial(first_pack, n),
        (((2 * video_rows, half), jnp.bfloat16),) * 2 + (((video_rows, half), jnp.bfloat16),),
        [SMEM] + [HBM] * 4,
        place,
        video_k,
        video_v,
        audio_k,
        audio_v,
        out_specs=(VMEM,) * 3,
        scratch_shapes=[pltpu.SemaphoreType.DMA((7,))],
    )
    outs = tuple(((2 * video_rows, length), jnp.bfloat16) for length in lengths[1:])
    outs += (((rows + audio_rows, half), jnp.bfloat16), ((video_rows, half), jnp.bfloat16))
    outs += (((video_rows, half), jnp.bfloat16),)
    outs += (((rows, n * video_rows), jnp.float32),) * 2 + (((rows, n * audio_rows), jnp.float32),)
    *sights, asks0, asks1, values1, mask0, mask1, near = call(
        functools.partial(second_pack, n),
        outs,
        [SMEM, SMEM, VMEM] + [HBM] * 4,
        place,
        counts,
        offsets.reshape(1, -1),
        video_k,
        video_v,
        video_q,
        audio_q,
        out_specs=(VMEM,) * len(outs),
        scratch_shapes=[pltpu.SemaphoreType.DMA((9,))],
    )
    asks = [asks0, asks1]
    sights = [first_over] + sights

    keys_across = cross(raw_keys)
    values_across = [cross(values0), cross(values1)]
    sight_mate = [mate(first_out)]
    sound_across = cross(first_out)
    second_mate = mate(first_over)
    sound_far = cross(second_mate)
    at = 0
    for i in (1, 2):
        part = sound_across[:, at : at + lengths[i]]
        sight_mate.append(mate(jnp.where(at_end, sights[i], part)))
        at += lengths[i]
    pieces = [(0, chunks[0], 0, 0)]
    sight_far = [cross(sight_mate[0])]
    for source in (1, 2):
        for i in range(chunks[source]):
            pieces.append((sum(chunks[:source]) + i, 1, source, i))
            part = sight_mate[source]
            if chunks[source] > 1:
                part = part[:, i * HEAD_DIM : (i + 1) * HEAD_DIM]
            sight_far.append(cross(part))
    last = len(pieces) - 1
    asks_mate = [mate(asks[i]) for i in range(2)]

    def look(i, queries, mask):
        at, size, source, offset = pieces[i]
        half = min(source, 1)
        return call(
            functools.partial(video_kernel, n, at, half * chunks[0], offset),
            (((rows, size * HEAD_DIM), jnp.bfloat16),),
            [SMEM] + [VMEM] * (7 + half),
            place,
            mask,
            *queries[: 1 + half],
            sights[source],
            sight_mate[source],
            keys_across,
            values_across[half],
            sight_far[i],
            out_specs=(VMEM,),
            cost_estimate=cost(rows, n * video_rows, size),
        )[0]

    back = [mate(look(i, asks_mate, mask1)) for i in range(last + 1)]
    mine = [look(i, asks, mask0) for i in range(last + 1)]
    theirs = call(
        functools.partial(audio_mate_kernel, n),
        (((audio_rows, width), jnp.bfloat16),),
        [SMEM] + [VMEM] * 5,
        place,
        asks_mate[0],
        first_out,
        second_mate,
        sound_across,
        sound_far,
        out_specs=(VMEM,),
        cost_estimate=cost(audio_rows, n * audio_rows, heads),
    )[0]
    own_cross, own = call(
        functools.partial(audio_own_kernel, n),
        (((video_rows, width), jnp.bfloat16), ((audio_rows, width), jnp.bfloat16)),
        [SMEM] + [VMEM] * 7,
        place,
        near,
        *asks,
        first_out,
        second_mate,
        sound_across,
        sound_far,
        out_specs=(VMEM,) * 2,
        cost_estimate=cost(rows, n * audio_rows, heads),
    )
    end_cross = call(
        functools.partial(audio_end_kernel, n),
        (((video_rows, width), jnp.bfloat16),),
        [SMEM] + [VMEM] * 8,
        place,
        near,
        *asks,
        first_over,
        sight_mate[0],
        sight_mate[1],
        sight_mate[2],
        sound_far,
        out_specs=(VMEM,),
        cost_estimate=cost(rows, n * audio_rows, heads),
    )[0]
    back_sound = mate(theirs)
    video_shape = ((video_rows, width), jnp.bfloat16)
    audio_shape = ((audio_rows, width), jnp.bfloat16)
    video_self, video_cross, audio_self, audio_cross = call(
        functools.partial(place_kernel, n),
        (video_shape, video_shape, audio_shape, audio_shape),
        [SMEM] + [VMEM] * (4 + 2 * last),
        place,
        own_cross,
        end_cross,
        own,
        *mine[:last],
        back_sound,
        *back[:last],
        out_specs=(HBM,) * 4,
        scratch_shapes=[pltpu.SemaphoreType.DMA((2 + 2 * last,))],
    )
    video_self, audio_cross = call(
        functools.partial(place_last_kernel, n, width - HEAD_DIM),
        (video_shape, audio_shape),
        [SMEM] + [VMEM] * 2 + [HBM] * 2,
        place,
        mine[last],
        back[last],
        video_self,
        audio_cross,
        out_specs=(HBM,) * 2,
        scratch_shapes=[pltpu.SemaphoreType.DMA((2,))],
        input_output_aliases={3: 0, 4: 1},
    )
    return video_self, video_cross, audio_self, audio_cross


def solution(mesh):
    split = P(("groups", "seq"), ("tower", "mp"))
    placed = (split,) * 6 + (P("groups"), P("groups"))
    sizes = mesh.shape
    line = sizes["seq"] == 4 and sizes["mp"] == 2

    def whole(*arrays):
        heads = arrays[0].shape[1] // HEAD_DIM // (sizes["tower"] * sizes["mp"])
        paired = heads % 2 == 0 and heads > 3 and arrays[0].shape[0] == 2 * arrays[3].shape[0]
        body = lined if line and paired else gathered
        return jax.shard_map(
            body, mesh=mesh, in_specs=placed, out_specs=(split,) * 4, check_vma=False
        )(*arrays)

    return whole
```

```python
import functools

import jax
import jax.numpy as jnp
from jax import lax
from jax.experimental import pallas as pl
from jax.experimental.pallas import tpu as pltpu
from jax.sharding import PartitionSpec as P


HEAD_DIM = 128
SPAN = 1
STEP = 128
MASKED = -1e30
LOG2E = 1.4426950408889634
VMEM = pl.BlockSpec(memory_space=pltpu.VMEM)
SMEM = pl.BlockSpec(memory_space=pltpu.SMEM)
HBM = pl.BlockSpec(memory_space=pltpu.HBM)
PARAMS = pltpu.CompilerParams(vmem_limit_bytes=16 << 20)


def attend(queries, key_rows, value_rows, allowed):
    scores = jnp.einsum(
        "qhe,khe->hqk", queries, key_rows, preferred_element_type=jnp.float32
    ) * HEAD_DIM ** (-0.5)
    scores = jnp.where(allowed[None], scores, MASKED)
    peak = jnp.max(scores, axis=2)
    weights = jnp.where(allowed[None], jnp.exp(scores - peak[:, :, None]), 0.0)
    total = jnp.sum(weights, axis=2)
    blended = jnp.einsum(
        "hqk,khe->hqe", weights.astype(jnp.bfloat16), value_rows, preferred_element_type=jnp.float32
    )
    blended = blended / total[:, :, None]
    return jnp.transpose(blended, (1, 0, 2)).reshape(blended.shape[1], -1).astype(jnp.bfloat16)


def gathered(video_q, video_k, video_v, audio_q, audio_k, audio_v, offsets, counts):
    my_frame = lax.axis_index("seq")
    video_rows, audio_rows = video_q.shape[0], audio_q.shape[0]

    def heads(rows):
        return rows.reshape(rows.shape[0], -1, HEAD_DIM)

    def everywhere(rows):
        return heads(lax.all_gather(rows, "seq", axis=0, tiled=True))

    my_offsets = lax.dynamic_slice_in_dim(offsets, my_frame * audio_rows, audio_rows)
    keys, values = everywhere(video_k), everywhere(video_v)
    audio_keys, audio_values = everywhere(audio_k), everywhere(audio_v)
    positions = jnp.arange(keys.shape[0], dtype=jnp.int32)
    source = positions // video_rows
    is_live = positions % video_rows < jnp.repeat(counts, video_rows)
    video_self = attend(heads(video_q), keys, values, is_live[None, :])
    in_reach = (jnp.abs(my_offsets[:, None] - source[None, :]) <= SPAN) & is_live[None, :]
    audio_cross = attend(heads(audio_q), keys, values, in_reach)
    every = jnp.ones((1, audio_keys.shape[0]), jnp.bool_)
    audio_self = attend(heads(audio_q), audio_keys, audio_values, every)
    in_reach = jnp.abs(offsets - my_frame) <= SPAN
    video_cross = attend(heads(video_q), audio_keys, audio_values, in_reach[None, :])
    return (video_self, video_cross, audio_self, audio_cross)


def blend(queries, keys, values, bias):
    scores = lax.dot_general(
        queries, keys, (((1,), (1,)), ((), ())), preferred_element_type=jnp.float32
    )
    if bias is not None:
        scores = scores + bias
    peak = jnp.max(scores, axis=1, keepdims=True)
    weights = jnp.exp2((scores - peak) * (HEAD_DIM ** (-0.5) * LOG2E))
    total = jnp.sum(weights, axis=1, keepdims=True)
    weights = weights.astype(jnp.bfloat16)
    mixed = 0.0
    for at in range(0, keys.shape[0], STEP):
        mixed += jnp.dot(
            weights[:, at : at + STEP], values[at : at + STEP], preferred_element_type=jnp.float32
        )
    return (mixed * (1.0 / total)).astype(jnp.bfloat16)


def pick(pieces, at):
    chosen = pieces[0]
    for i in range(1, len(pieces)):
        chosen = jnp.where(at == i, pieces[i], chosen)
    return chosen


def move_all(moves, sem):
    copies = [pltpu.make_async_copy(src, dst, sem.at[i]) for i, (src, dst) in enumerate(moves)]
    for copy in copies:
        copy.start()
    return copies


def sight_moves(video_k, video_v, first, out):
    rows, cols = video_k.shape[0], pl.ds(first, out.shape[1])
    return [(video_k.at[:, cols], out.at[:rows]), (video_v.at[:, cols], out.at[rows:])]


def sound_moves(audio_k, audio_v, out):
    rows, width = audio_k.shape[0], out.shape[1]
    moves = []
    for src in (audio_k, audio_v):
        for half in range(2):
            at = len(moves) * rows
            moves.append((src.at[:, pl.ds(half * width, width)], out.at[at : at + rows]))
    return moves


def first_pack(n, me_ref, video_k, video_v, audio_k, audio_v, out_ref, over_ref, values_ref, sem):
    me = me_ref[0]
    half = values_ref.shape[1]
    at_end = (me == 0) | (me == n - 1)
    for role, sight, sound in ((at_end, out_ref, over_ref), (jnp.logical_not(at_end), over_ref, out_ref)):

        @pl.when(role)
        def _(sight=sight, sound=sound):
            moves = sight_moves(video_k, video_v, 0, sight) + sound_moves(audio_k, audio_v, sound)
            moves.append((video_v.at[:, pl.ds(0, half)], values_ref))
            for copy in move_all(moves, sem):
                copy.wait()


def second_pack(n, me_ref, count_ref, offset_ref, video_k, video_v, video_q, audio_q, *outs):
    sight1, sight2, asks0, asks1, values_ref, mask0_ref, mask1_ref, near_ref, sem = outs
    rows = video_q.shape[0]
    at = asks0.shape[1]
    moves = [(video_v.at[:, pl.ds(at, at)], values_ref)]
    for half, out in enumerate((asks0, asks1)):
        cols = pl.ds(half * at, at)
        moves += [(video_q.at[:, cols], out.at[:rows]), (audio_q.at[:, cols], out.at[rows:])]
    for out in (sight1, sight2):
        moves += sight_moves(video_k, video_v, at, out)
        at += out.shape[1]
    copies = move_all(moves, sem)
    tables(n, me_ref[0], count_ref, offset_ref, (mask0_ref, mask1_ref), near_ref)
    for copy in copies:
        copy.wait()


def tables(n, me, count_ref, offset_ref, mask_refs, near_ref):
    upper = me * 2 >= n
    inner, end = jnp.where(upper, 1, n - 2), jnp.where(upper, 0, n - 1)
    frames = (me, me ^ 1, inner, end)
    audio_rows = offset_ref.shape[1] // n
    video_rows = mask_refs[0].shape[1] // n
    pieces = [offset_ref[:, i * audio_rows : (i + 1) * audio_rows] for i in range(n)]
    offsets = jnp.concatenate([pick(pieces, frame) for frame in frames], axis=1)
    near = jnp.where(jnp.abs(offsets - me) <= SPAN, 0.0, MASKED)
    near_ref[:video_rows, :] = jnp.broadcast_to(near, (video_rows, n * audio_rows))
    near_ref[video_rows:, :] = jnp.zeros((audio_rows, n * audio_rows), jnp.float32)
    size = 2 * audio_rows
    corner = lax.broadcasted_iota(jnp.int32, (size, size), 0) == lax.broadcasted_iota(
        jnp.int32, (size, size), 1
    )
    asking = jnp.sum(jnp.where(corner, offsets[:, :size], 0), axis=1, keepdims=True)
    within = lax.broadcasted_iota(jnp.int32, (1, video_rows), 1)
    for i, frame in enumerate(frames):
        cols = slice(i * video_rows, (i + 1) * video_rows)
        live = jnp.where(within < count_ref[frame], 0.0, MASKED)
        reach = jnp.where(jnp.abs(asking - frame) <= SPAN, live, MASKED)
        for who, mask_ref in enumerate(mask_refs):
            mask_ref[:video_rows, cols] = jnp.broadcast_to(live, (video_rows, video_rows))
            mask_ref[video_rows:, cols] = reach[who * audio_rows : (who + 1) * audio_rows]


def sound_blocks(blocks, audio_rows, half, cols):
    key_rows = slice(half * audio_rows, (half + 1) * audio_rows)
    value_rows = slice((2 + half) * audio_rows, (3 + half) * audio_rows)
    keys = jnp.concatenate([b[key_rows, cols] for b in blocks], axis=0)
    values = jnp.concatenate([b[value_rows, cols] for b in blocks], axis=0)
    return keys, values


def audio_mate_kernel(n, me_ref, asks0, asks1, out, second, across, far, mate_ref):
    audio_rows, width = mate_ref.shape[0], out.shape[1]
    video_rows = asks0.shape[0] - audio_rows
    me = me_ref[0]

    @pl.when((me > 0) & (me < n - 1))
    def _():
        for half, asks in enumerate((asks0, asks1)):
            for at in range(0, width, HEAD_DIM):
                cols = slice(at, at + HEAD_DIM)
                to = slice(half * width + at, half * width + at + HEAD_DIM)
                keys, values = sound_blocks((out, second, across, far), audio_rows, half, cols)
                mate_ref[:, to] = blend(asks[video_rows:, cols], keys, values, None)


def audio_own_kernel(n, me_ref, near_ref, asks0, asks1, out, second, across, far, cross_ref, own_ref):
    audio_rows, width = own_ref.shape[0], out.shape[1]
    video_rows = cross_ref.shape[0]
    me = me_ref[0]

    @pl.when((me > 0) & (me < n - 1))
    def _():
        for half, asks in enumerate((asks0, asks1)):
            for at in range(0, width, HEAD_DIM):
                cols = slice(at, at + HEAD_DIM)
                to = slice(half * width + at, half * width + at + HEAD_DIM)
                keys, values = sound_blocks((out, second, across, far), audio_rows, half, cols)
                mixed = blend(asks[:, cols], keys, values, near_ref[...])
                cross_ref[:, to] = mixed[:video_rows]
                own_ref[:, to] = mixed[video_rows:]


def audio_end_kernel(n, me_ref, near_ref, asks0, asks1, over, first, part1, part2, far, cross_ref):
    video_rows, width = cross_ref.shape[0], over.shape[1]
    audio_rows = over.shape[0] // 4
    me = me_ref[0]

    @pl.when((me == 0) | (me == n - 1))
    def _():
        for half, asks in enumerate((asks0, asks1)):
            for at in range(0, width, HEAD_DIM):
                cols = slice(at, at + HEAD_DIM)
                to = slice(half * width + at, half * width + at + HEAD_DIM)
                shift = 0 if at < part1.shape[1] else part1.shape[1]
                part = (part2 if shift else part1).at[:, at - shift : at - shift + HEAD_DIM]
                blocks = [b.at[:, cols] for b in (over, first)] + [part, far.at[:, cols]]
                every = slice(0, HEAD_DIM)
                keys, values = sound_blocks(blocks, audio_rows, half, every)
                cross_ref[:, to] = blend(asks[:video_rows, cols], keys, values, near_ref[:video_rows])


def video_kernel(n, at, half, me_ref, mask_ref, asks, own, mate, keys2, values2, far, out_ref):
    video_rows = own.shape[0] // 2
    me = me_ref[0]

    @pl.when((me > 0) & (me < n - 1))
    def _():
        for head in range(own.shape[1] // HEAD_DIM):
            cols = slice(head * HEAD_DIM, (head + 1) * HEAD_DIM)
            all_cols = slice((at + head) * HEAD_DIM, (at + head + 1) * HEAD_DIM)
            half_cols = slice((at - half + head) * HEAD_DIM, (at - half + head + 1) * HEAD_DIM)
            top, low = slice(0, video_rows), slice(video_rows, 2 * video_rows)
            keys = jnp.concatenate(
                [own[top, cols], mate[top, cols], keys2[:, all_cols], far[top, cols]], axis=0
            )
            values = jnp.concatenate(
                [own[low, cols], mate[low, cols], values2[:, half_cols], far[low, cols]], axis=0
            )
            out_ref[:, cols] = blend(asks[:, half_cols], keys, values, mask_ref[...])


def place_pieces(parts, first, video_rows, video_self, audio_cross):
    moves, at = [], first
    for part in parts:
        cols = pl.ds(at, part.shape[1])
        moves.append((part.at[:video_rows], video_self.at[:, cols]))
        moves.append((part.at[video_rows:], audio_cross.at[:, cols]))
        at += part.shape[1]
    return moves


def place_kernel(n, me_ref, own_cross, end_cross, own0, own1, own2, back0, back1, back2, *outs):
    video_self, video_cross, audio_self, audio_cross, sem = outs
    at_end = (me_ref[0] == 0) | (me_ref[0] == n - 1)
    for role, cross, sound, parts in (
        (jnp.logical_not(at_end), own_cross, own0, (own1, own2)),
        (at_end, end_cross, back0, (back1, back2)),
    ):

        @pl.when(role)
        def _(cross=cross, sound=sound, parts=parts):
            moves = [(cross, video_cross), (sound, audio_self)]
            moves += place_pieces(parts, 0, cross.shape[0], video_self, audio_cross)
            for copy in move_all(moves, sem):
                copy.wait()


def place_last_kernel(n, first, me_ref, own, back, old_self, old_cross, video_self, audio_cross, sem):
    at_end = (me_ref[0] == 0) | (me_ref[0] == n - 1)
    for role, part in ((jnp.logical_not(at_end), own), (at_end, back)):

        @pl.when(role)
        def _(part=part):
            moves = place_pieces((part,), first, video_self.shape[0], video_self, audio_cross)
            for copy in move_all(moves, sem):
                copy.wait()


def cost(rows, keys, heads):
    scores = rows * keys * heads
    return pl.CostEstimate(flops=4 * scores * HEAD_DIM, bytes_accessed=rows * heads * 512, transcendentals=scores)


def chunks_of(heads):
    head = heads // 2
    return head, (head + 1) // 2, head // 2


def lined(video_q, video_k, video_v, audio_q, audio_k, audio_v, offsets, counts):
    n, cores = lax.axis_size("seq"), lax.axis_size("mp")
    me = lax.axis_index("seq")
    video_rows, audio_rows = video_q.shape[0], audio_q.shape[0]
    rows = video_rows + audio_rows
    width = video_q.shape[1]
    heads = width // HEAD_DIM
    chunks = chunks_of(heads)
    mate_pairs = [(i, i ^ 1) for i in range(n)]
    cross_pairs = []
    for i in range(n):
        for core in range(cores):
            inner = 0 < i < n - 1
            to = (n - 1 - i) * cores + core if inner else i * cores + cores - 1 - core
            cross_pairs.append((i * cores + core, to))

    def mate(block):
        return lax.ppermute(block, "seq", mate_pairs)

    def cross(block):
        return lax.ppermute(block, ("seq", "mp"), cross_pairs)

    def call(kernel, outs, spaces, *args, **more):
        return pl.pallas_call(
            kernel,
            out_shape=tuple(jax.ShapeDtypeStruct(shape, dtype) for shape, dtype in outs),
            in_specs=spaces,
            compiler_params=PARAMS,
            **more,
        )(*args)

    place = me.astype(jnp.int32).reshape(1)
    raw_keys = video_k
    video_q, video_k, video_v, audio_q, audio_k, audio_v = (
        pltpu.with_memory_space_constraint(block, pltpu.HBM)
        for block in (video_q, video_k, video_v, audio_q, audio_k, audio_v)
    )
    at_end = (me == 0) | (me == n - 1)
    lengths = [size * HEAD_DIM for size in chunks]
    half = lengths[0]
    first_out, first_over, values0 = call(
        functools.partial(first_pack, n),
        (((2 * video_rows, half), jnp.bfloat16),) * 2 + (((video_rows, half), jnp.bfloat16),),
        [SMEM] + [HBM] * 4,
        place,
        video_k,
        video_v,
        audio_k,
        audio_v,
        out_specs=(VMEM,) * 3,
        scratch_shapes=[pltpu.SemaphoreType.DMA((7,))],
    )
    outs = tuple(((2 * video_rows, length), jnp.bfloat16) for length in lengths[1:])
    outs += (((rows, half), jnp.bfloat16),) * 2
    outs += (((video_rows, half), jnp.bfloat16),)
    outs += (((rows, n * video_rows), jnp.float32),) * 2 + (((rows, n * audio_rows), jnp.float32),)
    *sights, asks0, asks1, values1, mask0, mask1, near = call(
        functools.partial(second_pack, n),
        outs,
        [SMEM, SMEM, VMEM] + [HBM] * 4,
        place,
        counts,
        offsets.reshape(1, -1),
        video_k,
        video_v,
        video_q,
        audio_q,
        out_specs=(VMEM,) * len(outs),
        scratch_shapes=[pltpu.SemaphoreType.DMA((9,))],
    )
    asks = [asks0, asks1]
    sights = [first_over] + sights

    keys_across = cross(raw_keys)
    values_across = [cross(values0), cross(values1)]
    sight_mate = [mate(first_out)]
    sound_across = cross(first_out)
    second_mate = mate(first_over)
    sound_far = cross(second_mate)
    at = 0
    for i in (1, 2):
        part = sound_across[:, at : at + lengths[i]]
        sight_mate.append(mate(jnp.where(at_end, sights[i], part)))
        at += lengths[i]
    sight_far = [cross(sight_mate[i]) for i in range(3)]
    asks_mate = [mate(asks[i]) for i in range(2)]

    def look(i, queries, mask):
        at, size = sum(chunks[:i]), chunks[i]
        half = min(i, 1)
        return call(
            functools.partial(video_kernel, n, at, half * chunks[0]),
            (((rows, size * HEAD_DIM), jnp.bfloat16),),
            [SMEM] + [VMEM] * 7,
            place,
            mask,
            queries[half],
            sights[i],
            sight_mate[i],
            keys_across,
            values_across[half],
            sight_far[i],
            out_specs=(VMEM,),
            cost_estimate=cost(rows, n * video_rows, size),
        )[0]

    back = [mate(look(i, asks_mate, mask1)) for i in range(3)]
    mine = [look(i, asks, mask0) for i in range(3)]
    theirs = call(
        functools.partial(audio_mate_kernel, n),
        (((audio_rows, width), jnp.bfloat16),),
        [SMEM] + [VMEM] * 6,
        place,
        *asks_mate,
        first_out,
        second_mate,
        sound_across,
        sound_far,
        out_specs=(VMEM,),
        cost_estimate=cost(audio_rows, n * audio_rows, heads),
    )[0]
    own_cross, own = call(
        functools.partial(audio_own_kernel, n),
        (((video_rows, width), jnp.bfloat16), ((audio_rows, width), jnp.bfloat16)),
        [SMEM] + [VMEM] * 7,
        place,
        near,
        *asks,
        first_out,
        second_mate,
        sound_across,
        sound_far,
        out_specs=(VMEM,) * 2,
        cost_estimate=cost(rows, n * audio_rows, heads),
    )
    end_cross = call(
        functools.partial(audio_end_kernel, n),
        (((video_rows, width), jnp.bfloat16),),
        [SMEM] + [VMEM] * 8,
        place,
        near,
        *asks,
        first_over,
        sight_mate[0],
        sight_mate[1],
        sight_mate[2],
        sound_far,
        out_specs=(VMEM,),
        cost_estimate=cost(rows, n * audio_rows, heads),
    )[0]
    back_sound = mate(theirs)
    video_shape = ((video_rows, width), jnp.bfloat16)
    audio_shape = ((audio_rows, width), jnp.bfloat16)
    video_self, video_cross, audio_self, audio_cross = call(
        functools.partial(place_kernel, n),
        (video_shape, video_shape, audio_shape, audio_shape),
        [SMEM] + [VMEM] * 8,
        place,
        own_cross,
        end_cross,
        own,
        *mine[:2],
        back_sound,
        *back[:2],
        out_specs=(HBM,) * 4,
        scratch_shapes=[pltpu.SemaphoreType.DMA((6,))],
    )
    video_self, audio_cross = call(
        functools.partial(place_last_kernel, n, width - lengths[2]),
        (video_shape, audio_shape),
        [SMEM] + [VMEM] * 2 + [HBM] * 2,
        place,
        mine[2],
        back[2],
        video_self,
        audio_cross,
        out_specs=(HBM,) * 2,
        scratch_shapes=[pltpu.SemaphoreType.DMA((2,))],
        input_output_aliases={3: 0, 4: 1},
    )
    return video_self, video_cross, audio_self, audio_cross


def solution(mesh):
    split = P(("groups", "seq"), ("tower", "mp"))
    placed = (split,) * 6 + (P("groups"), P("groups"))
    sizes = mesh.shape
    line = sizes["seq"] == 4 and sizes["mp"] == 2

    def whole(*arrays):
        heads = arrays[0].shape[1] // HEAD_DIM // (sizes["tower"] * sizes["mp"])
        paired = heads % 2 == 0 and heads > 3 and arrays[0].shape[0] == 2 * arrays[3].shape[0]
        body = lined if line and paired else gathered
        return jax.shard_map(
            body, mesh=mesh, in_specs=placed, out_specs=(split,) * 4, check_vma=False
        )(*arrays)

    return whole
```

```python
import functools

import jax
import jax.numpy as jnp
from jax import lax
from jax.experimental import pallas as pl
from jax.experimental.pallas import tpu as pltpu
from jax.sharding import PartitionSpec as P


HEAD_DIM = 128
SPAN = 1
STEP = 128
MASKED = -1e30
LOG2E = 1.4426950408889634
VMEM = pl.BlockSpec(memory_space=pltpu.VMEM)
SMEM = pl.BlockSpec(memory_space=pltpu.SMEM)
HBM = pl.BlockSpec(memory_space=pltpu.HBM)
PARAMS = pltpu.CompilerParams(vmem_limit_bytes=16 << 20)


def attend(queries, key_rows, value_rows, allowed):
    scores = jnp.einsum(
        "qhe,khe->hqk", queries, key_rows, preferred_element_type=jnp.float32
    ) * HEAD_DIM ** (-0.5)
    scores = jnp.where(allowed[None], scores, MASKED)
    peak = jnp.max(scores, axis=2)
    weights = jnp.where(allowed[None], jnp.exp(scores - peak[:, :, None]), 0.0)
    total = jnp.sum(weights, axis=2)
    blended = jnp.einsum(
        "hqk,khe->hqe", weights.astype(jnp.bfloat16), value_rows, preferred_element_type=jnp.float32
    )
    blended = blended / total[:, :, None]
    return jnp.transpose(blended, (1, 0, 2)).reshape(blended.shape[1], -1).astype(jnp.bfloat16)


def gathered(video_q, video_k, video_v, audio_q, audio_k, audio_v, offsets, counts):
    my_frame = lax.axis_index("seq")
    video_rows, audio_rows = video_q.shape[0], audio_q.shape[0]

    def heads(rows):
        return rows.reshape(rows.shape[0], -1, HEAD_DIM)

    def everywhere(rows):
        return heads(lax.all_gather(rows, "seq", axis=0, tiled=True))

    my_offsets = lax.dynamic_slice_in_dim(offsets, my_frame * audio_rows, audio_rows)
    keys, values = everywhere(video_k), everywhere(video_v)
    audio_keys, audio_values = everywhere(audio_k), everywhere(audio_v)
    positions = jnp.arange(keys.shape[0], dtype=jnp.int32)
    source = positions // video_rows
    is_live = positions % video_rows < jnp.repeat(counts, video_rows)
    video_self = attend(heads(video_q), keys, values, is_live[None, :])
    in_reach = (jnp.abs(my_offsets[:, None] - source[None, :]) <= SPAN) & is_live[None, :]
    audio_cross = attend(heads(audio_q), keys, values, in_reach)
    every = jnp.ones((1, audio_keys.shape[0]), jnp.bool_)
    audio_self = attend(heads(audio_q), audio_keys, audio_values, every)
    in_reach = jnp.abs(offsets - my_frame) <= SPAN
    video_cross = attend(heads(video_q), audio_keys, audio_values, in_reach[None, :])
    return (video_self, video_cross, audio_self, audio_cross)


def gather_up(queries, keys, values, bias):
    scores = lax.dot_general(
        queries, keys, (((1,), (1,)), ((), ())), preferred_element_type=jnp.float32
    )
    if bias is not None:
        scores = scores + bias
    peak = jnp.max(scores, axis=1, keepdims=True)
    weights = jnp.exp2((scores - peak) * (HEAD_DIM ** (-0.5) * LOG2E))
    total = jnp.sum(weights, axis=1, keepdims=True)
    weights = weights.astype(jnp.bfloat16)
    mixed = 0.0
    for at in range(0, keys.shape[0], STEP):
        mixed += jnp.dot(
            weights[:, at : at + STEP], values[at : at + STEP], preferred_element_type=jnp.float32
        )
    return peak, total, mixed


def blend(queries, keys, values, bias):
    _, total, mixed = gather_up(queries, keys, values, bias)
    return (mixed * (1.0 / total)).astype(jnp.bfloat16)


def pick(pieces, at):
    chosen = pieces[0]
    for i in range(1, len(pieces)):
        chosen = jnp.where(at == i, pieces[i], chosen)
    return chosen


def move_all(moves, sem):
    copies = [pltpu.make_async_copy(src, dst, sem.at[i]) for i, (src, dst) in enumerate(moves)]
    for copy in copies:
        copy.start()
    return copies


def sight_moves(video_k, video_v, first, out):
    rows, cols = video_k.shape[0], pl.ds(first, out.shape[1])
    return [(video_k.at[:, cols], out.at[:rows]), (video_v.at[:, cols], out.at[rows:])]


def sound_moves(audio_k, audio_v, out):
    rows, width = audio_k.shape[0], out.shape[1]
    moves = []
    for src in (audio_k, audio_v):
        for half in range(2):
            at = len(moves) * rows
            moves.append((src.at[:, pl.ds(half * width, width)], out.at[at : at + rows]))
    return moves


def first_pack(n, me_ref, video_k, video_v, audio_k, audio_v, out_ref, over_ref, values_ref, sem):
    me = me_ref[0]
    half = values_ref.shape[1]
    at_end = (me == 0) | (me == n - 1)
    for role, sight, sound in ((at_end, out_ref, over_ref), (jnp.logical_not(at_end), over_ref, out_ref)):

        @pl.when(role)
        def _(sight=sight, sound=sound):
            moves = sight_moves(video_k, video_v, 0, sight) + sound_moves(audio_k, audio_v, sound)
            moves.append((video_v.at[:, pl.ds(0, half)], values_ref))
            for copy in move_all(moves, sem):
                copy.wait()


def second_pack(n, me_ref, count_ref, offset_ref, video_k, video_v, video_q, audio_q, *outs):
    sight1, sight2, asks0, asks1, values_ref, mask0_ref, mask1_ref, near_ref, sem = outs
    half = asks0.shape[1]
    low, high = pl.ds(0, half), pl.ds(half, half)
    rows, more = video_q.shape[0], audio_q.shape[0]
    moves = [
        (video_q.at[:, low], asks0.at[:rows]),
        (audio_q.at[:, low], asks0.at[rows : rows + more]),
        (audio_q.at[:, high], asks0.at[rows + more :]),
        (video_q.at[:, high], asks1),
        (video_v.at[:, high], values_ref),
    ]
    at = half
    for out in (sight1, sight2):
        moves += sight_moves(video_k, video_v, at, out)
        at += out.shape[1]
    copies = move_all(moves, sem)
    tables(n, me_ref[0], count_ref, offset_ref, (mask0_ref, mask1_ref), near_ref)
    for copy in copies:
        copy.wait()


def tables(n, me, count_ref, offset_ref, mask_refs, near_ref):
    upper = me * 2 >= n
    inner, end = jnp.where(upper, 1, n - 2), jnp.where(upper, 0, n - 1)
    frames = (me, me ^ 1, inner, end)
    audio_rows = offset_ref.shape[1] // n
    video_rows = mask_refs[0].shape[1] // n
    pieces = [offset_ref[:, i * audio_rows : (i + 1) * audio_rows] for i in range(n)]
    offsets = jnp.concatenate([pick(pieces, frame) for frame in frames], axis=1)
    near = jnp.where(jnp.abs(offsets - me) <= SPAN, 0.0, MASKED)
    near_ref[:video_rows, :] = jnp.broadcast_to(near, (video_rows, n * audio_rows))
    near_ref[video_rows:, :] = jnp.zeros((audio_rows, n * audio_rows), jnp.float32)
    size = 2 * audio_rows
    corner = lax.broadcasted_iota(jnp.int32, (size, size), 0) == lax.broadcasted_iota(
        jnp.int32, (size, size), 1
    )
    asking = jnp.sum(jnp.where(corner, offsets[:, :size], 0), axis=1, keepdims=True)
    within = lax.broadcasted_iota(jnp.int32, (1, video_rows), 1)
    for i, frame in enumerate(frames):
        cols = slice(i * video_rows, (i + 1) * video_rows)
        live = jnp.where(within < count_ref[frame], 0.0, MASKED)
        reach = jnp.where(jnp.abs(asking - frame) <= SPAN, live, MASKED)
        for who, mask_ref in enumerate(mask_refs):
            mask_ref[:video_rows, cols] = jnp.broadcast_to(live, (video_rows, video_rows))
            mask_ref[video_rows:, cols] = reach[who * audio_rows : (who + 1) * audio_rows]


def sound_blocks(blocks, audio_rows, half, cols):
    key_rows = slice(half * audio_rows, (half + 1) * audio_rows)
    value_rows = slice((2 + half) * audio_rows, (3 + half) * audio_rows)
    keys = jnp.concatenate([b[key_rows, cols] for b in blocks], axis=0)
    values = jnp.concatenate([b[value_rows, cols] for b in blocks], axis=0)
    return keys, values


def queries_of(half, asks0, asks1, video_rows, audio_rows, cols):
    rows = video_rows + audio_rows
    if half == 0:
        return asks0[:rows, cols]
    return jnp.concatenate([asks1[:, cols], asks0[rows:, cols]], axis=0)


def audio_mate_kernel(n, me_ref, asks0, out, second, across, far, mate_ref):
    audio_rows, width = mate_ref.shape[0], out.shape[1]
    me = me_ref[0]

    @pl.when((me > 0) & (me < n - 1))
    def _():
        for half in range(2):
            first = asks0.shape[0] - (2 - half) * audio_rows
            for at in range(0, width, HEAD_DIM):
                cols = slice(at, at + HEAD_DIM)
                to = slice(half * width + at, half * width + at + HEAD_DIM)
                keys, values = sound_blocks((out, second, across, far), audio_rows, half, cols)
                mate_ref[:, to] = blend(asks0[first : first + audio_rows, cols], keys, values, None)


def audio_own_kernel(n, me_ref, near_ref, asks0, asks1, out, second, across, far, cross_ref, own_ref):
    audio_rows, width = own_ref.shape[0], out.shape[1]
    video_rows = cross_ref.shape[0]
    me = me_ref[0]

    @pl.when((me > 0) & (me < n - 1))
    def _():
        for half in range(2):
            for at in range(0, width, HEAD_DIM):
                cols = slice(at, at + HEAD_DIM)
                to = slice(half * width + at, half * width + at + HEAD_DIM)
                keys, values = sound_blocks((out, second, across, far), audio_rows, half, cols)
                queries = queries_of(half, asks0, asks1, video_rows, audio_rows, cols)
                mixed = blend(queries, keys, values, near_ref[...])
                cross_ref[:, to] = mixed[:video_rows]
                own_ref[:, to] = mixed[video_rows:]


def audio_end_kernel(n, me_ref, near_ref, asks0, asks1, over, first, part1, part2, far, cross_ref):
    video_rows, width = cross_ref.shape[0], over.shape[1]
    audio_rows = over.shape[0] // 4
    me = me_ref[0]

    @pl.when((me == 0) | (me == n - 1))
    def _():
        for half, asks in enumerate((asks0, asks1)):
            for at in range(0, width, HEAD_DIM):
                cols = slice(at, at + HEAD_DIM)
                to = slice(half * width + at, half * width + at + HEAD_DIM)
                shift = 0 if at < part1.shape[1] else part1.shape[1]
                part = (part2 if shift else part1).at[:, at - shift : at - shift + HEAD_DIM]
                blocks = [b.at[:, cols] for b in (over, first)] + [part, far.at[:, cols]]
                every = slice(0, HEAD_DIM)
                keys, values = sound_blocks(blocks, audio_rows, half, every)
                cross_ref[:, to] = blend(asks[:video_rows, cols], keys, values, near_ref[:video_rows])


def video_kernel(n, at, half, offset, me_ref, mask_ref, *refs):
    *asks, own, mate, keys2, values2, far, out_ref = refs
    video_rows = own.shape[0] // 2
    audio_rows = out_ref.shape[0] - video_rows
    me = me_ref[0]

    @pl.when((me > 0) & (me < n - 1))
    def _():
        for head in range(far.shape[1] // HEAD_DIM):
            cols = slice(head * HEAD_DIM, (head + 1) * HEAD_DIM)
            near_cols = slice((offset + head) * HEAD_DIM, (offset + head + 1) * HEAD_DIM)
            all_cols = slice((at + head) * HEAD_DIM, (at + head + 1) * HEAD_DIM)
            half_cols = slice((at - half + head) * HEAD_DIM, (at - half + head + 1) * HEAD_DIM)
            top, low = slice(0, video_rows), slice(video_rows, 2 * video_rows)
            keys = jnp.concatenate(
                [own[top, near_cols], mate[top, near_cols], keys2[:, all_cols], far[top, cols]], axis=0
            )
            values = jnp.concatenate(
                [own[low, near_cols], mate[low, near_cols], values2[:, half_cols], far[low, cols]],
                axis=0,
            )
            queries = queries_of(len(asks) - 1, asks[0], asks[-1], video_rows, audio_rows, half_cols)
            out_ref[:, cols] = blend(queries, keys, values, mask_ref[...])


def early_kernel(n, at, half, me_ref, mask_ref, asks0, asks1, own, mate, keys2, values2, *outs):
    peak_ref, total_ref, mixed_ref = outs
    video_rows = own.shape[0] // 2
    audio_rows = peak_ref.shape[0] - video_rows
    me = me_ref[0]

    @pl.when((me > 0) & (me < n - 1))
    def _():
        for head in range(own.shape[1] // HEAD_DIM):
            cols = slice(head * HEAD_DIM, (head + 1) * HEAD_DIM)
            all_cols = slice((at + head) * HEAD_DIM, (at + head + 1) * HEAD_DIM)
            half_cols = slice((at - half + head) * HEAD_DIM, (at - half + head + 1) * HEAD_DIM)
            top, low = slice(0, video_rows), slice(video_rows, 2 * video_rows)
            keys = jnp.concatenate([own[top, cols], mate[top, cols], keys2[:, all_cols]], axis=0)
            values = jnp.concatenate([own[low, cols], mate[low, cols], values2[:, half_cols]], axis=0)
            queries = queries_of(1, asks0, asks1, video_rows, audio_rows, half_cols)
            peak, total, mixed = gather_up(queries, keys, values, mask_ref[:, : keys.shape[0]])
            peak_ref[:, cols] = jnp.broadcast_to(peak, mixed.shape)
            total_ref[:, cols] = jnp.broadcast_to(total, mixed.shape)
            mixed_ref[:, cols] = mixed


def late_kernel(n, at, half, me_ref, mask_ref, asks0, asks1, far, peak_ref, total_ref, mixed_ref, out_ref):
    video_rows = far.shape[0] // 2
    audio_rows = out_ref.shape[0] - video_rows
    me = me_ref[0]

    @pl.when((me > 0) & (me < n - 1))
    def _():
        for head in range(far.shape[1] // HEAD_DIM):
            cols = slice(head * HEAD_DIM, (head + 1) * HEAD_DIM)
            half_cols = slice((at - half + head) * HEAD_DIM, (at - half + head + 1) * HEAD_DIM)
            queries = queries_of(1, asks0, asks1, video_rows, audio_rows, half_cols)
            scores = lax.dot_general(
                queries,
                far[:video_rows, cols],
                (((1,), (1,)), ((), ())),
                preferred_element_type=jnp.float32,
            )
            scores = scores + mask_ref[:, mask_ref.shape[1] - video_rows :]
            before = peak_ref[:, cols]
            peak = jnp.maximum(before, jnp.max(scores, axis=1, keepdims=True))
            kept = jnp.exp2((before - peak) * (HEAD_DIM ** (-0.5) * LOG2E))
            weights = jnp.exp2((scores - peak[:, :1]) * (HEAD_DIM ** (-0.5) * LOG2E))
            total = total_ref[:, cols] * kept + jnp.sum(weights, axis=1, keepdims=True)
            mixed = jnp.dot(
                weights.astype(jnp.bfloat16),
                far[video_rows:, cols],
                preferred_element_type=jnp.float32,
            )
            out_ref[:, cols] = ((mixed_ref[:, cols] * kept + mixed) / total).astype(jnp.bfloat16)


def place_pieces(parts, first, video_rows, video_self, audio_cross):
    moves, at = [], first
    for part in parts:
        cols = pl.ds(at, part.shape[1])
        moves.append((part.at[:video_rows], video_self.at[:, cols]))
        moves.append((part.at[video_rows:], audio_cross.at[:, cols]))
        at += part.shape[1]
    return moves


def place_kernel(n, me_ref, own_cross, end_cross, *refs):
    count = (len(refs) - 5) // 2
    own, back = refs[:count], refs[count : 2 * count]
    video_self, video_cross, audio_self, audio_cross, sem = refs[2 * count :]
    at_end = (me_ref[0] == 0) | (me_ref[0] == n - 1)
    for role, cross, parts in (
        (jnp.logical_not(at_end), own_cross, own),
        (at_end, end_cross, back),
    ):

        @pl.when(role)
        def _(cross=cross, parts=parts):
            moves = [(cross, video_cross), (parts[0], audio_self)]
            moves += place_pieces(parts[1:], 0, cross.shape[0], video_self, audio_cross)
            for copy in move_all(moves, sem):
                copy.wait()


def place_last_kernel(n, first, me_ref, own, back, old_self, old_cross, video_self, audio_cross, sem):
    at_end = (me_ref[0] == 0) | (me_ref[0] == n - 1)
    for role, part in ((jnp.logical_not(at_end), own), (at_end, back)):

        @pl.when(role)
        def _(part=part):
            moves = place_pieces((part,), first, video_self.shape[0], video_self, audio_cross)
            for copy in move_all(moves, sem):
                copy.wait()


def cost(rows, keys, heads):
    scores = rows * keys * heads
    return pl.CostEstimate(flops=4 * scores * HEAD_DIM, bytes_accessed=rows * heads * 512, transcendentals=scores)


def chunks_of(heads):
    head = heads // 2
    return head, (head + 1) // 2, head // 2


def lined(video_q, video_k, video_v, audio_q, audio_k, audio_v, offsets, counts):
    n, cores = lax.axis_size("seq"), lax.axis_size("mp")
    me = lax.axis_index("seq")
    video_rows, audio_rows = video_q.shape[0], audio_q.shape[0]
    rows = video_rows + audio_rows
    width = video_q.shape[1]
    heads = width // HEAD_DIM
    chunks = chunks_of(heads)
    mate_pairs = [(i, i ^ 1) for i in range(n)]
    cross_pairs = []
    for i in range(n):
        for core in range(cores):
            inner = 0 < i < n - 1
            to = (n - 1 - i) * cores + core if inner else i * cores + cores - 1 - core
            cross_pairs.append((i * cores + core, to))

    def mate(block):
        return lax.ppermute(block, "seq", mate_pairs)

    def cross(block):
        return lax.ppermute(block, ("seq", "mp"), cross_pairs)

    def call(kernel, outs, spaces, *args, **more):
        return pl.pallas_call(
            kernel,
            out_shape=tuple(jax.ShapeDtypeStruct(shape, dtype) for shape, dtype in outs),
            in_specs=spaces,
            compiler_params=PARAMS,
            **more,
        )(*args)

    place = me.astype(jnp.int32).reshape(1)
    raw_keys = video_k
    video_q, video_k, video_v, audio_q, audio_k, audio_v = (
        pltpu.with_memory_space_constraint(block, pltpu.HBM)
        for block in (video_q, video_k, video_v, audio_q, audio_k, audio_v)
    )
    at_end = (me == 0) | (me == n - 1)
    lengths = [size * HEAD_DIM for size in chunks]
    half = lengths[0]
    first_out, first_over, values0 = call(
        functools.partial(first_pack, n),
        (((2 * video_rows, half), jnp.bfloat16),) * 2 + (((video_rows, half), jnp.bfloat16),),
        [SMEM] + [HBM] * 4,
        place,
        video_k,
        video_v,
        audio_k,
        audio_v,
        out_specs=(VMEM,) * 3,
        scratch_shapes=[pltpu.SemaphoreType.DMA((7,))],
    )
    outs = tuple(((2 * video_rows, length), jnp.bfloat16) for length in lengths[1:])
    outs += (((rows + audio_rows, half), jnp.bfloat16), ((video_rows, half), jnp.bfloat16))
    outs += (((video_rows, half), jnp.bfloat16),)
    outs += (((rows, n * video_rows), jnp.float32),) * 2 + (((rows, n * audio_rows), jnp.float32),)
    *sights, asks0, asks1, values1, mask0, mask1, near = call(
        functools.partial(second_pack, n),
        outs,
        [SMEM, SMEM, VMEM] + [HBM] * 4,
        place,
        counts,
        offsets.reshape(1, -1),
        video_k,
        video_v,
        video_q,
        audio_q,
        out_specs=(VMEM,) * len(outs),
        scratch_shapes=[pltpu.SemaphoreType.DMA((9,))],
    )
    asks = [asks0, asks1]
    sights = [first_over] + sights

    keys_across = cross(raw_keys)
    values_across = [cross(values0), cross(values1)]
    sight_mate = [mate(first_out)]
    sound_across = cross(first_out)
    second_mate = mate(first_over)
    sound_far = cross(second_mate)
    at = 0
    for i in (1, 2):
        part = sound_across[:, at : at + lengths[i]]
        sight_mate.append(mate(jnp.where(at_end, sights[i], part)))
        at += lengths[i]
    pieces = [(0, chunks[0], 0, 0)]
    sight_far = [cross(sight_mate[0])]
    for source in (1, 2):
        pieces.append((sum(chunks[:source]), chunks[source], source, 0))
        sight_far.append(cross(sight_mate[source]))
    last = len(pieces) - 1
    asks_mate = [mate(asks[i]) for i in range(2)]

    def look(i, queries, mask):
        at, size, source, offset = pieces[i]
        half = min(source, 1)
        return call(
            functools.partial(video_kernel, n, at, half * chunks[0], offset),
            (((rows, size * HEAD_DIM), jnp.bfloat16),),
            [SMEM] + [VMEM] * (7 + half),
            place,
            mask,
            *queries[: 1 + half],
            sights[source],
            sight_mate[source],
            keys_across,
            values_across[half],
            sight_far[i],
            out_specs=(VMEM,),
            cost_estimate=cost(rows, n * video_rows, size),
        )[0]

    at, size, source, _ = pieces[1]
    early = call(
        functools.partial(early_kernel, n, at, chunks[0]),
        (((rows, size * HEAD_DIM), jnp.float32),) * 3,
        [SMEM] + [VMEM] * 7,
        place,
        mask1,
        *asks_mate,
        sights[source],
        sight_mate[source],
        keys_across,
        values_across[1],
        out_specs=(VMEM,) * 3,
        cost_estimate=cost(rows, (n - 1) * video_rows, size),
    )
    late = call(
        functools.partial(late_kernel, n, at, chunks[0]),
        (((rows, size * HEAD_DIM), jnp.bfloat16),),
        [SMEM] + [VMEM] * 7,
        place,
        mask1,
        *asks_mate,
        sight_far[1],
        *early,
        out_specs=(VMEM,),
        cost_estimate=cost(rows, video_rows, size),
    )[0]
    results = [look(0, asks_mate, mask1), late, look(2, asks_mate, mask1)]
    back = [mate(result) for result in results]
    mine = [look(i, asks, mask0) for i in range(last + 1)]
    theirs = call(
        functools.partial(audio_mate_kernel, n),
        (((audio_rows, width), jnp.bfloat16),),
        [SMEM] + [VMEM] * 5,
        place,
        asks_mate[0],
        first_out,
        second_mate,
        sound_across,
        sound_far,
        out_specs=(VMEM,),
        cost_estimate=cost(audio_rows, n * audio_rows, heads),
    )[0]
    own_cross, own = call(
        functools.partial(audio_own_kernel, n),
        (((video_rows, width), jnp.bfloat16), ((audio_rows, width), jnp.bfloat16)),
        [SMEM] + [VMEM] * 7,
        place,
        near,
        *asks,
        first_out,
        second_mate,
        sound_across,
        sound_far,
        out_specs=(VMEM,) * 2,
        cost_estimate=cost(rows, n * audio_rows, heads),
    )
    end_cross = call(
        functools.partial(audio_end_kernel, n),
        (((video_rows, width), jnp.bfloat16),),
        [SMEM] + [VMEM] * 8,
        place,
        near,
        *asks,
        first_over,
        sight_mate[0],
        sight_mate[1],
        sight_mate[2],
        sound_far,
        out_specs=(VMEM,),
        cost_estimate=cost(rows, n * audio_rows, heads),
    )[0]
    back_sound = mate(theirs)
    video_shape = ((video_rows, width), jnp.bfloat16)
    audio_shape = ((audio_rows, width), jnp.bfloat16)
    video_self, video_cross, audio_self, audio_cross = call(
        functools.partial(place_kernel, n),
        (video_shape, video_shape, audio_shape, audio_shape),
        [SMEM] + [VMEM] * (4 + 2 * last),
        place,
        own_cross,
        end_cross,
        own,
        *mine[:last],
        back_sound,
        *back[:last],
        out_specs=(HBM,) * 4,
        scratch_shapes=[pltpu.SemaphoreType.DMA((2 + 2 * last,))],
    )
    video_self, audio_cross = call(
        functools.partial(place_last_kernel, n, width - chunks[2] * HEAD_DIM),
        (video_shape, audio_shape),
        [SMEM] + [VMEM] * 2 + [HBM] * 2,
        place,
        mine[last],
        back[last],
        video_self,
        audio_cross,
        out_specs=(HBM,) * 2,
        scratch_shapes=[pltpu.SemaphoreType.DMA((2,))],
        input_output_aliases={3: 0, 4: 1},
    )
    return video_self, video_cross, audio_self, audio_cross


def solution(mesh):
    split = P(("groups", "seq"), ("tower", "mp"))
    placed = (split,) * 6 + (P("groups"), P("groups"))
    sizes = mesh.shape
    line = sizes["seq"] == 4 and sizes["mp"] == 2

    def whole(*arrays):
        heads = arrays[0].shape[1] // HEAD_DIM // (sizes["tower"] * sizes["mp"])
        paired = heads % 2 == 0 and heads > 3 and arrays[0].shape[0] == 2 * arrays[3].shape[0]
        body = lined if line and paired else gathered
        return jax.shard_map(
            body, mesh=mesh, in_specs=placed, out_specs=(split,) * 4, check_vma=False
        )(*arrays)

    return whole
```

```python
import functools

import jax
import jax.numpy as jnp
from jax import lax
from jax.experimental import pallas as pl
from jax.experimental.pallas import tpu as pltpu
from jax.sharding import PartitionSpec as P


HEAD_DIM = 128
SPAN = 1
STEP = 128
MASKED = -1e30
LOG2E = 1.4426950408889634
VMEM = pl.BlockSpec(memory_space=pltpu.VMEM)
SMEM = pl.BlockSpec(memory_space=pltpu.SMEM)
HBM = pl.BlockSpec(memory_space=pltpu.HBM)
PARAMS = pltpu.CompilerParams(vmem_limit_bytes=16 << 20)


def attend(queries, key_rows, value_rows, allowed):
    scores = jnp.einsum(
        "qhe,khe->hqk", queries, key_rows, preferred_element_type=jnp.float32
    ) * HEAD_DIM ** (-0.5)
    scores = jnp.where(allowed[None], scores, MASKED)
    peak = jnp.max(scores, axis=2)
    weights = jnp.where(allowed[None], jnp.exp(scores - peak[:, :, None]), 0.0)
    total = jnp.sum(weights, axis=2)
    blended = jnp.einsum(
        "hqk,khe->hqe", weights.astype(jnp.bfloat16), value_rows, preferred_element_type=jnp.float32
    )
    blended = blended / total[:, :, None]
    return jnp.transpose(blended, (1, 0, 2)).reshape(blended.shape[1], -1).astype(jnp.bfloat16)


def gathered(video_q, video_k, video_v, audio_q, audio_k, audio_v, offsets, counts):
    my_frame = lax.axis_index("seq")
    video_rows, audio_rows = video_q.shape[0], audio_q.shape[0]

    def heads(rows):
        return rows.reshape(rows.shape[0], -1, HEAD_DIM)

    def everywhere(rows):
        return heads(lax.all_gather(rows, "seq", axis=0, tiled=True))

    my_offsets = lax.dynamic_slice_in_dim(offsets, my_frame * audio_rows, audio_rows)
    keys, values = everywhere(video_k), everywhere(video_v)
    audio_keys, audio_values = everywhere(audio_k), everywhere(audio_v)
    positions = jnp.arange(keys.shape[0], dtype=jnp.int32)
    source = positions // video_rows
    is_live = positions % video_rows < jnp.repeat(counts, video_rows)
    video_self = attend(heads(video_q), keys, values, is_live[None, :])
    in_reach = (jnp.abs(my_offsets[:, None] - source[None, :]) <= SPAN) & is_live[None, :]
    audio_cross = attend(heads(audio_q), keys, values, in_reach)
    every = jnp.ones((1, audio_keys.shape[0]), jnp.bool_)
    audio_self = attend(heads(audio_q), audio_keys, audio_values, every)
    in_reach = jnp.abs(offsets - my_frame) <= SPAN
    video_cross = attend(heads(video_q), audio_keys, audio_values, in_reach[None, :])
    return (video_self, video_cross, audio_self, audio_cross)


def blend(queries, keys, values, bias):
    scores = lax.dot_general(
        queries, keys, (((1,), (1,)), ((), ())), preferred_element_type=jnp.float32
    )
    if bias is not None:
        scores = scores + bias
    peak = jnp.max(scores, axis=1, keepdims=True)
    weights = jnp.exp2((scores - peak) * (HEAD_DIM ** (-0.5) * LOG2E))
    total = jnp.sum(weights, axis=1, keepdims=True)
    weights = weights.astype(jnp.bfloat16)
    mixed = 0.0
    for at in range(0, keys.shape[0], STEP):
        mixed += jnp.dot(
            weights[:, at : at + STEP], values[at : at + STEP], preferred_element_type=jnp.float32
        )
    return (mixed * (1.0 / total)).astype(jnp.bfloat16)


def pick(pieces, at):
    chosen = pieces[0]
    for i in range(1, len(pieces)):
        chosen = jnp.where(at == i, pieces[i], chosen)
    return chosen


def move_all(moves, sem):
    copies = [pltpu.make_async_copy(src, dst, sem.at[i]) for i, (src, dst) in enumerate(moves)]
    for copy in copies:
        copy.start()
    return copies


def sight_moves(video_k, video_v, first, out):
    rows, cols = video_k.shape[0], pl.ds(first, out.shape[1])
    return [(video_k.at[:, cols], out.at[:rows]), (video_v.at[:, cols], out.at[rows:])]


def sound_moves(audio_k, audio_v, out):
    rows, width = audio_k.shape[0], out.shape[1]
    moves = []
    for src in (audio_k, audio_v):
        for half in range(2):
            at = len(moves) * rows
            moves.append((src.at[:, pl.ds(half * width, width)], out.at[at : at + rows]))
    return moves


def first_pack(n, me_ref, video_k, video_v, audio_k, audio_v, out_ref, over_ref, values_ref, sem):
    me = me_ref[0]
    half = values_ref.shape[1]
    at_end = (me == 0) | (me == n - 1)
    for role, sight, sound in ((at_end, out_ref, over_ref), (jnp.logical_not(at_end), over_ref, out_ref)):

        @pl.when(role)
        def _(sight=sight, sound=sound):
            moves = sight_moves(video_k, video_v, 0, sight) + sound_moves(audio_k, audio_v, sound)
            moves.append((video_v.at[:, pl.ds(0, half)], values_ref))
            for copy in move_all(moves, sem):
                copy.wait()


def second_pack(n, me_ref, count_ref, offset_ref, video_k, video_v, video_q, audio_q, *outs):
    sight1, sight2, asks0, asks1, values_ref, mask0_ref, mask1_ref, near_ref, sem = outs
    half = asks0.shape[1]
    low, high = pl.ds(0, half), pl.ds(half, half)
    rows, more = video_q.shape[0], audio_q.shape[0]
    moves = [
        (video_q.at[:, low], asks0.at[:rows]),
        (audio_q.at[:, low], asks0.at[rows : rows + more]),
        (audio_q.at[:, high], asks0.at[rows + more :]),
        (video_q.at[:, high], asks1),
        (video_v.at[:, high], values_ref),
    ]
    at = half
    for out in (sight1, sight2):
        moves += sight_moves(video_k, video_v, at, out)
        at += out.shape[1]
    copies = move_all(moves, sem)
    tables(n, me_ref[0], count_ref, offset_ref, (mask0_ref, mask1_ref), near_ref)
    for copy in copies:
        copy.wait()


def tables(n, me, count_ref, offset_ref, mask_refs, near_ref):
    upper = me * 2 >= n
    inner, end = jnp.where(upper, 1, n - 2), jnp.where(upper, 0, n - 1)
    frames = (me, me ^ 1, inner, end)
    audio_rows = offset_ref.shape[1] // n
    video_rows = mask_refs[0].shape[1] // n
    pieces = [offset_ref[:, i * audio_rows : (i + 1) * audio_rows] for i in range(n)]
    offsets = jnp.concatenate([pick(pieces, frame) for frame in frames], axis=1)
    near = jnp.where(jnp.abs(offsets - me) <= SPAN, 0.0, MASKED)
    near_ref[:video_rows, :] = jnp.broadcast_to(near, (video_rows, n * audio_rows))
    near_ref[video_rows:, :] = jnp.zeros((audio_rows, n * audio_rows), jnp.float32)
    size = 2 * audio_rows
    corner = lax.broadcasted_iota(jnp.int32, (size, size), 0) == lax.broadcasted_iota(
        jnp.int32, (size, size), 1
    )
    asking = jnp.sum(jnp.where(corner, offsets[:, :size], 0), axis=1, keepdims=True)
    within = lax.broadcasted_iota(jnp.int32, (1, video_rows), 1)
    for i, frame in enumerate(frames):
        cols = slice(i * video_rows, (i + 1) * video_rows)
        live = jnp.where(within < count_ref[frame], 0.0, MASKED)
        reach = jnp.where(jnp.abs(asking - frame) <= SPAN, live, MASKED)
        for who, mask_ref in enumerate(mask_refs):
            mask_ref[:video_rows, cols] = jnp.broadcast_to(live, (video_rows, video_rows))
            mask_ref[video_rows:, cols] = reach[who * audio_rows : (who + 1) * audio_rows]


def sound_blocks(blocks, audio_rows, half, cols):
    key_rows = slice(half * audio_rows, (half + 1) * audio_rows)
    value_rows = slice((2 + half) * audio_rows, (3 + half) * audio_rows)
    keys = jnp.concatenate([b[key_rows, cols] for b in blocks], axis=0)
    values = jnp.concatenate([b[value_rows, cols] for b in blocks], axis=0)
    return keys, values


def queries_of(half, asks0, asks1, video_rows, audio_rows, cols):
    rows = video_rows + audio_rows
    if half == 0:
        return asks0[:rows, cols]
    return jnp.concatenate([asks1[:, cols], asks0[rows:, cols]], axis=0)


def audio_mate_kernel(n, me_ref, asks0, out, second, across, far, mate_ref):
    audio_rows, width = mate_ref.shape[0], out.shape[1]
    me = me_ref[0]

    @pl.when((me > 0) & (me < n - 1))
    def _():
        for half in range(2):
            first = asks0.shape[0] - (2 - half) * audio_rows
            for at in range(0, width, HEAD_DIM):
                cols = slice(at, at + HEAD_DIM)
                to = slice(half * width + at, half * width + at + HEAD_DIM)
                keys, values = sound_blocks((out, second, across, far), audio_rows, half, cols)
                mate_ref[:, to] = blend(asks0[first : first + audio_rows, cols], keys, values, None)


def audio_own_kernel(n, me_ref, near_ref, asks0, asks1, out, second, across, far, cross_ref, own_ref):
    audio_rows, width = own_ref.shape[0], out.shape[1]
    video_rows = cross_ref.shape[0]
    me = me_ref[0]

    @pl.when((me > 0) & (me < n - 1))
    def _():
        for half in range(2):
            for at in range(0, width, HEAD_DIM):
                cols = slice(at, at + HEAD_DIM)
                to = slice(half * width + at, half * width + at + HEAD_DIM)
                keys, values = sound_blocks((out, second, across, far), audio_rows, half, cols)
                queries = queries_of(half, asks0, asks1, video_rows, audio_rows, cols)
                mixed = blend(queries, keys, values, near_ref[...])
                cross_ref[:, to] = mixed[:video_rows]
                own_ref[:, to] = mixed[video_rows:]


def audio_end_kernel(n, me_ref, near_ref, asks0, asks1, over, first, part1, part2, far, cross_ref):
    video_rows, width = cross_ref.shape[0], over.shape[1]
    audio_rows = over.shape[0] // 4
    me = me_ref[0]

    @pl.when((me == 0) | (me == n - 1))
    def _():
        for half, asks in enumerate((asks0, asks1)):
            for at in range(0, width, HEAD_DIM):
                cols = slice(at, at + HEAD_DIM)
                to = slice(half * width + at, half * width + at + HEAD_DIM)
                shift = 0 if at < part1.shape[1] else part1.shape[1]
                part = (part2 if shift else part1).at[:, at - shift : at - shift + HEAD_DIM]
                blocks = [b.at[:, cols] for b in (over, first)] + [part, far.at[:, cols]]
                every = slice(0, HEAD_DIM)
                keys, values = sound_blocks(blocks, audio_rows, half, every)
                cross_ref[:, to] = blend(asks[:video_rows, cols], keys, values, near_ref[:video_rows])


def video_kernel(n, at, half, offset, me_ref, mask_ref, *refs):
    *asks, own, mate, keys2, values2, far, out_ref = refs
    video_rows = own.shape[0] // 2
    audio_rows = out_ref.shape[0] - video_rows
    me = me_ref[0]

    @pl.when((me > 0) & (me < n - 1))
    def _():
        for head in range(far.shape[1] // HEAD_DIM):
            cols = slice(head * HEAD_DIM, (head + 1) * HEAD_DIM)
            near_cols = slice((offset + head) * HEAD_DIM, (offset + head + 1) * HEAD_DIM)
            all_cols = slice((at + head) * HEAD_DIM, (at + head + 1) * HEAD_DIM)
            half_cols = slice((at - half + head) * HEAD_DIM, (at - half + head + 1) * HEAD_DIM)
            top, low = slice(0, video_rows), slice(video_rows, 2 * video_rows)
            keys = jnp.concatenate(
                [own[top, near_cols], mate[top, near_cols], keys2[:, all_cols], far[top, cols]], axis=0
            )
            values = jnp.concatenate(
                [own[low, near_cols], mate[low, near_cols], values2[:, half_cols], far[low, cols]],
                axis=0,
            )
            queries = queries_of(len(asks) - 1, asks[0], asks[-1], video_rows, audio_rows, half_cols)
            out_ref[:, cols] = blend(queries, keys, values, mask_ref[...])


def place_pieces(parts, first, video_rows, video_self, audio_cross):
    moves, at = [], first
    for part in parts:
        cols = pl.ds(at, part.shape[1])
        moves.append((part.at[:video_rows], video_self.at[:, cols]))
        moves.append((part.at[video_rows:], audio_cross.at[:, cols]))
        at += part.shape[1]
    return moves


def place_end_kernel(n, me_ref, cross, back0, video_self, video_cross, audio_self, audio_cross, sem):
    @pl.when((me_ref[0] == 0) | (me_ref[0] == n - 1))
    def _():
        moves = [(cross, video_cross)]
        moves += place_pieces((back0,), 0, cross.shape[0], video_self, audio_cross)
        for copy in move_all(moves, sem):
            copy.wait()


def place_kernel(n, me_ref, own_cross, own_sound, own0, own1, back_sound, back1, *refs):
    video_self, video_cross, audio_self, audio_cross, sem = refs[4:]
    video_rows, first = own_cross.shape[0], own0.shape[1]
    at_end = (me_ref[0] == 0) | (me_ref[0] == n - 1)

    @pl.when(jnp.logical_not(at_end))
    def _():
        moves = [(own_cross, video_cross), (own_sound, audio_self)]
        moves += place_pieces((own0, own1), 0, video_rows, video_self, audio_cross)
        for copy in move_all(moves, sem):
            copy.wait()

    @pl.when(at_end)
    def _():
        moves = [(back_sound, audio_self)]
        moves += place_pieces((back1,), first, video_rows, video_self, audio_cross)
        for copy in move_all(moves, sem):
            copy.wait()


def place_last_kernel(n, first, me_ref, own, back, old_self, old_cross, video_self, audio_cross, sem):
    at_end = (me_ref[0] == 0) | (me_ref[0] == n - 1)
    for role, part in ((jnp.logical_not(at_end), own), (at_end, back)):

        @pl.when(role)
        def _(part=part):
            moves = place_pieces((part,), first, video_self.shape[0], video_self, audio_cross)
            for copy in move_all(moves, sem):
                copy.wait()


def cost(rows, keys, heads):
    scores = rows * keys * heads
    return pl.CostEstimate(flops=4 * scores * HEAD_DIM, bytes_accessed=rows * heads * 512, transcendentals=scores)


def chunks_of(heads):
    head = heads // 2
    return head, (head + 1) // 2, head // 2


def lined(video_q, video_k, video_v, audio_q, audio_k, audio_v, offsets, counts):
    n, cores = lax.axis_size("seq"), lax.axis_size("mp")
    me = lax.axis_index("seq")
    video_rows, audio_rows = video_q.shape[0], audio_q.shape[0]
    rows = video_rows + audio_rows
    width = video_q.shape[1]
    heads = width // HEAD_DIM
    chunks = chunks_of(heads)
    mate_pairs = [(i, i ^ 1) for i in range(n)]
    cross_pairs = []
    for i in range(n):
        for core in range(cores):
            inner = 0 < i < n - 1
            to = (n - 1 - i) * cores + core if inner else i * cores + cores - 1 - core
            cross_pairs.append((i * cores + core, to))

    def mate(block):
        return lax.ppermute(block, "seq", mate_pairs)

    def cross(block):
        return lax.ppermute(block, ("seq", "mp"), cross_pairs)

    def call(kernel, outs, spaces, *args, **more):
        return pl.pallas_call(
            kernel,
            out_shape=tuple(jax.ShapeDtypeStruct(shape, dtype) for shape, dtype in outs),
            in_specs=spaces,
            compiler_params=PARAMS,
            **more,
        )(*args)

    place = me.astype(jnp.int32).reshape(1)
    raw_keys = video_k
    video_q, video_k, video_v, audio_q, audio_k, audio_v = (
        pltpu.with_memory_space_constraint(block, pltpu.HBM)
        for block in (video_q, video_k, video_v, audio_q, audio_k, audio_v)
    )
    at_end = (me == 0) | (me == n - 1)
    lengths = [size * HEAD_DIM for size in chunks]
    half = lengths[0]
    first_out, first_over, values0 = call(
        functools.partial(first_pack, n),
        (((2 * video_rows, half), jnp.bfloat16),) * 2 + (((video_rows, half), jnp.bfloat16),),
        [SMEM] + [HBM] * 4,
        place,
        video_k,
        video_v,
        audio_k,
        audio_v,
        out_specs=(VMEM,) * 3,
        scratch_shapes=[pltpu.SemaphoreType.DMA((7,))],
    )
    outs = tuple(((2 * video_rows, length), jnp.bfloat16) for length in lengths[1:])
    outs += (((rows + audio_rows, half), jnp.bfloat16), ((video_rows, half), jnp.bfloat16))
    outs += (((video_rows, half), jnp.bfloat16),)
    outs += (((rows, n * video_rows), jnp.float32),) * 2 + (((rows, n * audio_rows), jnp.float32),)
    *sights, asks0, asks1, values1, mask0, mask1, near = call(
        functools.partial(second_pack, n),
        outs,
        [SMEM, SMEM, VMEM] + [HBM] * 4,
        place,
        counts,
        offsets.reshape(1, -1),
        video_k,
        video_v,
        video_q,
        audio_q,
        out_specs=(VMEM,) * len(outs),
        scratch_shapes=[pltpu.SemaphoreType.DMA((9,))],
    )
    asks = [asks0, asks1]
    sights = [first_over] + sights

    keys_across = cross(raw_keys)
    values_across = [cross(values0), cross(values1)]
    sight_mate = [mate(first_out)]
    sound_across = cross(first_out)
    second_mate = mate(first_over)
    sound_far = cross(second_mate)
    at = 0
    for i in (1, 2):
        part = sound_across[:, at : at + lengths[i]]
        sight_mate.append(mate(jnp.where(at_end, sights[i], part)))
        at += lengths[i]
    pieces = [(0, chunks[0], 0, 0)]
    sight_far = [cross(sight_mate[0])]
    for source in (1, 2):
        pieces.append((sum(chunks[:source]), chunks[source], source, 0))
        sight_far.append(cross(sight_mate[source]))
    last = len(pieces) - 1
    asks_mate = [mate(asks[i]) for i in range(2)]

    def look(i, queries, mask):
        at, size, source, offset = pieces[i]
        half = min(source, 1)
        return call(
            functools.partial(video_kernel, n, at, half * chunks[0], offset),
            (((rows, size * HEAD_DIM), jnp.bfloat16),),
            [SMEM] + [VMEM] * (7 + half),
            place,
            mask,
            *queries[: 1 + half],
            sights[source],
            sight_mate[source],
            keys_across,
            values_across[half],
            sight_far[i],
            out_specs=(VMEM,),
            cost_estimate=cost(rows, n * video_rows, size),
        )[0]

    results = [look(i, asks_mate, mask1) for i in range(last + 1)]
    back = [mate(result) for result in results]
    mine = [look(i, asks, mask0) for i in range(last + 1)]
    theirs = call(
        functools.partial(audio_mate_kernel, n),
        (((audio_rows, width), jnp.bfloat16),),
        [SMEM] + [VMEM] * 5,
        place,
        asks_mate[0],
        first_out,
        second_mate,
        sound_across,
        sound_far,
        out_specs=(VMEM,),
        cost_estimate=cost(audio_rows, n * audio_rows, heads),
    )[0]
    own_cross, own = call(
        functools.partial(audio_own_kernel, n),
        (((video_rows, width), jnp.bfloat16), ((audio_rows, width), jnp.bfloat16)),
        [SMEM] + [VMEM] * 7,
        place,
        near,
        *asks,
        first_out,
        second_mate,
        sound_across,
        sound_far,
        out_specs=(VMEM,) * 2,
        cost_estimate=cost(rows, n * audio_rows, heads),
    )
    end_cross = call(
        functools.partial(audio_end_kernel, n),
        (((video_rows, width), jnp.bfloat16),),
        [SMEM] + [VMEM] * 8,
        place,
        near,
        *asks,
        first_over,
        sight_mate[0],
        sight_mate[1],
        sight_mate[2],
        sound_far,
        out_specs=(VMEM,),
        cost_estimate=cost(rows, n * audio_rows, heads),
    )[0]
    back_sound = mate(theirs)
    video_shape = ((video_rows, width), jnp.bfloat16)
    audio_shape = ((audio_rows, width), jnp.bfloat16)
    shapes = (video_shape, video_shape, audio_shape, audio_shape)
    begun = call(
        functools.partial(place_end_kernel, n),
        shapes,
        [SMEM] + [VMEM] * 2,
        place,
        end_cross,
        back[0],
        out_specs=(HBM,) * 4,
        scratch_shapes=[pltpu.SemaphoreType.DMA((3,))],
    )
    video_self, video_cross, audio_self, audio_cross = call(
        functools.partial(place_kernel, n),
        shapes,
        [SMEM] + [VMEM] * 6 + [HBM] * 4,
        place,
        own_cross,
        own,
        *mine[:2],
        back_sound,
        back[1],
        *begun,
        out_specs=(HBM,) * 4,
        scratch_shapes=[pltpu.SemaphoreType.DMA((6,))],
        input_output_aliases={7: 0, 8: 1, 9: 2, 10: 3},
    )
    video_self, audio_cross = call(
        functools.partial(place_last_kernel, n, width - chunks[2] * HEAD_DIM),
        (video_shape, audio_shape),
        [SMEM] + [VMEM] * 2 + [HBM] * 2,
        place,
        mine[last],
        back[last],
        video_self,
        audio_cross,
        out_specs=(HBM,) * 2,
        scratch_shapes=[pltpu.SemaphoreType.DMA((2,))],
        input_output_aliases={3: 0, 4: 1},
    )
    return video_self, video_cross, audio_self, audio_cross


def solution(mesh):
    split = P(("groups", "seq"), ("tower", "mp"))
    placed = (split,) * 6 + (P("groups"), P("groups"))
    sizes = mesh.shape
    line = sizes["seq"] == 4 and sizes["mp"] == 2

    def whole(*arrays):
        heads = arrays[0].shape[1] // HEAD_DIM // (sizes["tower"] * sizes["mp"])
        paired = heads % 2 == 0 and heads > 3 and arrays[0].shape[0] == 2 * arrays[3].shape[0]
        body = lined if line and paired else gathered
        return jax.shard_map(
            body, mesh=mesh, in_specs=placed, out_specs=(split,) * 4, check_vma=False
        )(*arrays)

    return whole
```

```python
import functools

import jax
import jax.numpy as jnp
from jax import lax
from jax.experimental import pallas as pl
from jax.experimental.pallas import tpu as pltpu
from jax.sharding import PartitionSpec as P


HEAD_DIM = 128
SPAN = 1
STEP = 128
MASKED = -1e30
LOG2E = 1.4426950408889634
VMEM = pl.BlockSpec(memory_space=pltpu.VMEM)
SMEM = pl.BlockSpec(memory_space=pltpu.SMEM)
HBM = pl.BlockSpec(memory_space=pltpu.HBM)
PARAMS = pltpu.CompilerParams(vmem_limit_bytes=16 << 20)


def attend(queries, key_rows, value_rows, allowed):
    scores = jnp.einsum(
        "qhe,khe->hqk", queries, key_rows, preferred_element_type=jnp.float32
    ) * HEAD_DIM ** (-0.5)
    scores = jnp.where(allowed[None], scores, MASKED)
    peak = jnp.max(scores, axis=2)
    weights = jnp.where(allowed[None], jnp.exp(scores - peak[:, :, None]), 0.0)
    total = jnp.sum(weights, axis=2)
    blended = jnp.einsum(
        "hqk,khe->hqe", weights.astype(jnp.bfloat16), value_rows, preferred_element_type=jnp.float32
    )
    blended = blended / total[:, :, None]
    return jnp.transpose(blended, (1, 0, 2)).reshape(blended.shape[1], -1).astype(jnp.bfloat16)


def gathered(video_q, video_k, video_v, audio_q, audio_k, audio_v, offsets, counts):
    my_frame = lax.axis_index("seq")
    video_rows, audio_rows = video_q.shape[0], audio_q.shape[0]

    def heads(rows):
        return rows.reshape(rows.shape[0], -1, HEAD_DIM)

    def everywhere(rows):
        return heads(lax.all_gather(rows, "seq", axis=0, tiled=True))

    my_offsets = lax.dynamic_slice_in_dim(offsets, my_frame * audio_rows, audio_rows)
    keys, values = everywhere(video_k), everywhere(video_v)
    audio_keys, audio_values = everywhere(audio_k), everywhere(audio_v)
    positions = jnp.arange(keys.shape[0], dtype=jnp.int32)
    source = positions // video_rows
    is_live = positions % video_rows < jnp.repeat(counts, video_rows)
    video_self = attend(heads(video_q), keys, values, is_live[None, :])
    in_reach = (jnp.abs(my_offsets[:, None] - source[None, :]) <= SPAN) & is_live[None, :]
    audio_cross = attend(heads(audio_q), keys, values, in_reach)
    every = jnp.ones((1, audio_keys.shape[0]), jnp.bool_)
    audio_self = attend(heads(audio_q), audio_keys, audio_values, every)
    in_reach = jnp.abs(offsets - my_frame) <= SPAN
    video_cross = attend(heads(video_q), audio_keys, audio_values, in_reach[None, :])
    return (video_self, video_cross, audio_self, audio_cross)


def blend(queries, keys, values, bias):
    scores = lax.dot_general(
        queries, keys, (((1,), (1,)), ((), ())), preferred_element_type=jnp.float32
    )
    if bias is not None:
        scores = scores + bias
    peak = jnp.max(scores, axis=1, keepdims=True)
    weights = jnp.exp2((scores - peak) * (HEAD_DIM ** (-0.5) * LOG2E))
    total = jnp.sum(weights, axis=1, keepdims=True)
    weights = weights.astype(jnp.bfloat16)
    mixed = 0.0
    for at in range(0, keys.shape[0], STEP):
        mixed += jnp.dot(
            weights[:, at : at + STEP], values[at : at + STEP], preferred_element_type=jnp.float32
        )
    return (mixed * (1.0 / total)).astype(jnp.bfloat16)


def pick(pieces, at):
    chosen = pieces[0]
    for i in range(1, len(pieces)):
        chosen = jnp.where(at == i, pieces[i], chosen)
    return chosen


def move_all(moves, sem):
    copies = [pltpu.make_async_copy(src, dst, sem.at[i]) for i, (src, dst) in enumerate(moves)]
    for copy in copies:
        copy.start()
    return copies


def sight_moves(video_k, video_v, first, out):
    rows, cols = video_k.shape[0], pl.ds(first, out.shape[1])
    return [(video_k.at[:, cols], out.at[:rows]), (video_v.at[:, cols], out.at[rows:])]


def sound_moves(audio_k, audio_v, out):
    rows, width = audio_k.shape[0], out.shape[1]
    moves = []
    for src in (audio_k, audio_v):
        for half in range(2):
            at = len(moves) * rows
            moves.append((src.at[:, pl.ds(half * width, width)], out.at[at : at + rows]))
    return moves


def first_pack(n, me_ref, video_k, video_v, audio_k, audio_v, out_ref, over_ref, values_ref, sem):
    me = me_ref[0]
    half = values_ref.shape[1]
    at_end = (me == 0) | (me == n - 1)
    for role, sight, sound in ((at_end, out_ref, over_ref), (jnp.logical_not(at_end), over_ref, out_ref)):

        @pl.when(role)
        def _(sight=sight, sound=sound):
            moves = sight_moves(video_k, video_v, 0, sight) + sound_moves(audio_k, audio_v, sound)
            moves.append((video_v.at[:, pl.ds(0, half)], values_ref))
            for copy in move_all(moves, sem):
                copy.wait()


def second_pack(n, me_ref, count_ref, offset_ref, video_k, video_v, video_q, audio_q, *outs):
    sight1, sight2, asks0, asks1, values_ref, mask0_ref, mask1_ref, near_ref, sem = outs
    half = asks0.shape[1]
    low, high = pl.ds(0, half), pl.ds(half, half)
    rows, more = video_q.shape[0], audio_q.shape[0]
    moves = [
        (video_q.at[:, low], asks0.at[:rows]),
        (audio_q.at[:, low], asks0.at[rows : rows + more]),
        (audio_q.at[:, high], asks0.at[rows + more :]),
        (video_q.at[:, high], asks1),
        (video_v.at[:, high], values_ref),
    ]
    at = half
    for out in (sight1, sight2):
        moves += sight_moves(video_k, video_v, at, out)
        at += out.shape[1]
    copies = move_all(moves, sem)
    tables(n, me_ref[0], count_ref, offset_ref, (mask0_ref, mask1_ref), near_ref)
    for copy in copies:
        copy.wait()


def tables(n, me, count_ref, offset_ref, mask_refs, near_ref):
    upper = me * 2 >= n
    inner, end = jnp.where(upper, 1, n - 2), jnp.where(upper, 0, n - 1)
    frames = (me, me ^ 1, inner, end)
    audio_rows = offset_ref.shape[1] // n
    video_rows = mask_refs[0].shape[1] // n
    pieces = [offset_ref[:, i * audio_rows : (i + 1) * audio_rows] for i in range(n)]
    offsets = jnp.concatenate([pick(pieces, frame) for frame in frames], axis=1)
    near = jnp.where(jnp.abs(offsets - me) <= SPAN, 0.0, MASKED)
    near_ref[:video_rows, :] = jnp.broadcast_to(near, (video_rows, n * audio_rows))
    near_ref[video_rows:, :] = jnp.zeros((audio_rows, n * audio_rows), jnp.float32)
    size = 2 * audio_rows
    corner = lax.broadcasted_iota(jnp.int32, (size, size), 0) == lax.broadcasted_iota(
        jnp.int32, (size, size), 1
    )
    asking = jnp.sum(jnp.where(corner, offsets[:, :size], 0), axis=1, keepdims=True)
    within = lax.broadcasted_iota(jnp.int32, (1, video_rows), 1)
    for i, frame in enumerate(frames):
        cols = slice(i * video_rows, (i + 1) * video_rows)
        live = jnp.where(within < count_ref[frame], 0.0, MASKED)
        reach = jnp.where(jnp.abs(asking - frame) <= SPAN, live, MASKED)
        for who, mask_ref in enumerate(mask_refs):
            mask_ref[:video_rows, cols] = jnp.broadcast_to(live, (video_rows, video_rows))
            mask_ref[video_rows:, cols] = reach[who * audio_rows : (who + 1) * audio_rows]


def sound_blocks(blocks, audio_rows, half, cols):
    key_rows = slice(half * audio_rows, (half + 1) * audio_rows)
    value_rows = slice((2 + half) * audio_rows, (3 + half) * audio_rows)
    keys = jnp.concatenate([b[key_rows, cols] for b in blocks], axis=0)
    values = jnp.concatenate([b[value_rows, cols] for b in blocks], axis=0)
    return keys, values


def queries_of(half, asks0, asks1, video_rows, audio_rows, cols):
    rows = video_rows + audio_rows
    if half == 0:
        return asks0[:rows, cols]
    return jnp.concatenate([asks1[:, cols], asks0[rows:, cols]], axis=0)


def audio_mate_kernel(n, me_ref, asks0, out, second, across, far, mate_ref):
    audio_rows, width = mate_ref.shape[0], out.shape[1]
    me = me_ref[0]

    @pl.when((me > 0) & (me < n - 1))
    def _():
        for half in range(2):
            first = asks0.shape[0] - (2 - half) * audio_rows
            for at in range(0, width, HEAD_DIM):
                cols = slice(at, at + HEAD_DIM)
                to = slice(half * width + at, half * width + at + HEAD_DIM)
                keys, values = sound_blocks((out, second, across, far), audio_rows, half, cols)
                mate_ref[:, to] = blend(asks0[first : first + audio_rows, cols], keys, values, None)


def audio_own_kernel(n, me_ref, near_ref, asks0, asks1, out, second, across, far, cross_ref, own_ref):
    audio_rows, width = own_ref.shape[0], out.shape[1]
    video_rows = cross_ref.shape[0]
    me = me_ref[0]

    @pl.when((me > 0) & (me < n - 1))
    def _():
        for half in range(2):
            for at in range(0, width, HEAD_DIM):
                cols = slice(at, at + HEAD_DIM)
                to = slice(half * width + at, half * width + at + HEAD_DIM)
                keys, values = sound_blocks((out, second, across, far), audio_rows, half, cols)
                queries = queries_of(half, asks0, asks1, video_rows, audio_rows, cols)
                mixed = blend(queries, keys, values, near_ref[...])
                cross_ref[:, to] = mixed[:video_rows]
                own_ref[:, to] = mixed[video_rows:]


def audio_end_kernel(n, me_ref, near_ref, asks0, asks1, over, first, part1, part2, far, cross_ref):
    video_rows, width = cross_ref.shape[0], over.shape[1]
    audio_rows = over.shape[0] // 4
    me = me_ref[0]

    @pl.when((me == 0) | (me == n - 1))
    def _():
        for half, asks in enumerate((asks0, asks1)):
            for at in range(0, width, HEAD_DIM):
                cols = slice(at, at + HEAD_DIM)
                to = slice(half * width + at, half * width + at + HEAD_DIM)
                shift = 0 if at < part1.shape[1] else part1.shape[1]
                part = (part2 if shift else part1).at[:, at - shift : at - shift + HEAD_DIM]
                blocks = [b.at[:, cols] for b in (over, first)] + [part, far.at[:, cols]]
                every = slice(0, HEAD_DIM)
                keys, values = sound_blocks(blocks, audio_rows, half, every)
                cross_ref[:, to] = blend(asks[:video_rows, cols], keys, values, near_ref[:video_rows])


def video_kernel(n, at, half, offset, me_ref, mask_ref, *refs):
    *asks, own, mate, keys2, values2, far, out_ref = refs
    video_rows = own.shape[0] // 2
    audio_rows = out_ref.shape[0] - video_rows
    me = me_ref[0]

    @pl.when((me > 0) & (me < n - 1))
    def _():
        for head in range(far.shape[1] // HEAD_DIM):
            cols = slice(head * HEAD_DIM, (head + 1) * HEAD_DIM)
            near_cols = slice((offset + head) * HEAD_DIM, (offset + head + 1) * HEAD_DIM)
            all_cols = slice((at + head) * HEAD_DIM, (at + head + 1) * HEAD_DIM)
            half_cols = slice((at - half + head) * HEAD_DIM, (at - half + head + 1) * HEAD_DIM)
            top, low = slice(0, video_rows), slice(video_rows, 2 * video_rows)
            keys = jnp.concatenate(
                [own[top, near_cols], mate[top, near_cols], keys2[:, all_cols], far[top, cols]], axis=0
            )
            values = jnp.concatenate(
                [own[low, near_cols], mate[low, near_cols], values2[:, half_cols], far[low, cols]],
                axis=0,
            )
            queries = queries_of(len(asks) - 1, asks[0], asks[-1], video_rows, audio_rows, half_cols)
            out_ref[:, cols] = blend(queries, keys, values, mask_ref[...])


def place_pieces(parts, first, video_rows, video_self, audio_cross):
    moves, at = [], first
    for part in parts:
        cols = pl.ds(at, part.shape[1])
        moves.append((part.at[:video_rows], video_self.at[:, cols]))
        moves.append((part.at[video_rows:], audio_cross.at[:, cols]))
        at += part.shape[1]
    return moves


def place_end_kernel(n, me_ref, cross, video_self, video_cross, audio_self, audio_cross, sem):
    @pl.when((me_ref[0] == 0) | (me_ref[0] == n - 1))
    def _():
        for copy in move_all([(cross, video_cross)], sem):
            copy.wait()


def place_kernel(n, me_ref, own_cross, own_sound, own0, own1, back_sound, back0, back1, *refs):
    video_self, video_cross, audio_self, audio_cross, sem = refs[4:]
    video_rows = own_cross.shape[0]
    at_end = (me_ref[0] == 0) | (me_ref[0] == n - 1)

    @pl.when(jnp.logical_not(at_end))
    def _():
        moves = [(own_cross, video_cross), (own_sound, audio_self)]
        moves += place_pieces((own0, own1), 0, video_rows, video_self, audio_cross)
        for copy in move_all(moves, sem):
            copy.wait()

    @pl.when(at_end)
    def _():
        moves = [(back_sound, audio_self)]
        moves += place_pieces((back0, back1), 0, video_rows, video_self, audio_cross)
        for copy in move_all(moves, sem):
            copy.wait()


def place_last_kernel(n, first, me_ref, own, back, old_self, old_cross, video_self, audio_cross, sem):
    at_end = (me_ref[0] == 0) | (me_ref[0] == n - 1)
    for role, part in ((jnp.logical_not(at_end), own), (at_end, back)):

        @pl.when(role)
        def _(part=part):
            moves = place_pieces((part,), first, video_self.shape[0], video_self, audio_cross)
            for copy in move_all(moves, sem):
                copy.wait()


def cost(rows, keys, heads):
    scores = rows * keys * heads
    return pl.CostEstimate(flops=4 * scores * HEAD_DIM, bytes_accessed=rows * heads * 512, transcendentals=scores)


def chunks_of(heads):
    head = heads // 2
    return head, (head + 1) // 2, head // 2


def lined(video_q, video_k, video_v, audio_q, audio_k, audio_v, offsets, counts):
    n, cores = lax.axis_size("seq"), lax.axis_size("mp")
    me = lax.axis_index("seq")
    video_rows, audio_rows = video_q.shape[0], audio_q.shape[0]
    rows = video_rows + audio_rows
    width = video_q.shape[1]
    heads = width // HEAD_DIM
    chunks = chunks_of(heads)
    mate_pairs = [(i, i ^ 1) for i in range(n)]
    cross_pairs = []
    for i in range(n):
        for core in range(cores):
            inner = 0 < i < n - 1
            to = (n - 1 - i) * cores + core if inner else i * cores + cores - 1 - core
            cross_pairs.append((i * cores + core, to))

    def mate(block):
        return lax.ppermute(block, "seq", mate_pairs)

    def cross(block):
        return lax.ppermute(block, ("seq", "mp"), cross_pairs)

    def call(kernel, outs, spaces, *args, **more):
        return pl.pallas_call(
            kernel,
            out_shape=tuple(jax.ShapeDtypeStruct(shape, dtype) for shape, dtype in outs),
            in_specs=spaces,
            compiler_params=PARAMS,
            **more,
        )(*args)

    place = me.astype(jnp.int32).reshape(1)
    raw_keys = video_k
    video_q, video_k, video_v, audio_q, audio_k, audio_v = (
        pltpu.with_memory_space_constraint(block, pltpu.HBM)
        for block in (video_q, video_k, video_v, audio_q, audio_k, audio_v)
    )
    at_end = (me == 0) | (me == n - 1)
    lengths = [size * HEAD_DIM for size in chunks]
    half = lengths[0]
    first_out, first_over, values0 = call(
        functools.partial(first_pack, n),
        (((2 * video_rows, half), jnp.bfloat16),) * 2 + (((video_rows, half), jnp.bfloat16),),
        [SMEM] + [HBM] * 4,
        place,
        video_k,
        video_v,
        audio_k,
        audio_v,
        out_specs=(VMEM,) * 3,
        scratch_shapes=[pltpu.SemaphoreType.DMA((7,))],
    )
    outs = tuple(((2 * video_rows, length), jnp.bfloat16) for length in lengths[1:])
    outs += (((rows + audio_rows, half), jnp.bfloat16), ((video_rows, half), jnp.bfloat16))
    outs += (((video_rows, half), jnp.bfloat16),)
    outs += (((rows, n * video_rows), jnp.float32),) * 2 + (((rows, n * audio_rows), jnp.float32),)
    *sights, asks0, asks1, values1, mask0, mask1, near = call(
        functools.partial(second_pack, n),
        outs,
        [SMEM, SMEM, VMEM] + [HBM] * 4,
        place,
        counts,
        offsets.reshape(1, -1),
        video_k,
        video_v,
        video_q,
        audio_q,
        out_specs=(VMEM,) * len(outs),
        scratch_shapes=[pltpu.SemaphoreType.DMA((9,))],
    )
    asks = [asks0, asks1]
    sights = [first_over] + sights

    keys_across = cross(raw_keys)
    values_across = [cross(values0), cross(values1)]
    sight_mate = [mate(first_out)]
    sound_across = cross(first_out)
    second_mate = mate(first_over)
    sound_far = cross(second_mate)
    at = 0
    for i in (1, 2):
        part = sound_across[:, at : at + lengths[i]]
        sight_mate.append(mate(jnp.where(at_end, sights[i], part)))
        at += lengths[i]
    pieces = [(0, chunks[0], 0, 0)]
    sight_far = [cross(sight_mate[0])]
    for source in (1, 2):
        pieces.append((sum(chunks[:source]), chunks[source], source, 0))
        sight_far.append(cross(sight_mate[source]))
    last = len(pieces) - 1
    asks_mate = [mate(asks[i]) for i in range(2)]

    def look(i, queries, mask):
        at, size, source, offset = pieces[i]
        half = min(source, 1)
        return call(
            functools.partial(video_kernel, n, at, half * chunks[0], offset),
            (((rows, size * HEAD_DIM), jnp.bfloat16),),
            [SMEM] + [VMEM] * (7 + half),
            place,
            mask,
            *queries[: 1 + half],
            sights[source],
            sight_mate[source],
            keys_across,
            values_across[half],
            sight_far[i],
            out_specs=(VMEM,),
            cost_estimate=cost(rows, n * video_rows, size),
        )[0]

    results = [look(i, asks_mate, mask1) for i in range(last + 1)]
    back = [mate(result) for result in results]
    mine = [look(i, asks, mask0) for i in range(last + 1)]
    theirs = call(
        functools.partial(audio_mate_kernel, n),
        (((audio_rows, width), jnp.bfloat16),),
        [SMEM] + [VMEM] * 5,
        place,
        asks_mate[0],
        first_out,
        second_mate,
        sound_across,
        sound_far,
        out_specs=(VMEM,),
        cost_estimate=cost(audio_rows, n * audio_rows, heads),
    )[0]
    own_cross, own = call(
        functools.partial(audio_own_kernel, n),
        (((video_rows, width), jnp.bfloat16), ((audio_rows, width), jnp.bfloat16)),
        [SMEM] + [VMEM] * 7,
        place,
        near,
        *asks,
        first_out,
        second_mate,
        sound_across,
        sound_far,
        out_specs=(VMEM,) * 2,
        cost_estimate=cost(rows, n * audio_rows, heads),
    )
    end_cross = call(
        functools.partial(audio_end_kernel, n),
        (((video_rows, width), jnp.bfloat16),),
        [SMEM] + [VMEM] * 8,
        place,
        near,
        *asks,
        first_over,
        sight_mate[0],
        sight_mate[1],
        sight_mate[2],
        sound_far,
        out_specs=(VMEM,),
        cost_estimate=cost(rows, n * audio_rows, heads),
    )[0]
    back_sound = mate(theirs)
    video_shape = ((video_rows, width), jnp.bfloat16)
    audio_shape = ((audio_rows, width), jnp.bfloat16)
    shapes = (video_shape, video_shape, audio_shape, audio_shape)
    begun = call(
        functools.partial(place_end_kernel, n),
        shapes,
        [SMEM, VMEM],
        place,
        end_cross,
        out_specs=(HBM,) * 4,
        scratch_shapes=[pltpu.SemaphoreType.DMA((1,))],
    )
    video_self, video_cross, audio_self, audio_cross = call(
        functools.partial(place_kernel, n),
        shapes,
        [SMEM] + [VMEM] * 7 + [HBM] * 4,
        place,
        own_cross,
        own,
        *mine[:2],
        back_sound,
        *back[:2],
        *begun,
        out_specs=(HBM,) * 4,
        scratch_shapes=[pltpu.SemaphoreType.DMA((6,))],
        input_output_aliases={8: 0, 9: 1, 10: 2, 11: 3},
    )
    video_self, audio_cross = call(
        functools.partial(place_last_kernel, n, width - chunks[2] * HEAD_DIM),
        (video_shape, audio_shape),
        [SMEM] + [VMEM] * 2 + [HBM] * 2,
        place,
        mine[last],
        back[last],
        video_self,
        audio_cross,
        out_specs=(HBM,) * 2,
        scratch_shapes=[pltpu.SemaphoreType.DMA((2,))],
        input_output_aliases={3: 0, 4: 1},
    )
    return video_self, video_cross, audio_self, audio_cross


def solution(mesh):
    split = P(("groups", "seq"), ("tower", "mp"))
    placed = (split,) * 6 + (P("groups"), P("groups"))
    sizes = mesh.shape
    line = sizes["seq"] == 4 and sizes["mp"] == 2

    def whole(*arrays):
        heads = arrays[0].shape[1] // HEAD_DIM // (sizes["tower"] * sizes["mp"])
        paired = heads % 2 == 0 and heads > 3 and arrays[0].shape[0] == 2 * arrays[3].shape[0]
        body = lined if line and paired else gathered
        return jax.shard_map(
            body, mesh=mesh, in_specs=placed, out_specs=(split,) * 4, check_vma=False
        )(*arrays)

    return whole
```

```python
import functools

import jax
import jax.numpy as jnp
from jax import lax
from jax.experimental import pallas as pl
from jax.experimental.pallas import tpu as pltpu
from jax.sharding import PartitionSpec as P


HEAD_DIM = 128
SPAN = 1
STEP = 128
MASKED = -1e30
LOG2E = 1.4426950408889634
VMEM = pl.BlockSpec(memory_space=pltpu.VMEM)
SMEM = pl.BlockSpec(memory_space=pltpu.SMEM)
HBM = pl.BlockSpec(memory_space=pltpu.HBM)
PARAMS = pltpu.CompilerParams(vmem_limit_bytes=16 << 20)


def attend(queries, key_rows, value_rows, allowed):
    scores = jnp.einsum(
        "qhe,khe->hqk", queries, key_rows, preferred_element_type=jnp.float32
    ) * HEAD_DIM ** (-0.5)
    scores = jnp.where(allowed[None], scores, MASKED)
    peak = jnp.max(scores, axis=2)
    weights = jnp.where(allowed[None], jnp.exp(scores - peak[:, :, None]), 0.0)
    total = jnp.sum(weights, axis=2)
    blended = jnp.einsum(
        "hqk,khe->hqe", weights.astype(jnp.bfloat16), value_rows, preferred_element_type=jnp.float32
    )
    blended = blended / total[:, :, None]
    return jnp.transpose(blended, (1, 0, 2)).reshape(blended.shape[1], -1).astype(jnp.bfloat16)


def gathered(video_q, video_k, video_v, audio_q, audio_k, audio_v, offsets, counts):
    my_frame = lax.axis_index("seq")
    video_rows, audio_rows = video_q.shape[0], audio_q.shape[0]

    def heads(rows):
        return rows.reshape(rows.shape[0], -1, HEAD_DIM)

    def everywhere(rows):
        return heads(lax.all_gather(rows, "seq", axis=0, tiled=True))

    my_offsets = lax.dynamic_slice_in_dim(offsets, my_frame * audio_rows, audio_rows)
    keys, values = everywhere(video_k), everywhere(video_v)
    audio_keys, audio_values = everywhere(audio_k), everywhere(audio_v)
    positions = jnp.arange(keys.shape[0], dtype=jnp.int32)
    source = positions // video_rows
    is_live = positions % video_rows < jnp.repeat(counts, video_rows)
    video_self = attend(heads(video_q), keys, values, is_live[None, :])
    in_reach = (jnp.abs(my_offsets[:, None] - source[None, :]) <= SPAN) & is_live[None, :]
    audio_cross = attend(heads(audio_q), keys, values, in_reach)
    every = jnp.ones((1, audio_keys.shape[0]), jnp.bool_)
    audio_self = attend(heads(audio_q), audio_keys, audio_values, every)
    in_reach = jnp.abs(offsets - my_frame) <= SPAN
    video_cross = attend(heads(video_q), audio_keys, audio_values, in_reach[None, :])
    return (video_self, video_cross, audio_self, audio_cross)


def blend(queries, keys, values, bias):
    scores = lax.dot_general(
        queries, keys, (((1,), (1,)), ((), ())), preferred_element_type=jnp.float32
    )
    if bias is not None:
        scores = scores + bias
    peak = jnp.max(scores, axis=1, keepdims=True)
    weights = jnp.exp2((scores - peak) * (HEAD_DIM ** (-0.5) * LOG2E))
    total = jnp.sum(weights, axis=1, keepdims=True)
    weights = weights.astype(jnp.bfloat16)
    mixed = 0.0
    for at in range(0, keys.shape[0], STEP):
        mixed += jnp.dot(
            weights[:, at : at + STEP], values[at : at + STEP], preferred_element_type=jnp.float32
        )
    return (mixed * (1.0 / total)).astype(jnp.bfloat16)


def pick(pieces, at):
    chosen = pieces[0]
    for i in range(1, len(pieces)):
        chosen = jnp.where(at == i, pieces[i], chosen)
    return chosen


def move_all(moves, sem):
    copies = [pltpu.make_async_copy(src, dst, sem.at[i]) for i, (src, dst) in enumerate(moves)]
    for copy in copies:
        copy.start()
    return copies


def sight_moves(video_k, video_v, first, out):
    rows, cols = video_k.shape[0], pl.ds(first, out.shape[1])
    return [(video_k.at[:, cols], out.at[:rows]), (video_v.at[:, cols], out.at[rows:])]


def sound_moves(audio_k, audio_v, out):
    rows, width = audio_k.shape[0], out.shape[1]
    moves = []
    for src in (audio_k, audio_v):
        for half in range(2):
            at = len(moves) * rows
            moves.append((src.at[:, pl.ds(half * width, width)], out.at[at : at + rows]))
    return moves


def first_pack(n, me_ref, video_k, video_v, audio_k, audio_v, out_ref, over_ref, values_ref, sem):
    me = me_ref[0]
    half = values_ref.shape[1]
    at_end = (me == 0) | (me == n - 1)
    for role, sight, sound in ((at_end, out_ref, over_ref), (jnp.logical_not(at_end), over_ref, out_ref)):

        @pl.when(role)
        def _(sight=sight, sound=sound):
            moves = sight_moves(video_k, video_v, 0, sight) + sound_moves(audio_k, audio_v, sound)
            moves.append((video_v.at[:, pl.ds(0, half)], values_ref))
            for copy in move_all(moves, sem):
                copy.wait()


def second_pack(n, me_ref, count_ref, offset_ref, video_k, video_v, video_q, audio_q, *outs):
    sight1, sight2, asks0, asks1, values_ref, mask0_ref, mask1_ref, near_ref, sem = outs
    half = asks0.shape[1]
    low, high = pl.ds(0, half), pl.ds(half, half)
    rows, more = video_q.shape[0], audio_q.shape[0]
    moves = [
        (video_q.at[:, low], asks0.at[:rows]),
        (audio_q.at[:, low], asks0.at[rows : rows + more]),
        (audio_q.at[:, high], asks0.at[rows + more :]),
        (video_q.at[:, high], asks1),
        (video_v.at[:, high], values_ref),
    ]
    at = half
    for out in (sight1, sight2):
        moves += sight_moves(video_k, video_v, at, out)
        at += out.shape[1]
    copies = move_all(moves, sem)
    tables(n, me_ref[0], count_ref, offset_ref, (mask0_ref, mask1_ref), near_ref)
    for copy in copies:
        copy.wait()


def tables(n, me, count_ref, offset_ref, mask_refs, near_ref):
    upper = me * 2 >= n
    inner, end = jnp.where(upper, 1, n - 2), jnp.where(upper, 0, n - 1)
    frames = (me, me ^ 1, inner, end)
    audio_rows = offset_ref.shape[1] // n
    video_rows = mask_refs[0].shape[1] // n
    pieces = [offset_ref[:, i * audio_rows : (i + 1) * audio_rows] for i in range(n)]
    offsets = jnp.concatenate([pick(pieces, frame) for frame in frames], axis=1)
    near = jnp.where(jnp.abs(offsets - me) <= SPAN, 0.0, MASKED)
    near_ref[:video_rows, :] = jnp.broadcast_to(near, (video_rows, n * audio_rows))
    near_ref[video_rows:, :] = jnp.zeros((audio_rows, n * audio_rows), jnp.float32)
    size = 2 * audio_rows
    corner = lax.broadcasted_iota(jnp.int32, (size, size), 0) == lax.broadcasted_iota(
        jnp.int32, (size, size), 1
    )
    asking = jnp.sum(jnp.where(corner, offsets[:, :size], 0), axis=1, keepdims=True)
    within = lax.broadcasted_iota(jnp.int32, (1, video_rows), 1)
    for i, frame in enumerate(frames):
        cols = slice(i * video_rows, (i + 1) * video_rows)
        live = jnp.where(within < count_ref[frame], 0.0, MASKED)
        reach = jnp.where(jnp.abs(asking - frame) <= SPAN, live, MASKED)
        for who, mask_ref in enumerate(mask_refs):
            mask_ref[:video_rows, cols] = jnp.broadcast_to(live, (video_rows, video_rows))
            mask_ref[video_rows:, cols] = reach[who * audio_rows : (who + 1) * audio_rows]


def sound_blocks(blocks, audio_rows, half, cols):
    key_rows = slice(half * audio_rows, (half + 1) * audio_rows)
    value_rows = slice((2 + half) * audio_rows, (3 + half) * audio_rows)
    keys = jnp.concatenate([b[key_rows, cols] for b in blocks], axis=0)
    values = jnp.concatenate([b[value_rows, cols] for b in blocks], axis=0)
    return keys, values


def queries_of(half, asks0, asks1, video_rows, audio_rows, cols):
    rows = video_rows + audio_rows
    if half == 0:
        return asks0[:rows, cols]
    return jnp.concatenate([asks1[:, cols], asks0[rows:, cols]], axis=0)


def audio_mate_kernel(n, me_ref, asks0, out, second, across, far, mate_ref):
    audio_rows, width = mate_ref.shape[0], out.shape[1]
    me = me_ref[0]

    @pl.when((me > 0) & (me < n - 1))
    def _():
        for half in range(2):
            first = asks0.shape[0] - (2 - half) * audio_rows
            for at in range(0, width, HEAD_DIM):
                cols = slice(at, at + HEAD_DIM)
                to = slice(half * width + at, half * width + at + HEAD_DIM)
                keys, values = sound_blocks((out, second, across, far), audio_rows, half, cols)
                mate_ref[:, to] = blend(asks0[first : first + audio_rows, cols], keys, values, None)


def audio_own_kernel(n, me_ref, near_ref, asks0, asks1, out, second, across, far, cross_ref, own_ref):
    audio_rows, width = own_ref.shape[0], out.shape[1]
    video_rows = cross_ref.shape[0]
    me = me_ref[0]

    @pl.when((me > 0) & (me < n - 1))
    def _():
        for half in range(2):
            for at in range(0, width, HEAD_DIM):
                cols = slice(at, at + HEAD_DIM)
                to = slice(half * width + at, half * width + at + HEAD_DIM)
                keys, values = sound_blocks((out, second, across, far), audio_rows, half, cols)
                queries = queries_of(half, asks0, asks1, video_rows, audio_rows, cols)
                mixed = blend(queries, keys, values, near_ref[...])
                cross_ref[:, to] = mixed[:video_rows]
                own_ref[:, to] = mixed[video_rows:]


def audio_end_kernel(n, me_ref, near_ref, asks0, asks1, over, first, part1, part2, far, cross_ref):
    video_rows, width = cross_ref.shape[0], over.shape[1]
    audio_rows = over.shape[0] // 4
    me = me_ref[0]

    @pl.when((me == 0) | (me == n - 1))
    def _():
        for half, asks in enumerate((asks0, asks1)):
            for at in range(0, width, HEAD_DIM):
                cols = slice(at, at + HEAD_DIM)
                to = slice(half * width + at, half * width + at + HEAD_DIM)
                shift = 0 if at < part1.shape[1] else part1.shape[1]
                part = (part2 if shift else part1).at[:, at - shift : at - shift + HEAD_DIM]
                blocks = [b.at[:, cols] for b in (over, first)] + [part, far.at[:, cols]]
                every = slice(0, HEAD_DIM)
                keys, values = sound_blocks(blocks, audio_rows, half, every)
                cross_ref[:, to] = blend(asks[:video_rows, cols], keys, values, near_ref[:video_rows])


def video_kernel(n, at, half, offset, me_ref, mask_ref, *refs):
    *asks, own, mate, keys2, values2, far, out_ref = refs
    video_rows = own.shape[0] // 2
    audio_rows = out_ref.shape[0] - video_rows
    me = me_ref[0]

    @pl.when((me > 0) & (me < n - 1))
    def _():
        for head in range(far.shape[1] // HEAD_DIM):
            cols = slice(head * HEAD_DIM, (head + 1) * HEAD_DIM)
            near_cols = slice((offset + head) * HEAD_DIM, (offset + head + 1) * HEAD_DIM)
            all_cols = slice((at + head) * HEAD_DIM, (at + head + 1) * HEAD_DIM)
            half_cols = slice((at - half + head) * HEAD_DIM, (at - half + head + 1) * HEAD_DIM)
            top, low = slice(0, video_rows), slice(video_rows, 2 * video_rows)
            keys = jnp.concatenate(
                [own[top, near_cols], mate[top, near_cols], keys2[:, all_cols], far[top, cols]], axis=0
            )
            values = jnp.concatenate(
                [own[low, near_cols], mate[low, near_cols], values2[:, half_cols], far[low, cols]],
                axis=0,
            )
            queries = queries_of(len(asks) - 1, asks[0], asks[-1], video_rows, audio_rows, half_cols)
            out_ref[:, cols] = blend(queries, keys, values, mask_ref[...])


def place_pieces(parts, first, video_rows, video_self, audio_cross):
    moves, at = [], first
    for part in parts:
        cols = pl.ds(at, part.shape[1])
        moves.append((part.at[:video_rows], video_self.at[:, cols]))
        moves.append((part.at[video_rows:], audio_cross.at[:, cols]))
        at += part.shape[1]
    return moves


def place_kernel(n, me_ref, own_cross, end_cross, *refs):
    count = (len(refs) - 5) // 2
    own, back = refs[:count], refs[count : 2 * count]
    video_self, video_cross, audio_self, audio_cross, sem = refs[2 * count :]
    at_end = (me_ref[0] == 0) | (me_ref[0] == n - 1)
    for role, cross, parts in (
        (jnp.logical_not(at_end), own_cross, own),
        (at_end, end_cross, back),
    ):

        @pl.when(role)
        def _(cross=cross, parts=parts):
            moves = [(cross, video_cross), (parts[0], audio_self)]
            moves += place_pieces(parts[1:], 0, cross.shape[0], video_self, audio_cross)
            for copy in move_all(moves, sem):
                copy.wait()


def place_last_kernel(n, first, me_ref, own, back, old_self, old_cross, video_self, audio_cross, sem):
    at_end = (me_ref[0] == 0) | (me_ref[0] == n - 1)
    for role, part in ((jnp.logical_not(at_end), own), (at_end, back)):

        @pl.when(role)
        def _(part=part):
            moves = place_pieces((part,), first, video_self.shape[0], video_self, audio_cross)
            for copy in move_all(moves, sem):
                copy.wait()


def cost(rows, keys, heads):
    scores = rows * keys * heads
    return pl.CostEstimate(flops=4 * scores * HEAD_DIM, bytes_accessed=rows * heads * 512, transcendentals=scores)


def chunks_of(heads):
    head = heads // 2
    return head, (head + 1) // 2, head // 2


def lined(video_q, video_k, video_v, audio_q, audio_k, audio_v, offsets, counts):
    n, cores = lax.axis_size("seq"), lax.axis_size("mp")
    me = lax.axis_index("seq")
    video_rows, audio_rows = video_q.shape[0], audio_q.shape[0]
    rows = video_rows + audio_rows
    width = video_q.shape[1]
    heads = width // HEAD_DIM
    chunks = chunks_of(heads)
    mate_pairs = [(i, i ^ 1) for i in range(n)]
    cross_pairs = []
    for i in range(n):
        for core in range(cores):
            inner = 0 < i < n - 1
            to = (n - 1 - i) * cores + core if inner else i * cores + cores - 1 - core
            cross_pairs.append((i * cores + core, to))

    def mate(block):
        return lax.ppermute(block, "seq", mate_pairs)

    def cross(block):
        return lax.ppermute(block, ("seq", "mp"), cross_pairs)

    def call(kernel, outs, spaces, *args, **more):
        return pl.pallas_call(
            kernel,
            out_shape=tuple(jax.ShapeDtypeStruct(shape, dtype) for shape, dtype in outs),
            in_specs=spaces,
            compiler_params=PARAMS,
            **more,
        )(*args)

    place = me.astype(jnp.int32).reshape(1)
    raw_keys = video_k
    video_q, video_k, video_v, audio_q, audio_k, audio_v = (
        pltpu.with_memory_space_constraint(block, pltpu.HBM)
        for block in (video_q, video_k, video_v, audio_q, audio_k, audio_v)
    )
    at_end = (me == 0) | (me == n - 1)
    lengths = [size * HEAD_DIM for size in chunks]
    half = lengths[0]
    first_out, first_over, values0 = call(
        functools.partial(first_pack, n),
        (((2 * video_rows, half), jnp.bfloat16),) * 2 + (((video_rows, half), jnp.bfloat16),),
        [SMEM] + [HBM] * 4,
        place,
        video_k,
        video_v,
        audio_k,
        audio_v,
        out_specs=(VMEM,) * 3,
        scratch_shapes=[pltpu.SemaphoreType.DMA((7,))],
    )
    outs = tuple(((2 * video_rows, length), jnp.bfloat16) for length in lengths[1:])
    outs += (((rows + audio_rows, half), jnp.bfloat16), ((video_rows, half), jnp.bfloat16))
    outs += (((video_rows, half), jnp.bfloat16),)
    outs += (((rows, n * video_rows), jnp.float32),) * 2 + (((rows, n * audio_rows), jnp.float32),)
    *sights, asks0, asks1, values1, mask0, mask1, near = call(
        functools.partial(second_pack, n),
        outs,
        [SMEM, SMEM, VMEM] + [HBM] * 4,
        place,
        counts,
        offsets.reshape(1, -1),
        video_k,
        video_v,
        video_q,
        audio_q,
        out_specs=(VMEM,) * len(outs),
        scratch_shapes=[pltpu.SemaphoreType.DMA((9,))],
    )
    asks = [asks0, asks1]
    sights = [first_over] + sights

    keys_across = cross(raw_keys)
    values_across = [cross(values0), cross(values1)]
    sight_mate = [mate(first_out)]
    sound_across = cross(first_out)
    second_mate = mate(first_over)
    sound_far = cross(second_mate)
    at = 0
    for i in (1, 2):
        part = sound_across[:, at : at + lengths[i]]
        sight_mate.append(mate(jnp.where(at_end, sights[i], part)))
        at += lengths[i]
    pieces = [(0, chunks[0], 0, 0)]
    sight_far = [cross(sight_mate[0])]
    for source in (1, 2):
        pieces.append((sum(chunks[:source]), chunks[source], source, 0))
        sight_far.append(cross(sight_mate[source]))
    last = len(pieces) - 1
    asks_mate = [mate(asks[i]) for i in range(2)]

    def look(i, queries, mask):
        at, size, source, offset = pieces[i]
        half = min(source, 1)
        return call(
            functools.partial(video_kernel, n, at, half * chunks[0], offset),
            (((rows, size * HEAD_DIM), jnp.bfloat16),),
            [SMEM] + [VMEM] * (7 + half),
            place,
            mask,
            *queries[: 1 + half],
            sights[source],
            sight_mate[source],
            keys_across,
            values_across[half],
            sight_far[i],
            out_specs=(VMEM,),
            cost_estimate=cost(rows, n * video_rows, size),
        )[0]

    results = [look(i, asks_mate, mask1) for i in range(last + 1)]
    back = [mate(result) for result in results]
    mine = [look(i, asks, mask0) for i in range(last + 1)]
    theirs = call(
        functools.partial(audio_mate_kernel, n),
        (((audio_rows, width), jnp.bfloat16),),
        [SMEM] + [VMEM] * 5,
        place,
        asks_mate[0],
        first_out,
        second_mate,
        sound_across,
        sound_far,
        out_specs=(VMEM,),
        cost_estimate=cost(audio_rows, n * audio_rows, heads),
    )[0]
    own_cross, own = call(
        functools.partial(audio_own_kernel, n),
        (((video_rows, width), jnp.bfloat16), ((audio_rows, width), jnp.bfloat16)),
        [SMEM] + [VMEM] * 7,
        place,
        near,
        *asks,
        first_out,
        second_mate,
        sound_across,
        sound_far,
        out_specs=(VMEM,) * 2,
        cost_estimate=cost(rows, n * audio_rows, heads),
    )
    end_cross = call(
        functools.partial(audio_end_kernel, n),
        (((video_rows, width), jnp.bfloat16),),
        [SMEM] + [VMEM] * 8,
        place,
        near,
        *asks,
        first_over,
        sight_mate[0],
        sight_mate[1],
        sight_mate[2],
        sound_far,
        out_specs=(VMEM,),
        cost_estimate=cost(rows, n * audio_rows, heads),
    )[0]
    back_sound = mate(theirs)
    video_shape = ((video_rows, width), jnp.bfloat16)
    audio_shape = ((audio_rows, width), jnp.bfloat16)
    video_self, video_cross, audio_self, audio_cross = call(
        functools.partial(place_kernel, n),
        (video_shape, video_shape, audio_shape, audio_shape),
        [SMEM] + [VMEM] * (4 + 2 * last),
        place,
        own_cross,
        end_cross,
        own,
        *mine[:last],
        back_sound,
        *back[:last],
        out_specs=(HBM,) * 4,
        scratch_shapes=[pltpu.SemaphoreType.DMA((2 + 2 * last,))],
    )
    video_self, audio_cross = call(
        functools.partial(place_last_kernel, n, width - chunks[2] * HEAD_DIM),
        (video_shape, audio_shape),
        [SMEM] + [VMEM] * 2 + [HBM] * 2,
        place,
        mine[last],
        back[last],
        video_self,
        audio_cross,
        out_specs=(HBM,) * 2,
        scratch_shapes=[pltpu.SemaphoreType.DMA((2,))],
        input_output_aliases={3: 0, 4: 1},
    )
    return video_self, video_cross, audio_self, audio_cross


def solution(mesh):
    split = P(("groups", "seq"), ("tower", "mp"))
    placed = (split,) * 6 + (P("groups"), P("groups"))
    sizes = mesh.shape
    line = sizes["seq"] == 4 and sizes["mp"] == 2

    def whole(*arrays):
        heads = arrays[0].shape[1] // HEAD_DIM // (sizes["tower"] * sizes["mp"])
        paired = heads % 2 == 0 and heads > 3 and arrays[0].shape[0] == 2 * arrays[3].shape[0]
        body = lined if line and paired else gathered
        return jax.shard_map(
            body, mesh=mesh, in_specs=placed, out_specs=(split,) * 4, check_vma=False
        )(*arrays)

    return whole
```
